512 devices in a mesh: outer: 32 (over z, x_hi), inner: 16 (over x_lo, y, core).
Axes of the slice: x: 4 (x_hi: 2, x_lo: 2; x = x_hi * 2 + x_lo), y: 4, z: 16, core: 2. Of those that a mesh axis runs over, the one named last changes fastest.
Arguments:
- fine_input: bfloat16 [98304, 2048], P(('outer', 'inner')), may hold values from -12 to 12
- fine_query: bfloat16 [98304, 1024], P(('outer', 'inner')), may hold values from -4.5 to 4.5
- fine_key: bfloat16 [98304, 1024], P(('outer', 'inner')), may hold values from -4.5 to 4.5
- fine_value: bfloat16 [98304, 1024], P(('outer', 'inner')), may hold values from -6 to 6
- w_fine_out: bfloat16 [1024, 2048], P(None, 'inner'), may hold values from -0.1875 to 0.1875
- norm_gain: float32 [2048], replicated, may hold values from 0.25 to 1.75
- w_query: bfloat16 [2048, 2048], P(None, 'inner'), may hold values from -1 to 1
- w_key: bfloat16 [2048, 2048], P(None, 'inner'), may hold values from -1 to 1
- w_value: bfloat16 [2048, 2048], P(None, 'inner'), may hold values from -0.125 to 0.125
- w_coarse_out: bfloat16 [2048, 2048], P('inner'), may hold values from -0.125 to 0.125
Outputs:
- mixed_stream: bfloat16 [98304, 2048], P(('outer', 'inner'))
The draws below stay inside these ranges and needn't reach their ends.
All inputs are finite; a program needn't handle non-finite values.
Results may differ from the reference program's by a relative error of at most 0.008.
Values may be sent and summed in bfloat16 or wider, within the bound.
A program may use at most 128 MiB of HBM per device.

```python
import math
import jax
import jax.numpy as jnp
from jax import lax

D = 2048
HE = 128
HF = 8
WIN = 512
POOL = 8
TOKENS = 98304
LC = 12288
HC = 16


def draw_fine_input(key, part):
    stream = jnp.clip(jax.random.normal(jax.random.fold_in(key, 7301), (TOKENS, D), jnp.float32), -6.0, 6.0)
    return stream.astype(jnp.bfloat16)


def draw_fine_query(key, part):
    noise = jnp.clip(jax.random.normal(jax.random.fold_in(key, 7101), (TOKENS, HF * HE), jnp.float32), -4.5, 4.5)
    return noise.astype(jnp.bfloat16)


def draw_fine_key(key, part):
    noise = jnp.clip(jax.random.normal(jax.random.fold_in(key, 7102), (TOKENS, HF * HE), jnp.float32), -4.5, 4.5)
    return noise.astype(jnp.bfloat16)


def projection_draw(key, salt, spread):
    matrix = spread * jnp.clip(jax.random.normal(jax.random.fold_in(key, salt), (D, HC * HE), jnp.float32), -4.0, 4.0) / math.sqrt(D)
    return jnp.clip(matrix, -1.0, 1.0).astype(jnp.bfloat16)


def draw_w_query(key, part):
    spread = 2.0
    return projection_draw(key, 7401, spread)


def draw_w_key(key, part):
    return projection_draw(key, 7402, 1.0)


def steps_of(key, dims, cuts, smallest, top_value):
    factor_of, own = 1.0, jax.random.fold_in(key, 6)
    for axis_at, blocks in cuts:
        heights = jnp.exp(jax.random.uniform(jax.random.fold_in(own, axis_at), (blocks,), jnp.float32, smallest / len(cuts), top_value / len(cuts)))
        factor_of = factor_of * jnp.repeat(heights, dims[axis_at] // blocks).reshape([-1 if axis == axis_at else 1 for axis in range(len(dims))])
    return factor_of


def normal_values(rng, extent, scale, most, shards=(), kind=jnp.bfloat16):
    result = scale * jax.random.normal(rng, extent, jnp.float32)
    if shards:
        result = result * steps_of(rng, extent, shards, -0.22, 0.18)
    return jnp.clip(result, -most, most).astype(kind)


def setup_inputs(seed: int = 0) -> dict:
    streams_of = jax.random.split(jax.random.key(seed), 11)
    return {
        "fine_input": draw_fine_input(jax.random.fold_in(streams_of[10], 71), 0),
        "fine_query": draw_fine_query(jax.random.fold_in(streams_of[10], 71), 0),
        "fine_key": draw_fine_key(jax.random.fold_in(streams_of[10], 71), 0),
        "fine_value": normal_values(streams_of[3], (TOKENS, HF * HE), 1.0, 6.0, ((0, 512),)),
        "w_fine_out": normal_values(streams_of[4], (HF * HE, D), (HF * HE) ** -0.5, 0.1875, ((1, 16),)),
        "norm_gain": jnp.clip(1.0 + 0.15 * jax.random.normal(streams_of[5], (D,), jnp.float32), 0.25, 1.75),
        "w_query": draw_w_query(jax.random.fold_in(streams_of[10], 71), 0),
        "w_key": draw_w_key(jax.random.fold_in(streams_of[10], 71), 0),
        "w_value": normal_values(streams_of[8], (D, HC * HE), D ** -0.5, 0.125, ((1, 16),)),
        "w_coarse_out": normal_values(streams_of[9], (HC * HE, D), (HC * HE) ** -0.5, 0.125, ((0, 16),)),
    }


very_negative = -1e+30

def softmax_mix(scores, allowed, values):
    masked = jnp.where(allowed, scores, very_negative)
    row_max = lax.optimization_barrier(jnp.max(masked, axis=-1, keepdims=True))
    exp_weights = jnp.where(allowed, jnp.exp(scores - row_max), 0.0)
    row_sum = lax.optimization_barrier(jnp.sum(exp_weights, axis=-1))
    rounded = lax.optimization_barrier(exp_weights.astype(jnp.bfloat16)).astype(jnp.float32)
    summed = jnp.einsum('hqk,khe->qhe', rounded, values.astype(jnp.float32))
    return (summed / jnp.transpose(row_sum)[:, :, None]).astype(jnp.bfloat16)

def fine_attention(fine_query, fine_key, fine_value):
    head_count = fine_query.shape[1] // HE
    score_scale = 1.0 / math.sqrt(HE)
    query_heads = fine_query.reshape(TOKENS, head_count, HE)
    padding = jnp.zeros((WIN, head_count * HE), jnp.bfloat16)
    key_heads = jnp.concatenate([padding, fine_key], axis=0).reshape(TOKENS + WIN, head_count, HE)
    value_heads = jnp.concatenate([padding, fine_value], axis=0).reshape(TOKENS + WIN, head_count, HE)
    row_ids = jnp.arange(WIN, dtype=jnp.int32)[:, None] + WIN
    col_ids = jnp.arange(2 * WIN, dtype=jnp.int32)[None, :]
    distance = row_ids - col_ids

    def one_block(number):
        first_row = (number * WIN).astype(jnp.int32)
        block_query = lax.dynamic_slice_in_dim(query_heads, first_row, WIN, 0)
        block_key = lax.dynamic_slice_in_dim(key_heads, first_row, 2 * WIN, 0)
        block_value = lax.dynamic_slice_in_dim(value_heads, first_row, 2 * WIN, 0)
        scores = jnp.einsum('qhe,khe->hqk', block_query.astype(jnp.float32), block_key.astype(jnp.float32)) * score_scale
        allowed = (distance >= 0) & (distance < WIN) & (first_row + col_ids >= WIN)
        return softmax_mix(scores, allowed[None], block_value)
    mixed = lax.map(one_block, jnp.arange(TOKENS // WIN, dtype=jnp.int32))
    return mixed.reshape(TOKENS, head_count * HE)

def coarse_attention(coarse_query, coarse_key, coarse_value):
    head_count = coarse_query.shape[1] // HE
    score_scale = 1.0 / math.sqrt(HE)
    block_size = math.gcd(LC, 256)
    query_heads = coarse_query.reshape(LC, head_count, HE)
    key_heads = coarse_key.reshape(LC, head_count, HE)
    value_heads = coarse_value.reshape(LC, head_count, HE)
    col_ids = jnp.arange(LC, dtype=jnp.int32)[None, :]

    def one_block(number):
        first_row = (number * block_size).astype(jnp.int32)
        block_query = lax.dynamic_slice_in_dim(query_heads, first_row, block_size, 0)
        scores = jnp.einsum('qhe,khe->hqk', block_query.astype(jnp.float32), key_heads.astype(jnp.float32)) * score_scale
        row_ids = first_row + jnp.arange(block_size, dtype=jnp.int32)[:, None]
        allowed = col_ids <= row_ids
        return softmax_mix(scores, allowed[None], value_heads)
    mixed = lax.map(one_block, jnp.arange(LC // block_size, dtype=jnp.int32))
    return mixed.reshape(LC, head_count * HE)

def reference(fine_input, fine_query, fine_key, fine_value, w_fine_out, norm_gain, w_query, w_key, w_value, w_coarse_out):
    fine_mix = fine_attention(fine_query, fine_key, fine_value)
    fine_state = (fine_input.astype(jnp.float32) + jnp.dot(fine_mix, w_fine_out, preferred_element_type=jnp.float32)).astype(jnp.bfloat16)
    shifted = jnp.concatenate([jnp.zeros((POOL - 1, D), jnp.bfloat16), fine_state[:TOKENS - POOL + 1]], axis=0)
    pooled = (lax.optimization_barrier(jnp.sum(shifted.reshape(LC, POOL, D).astype(jnp.float32), axis=1)) / POOL).astype(jnp.bfloat16)
    pooled_wide = pooled.astype(jnp.float32)
    moment = lax.optimization_barrier(jnp.mean(pooled_wide * pooled_wide, axis=-1, keepdims=True))
    normed = (pooled_wide * lax.rsqrt(moment + 1e-06) * norm_gain).astype(jnp.bfloat16)
    coarse_query = jnp.dot(normed, w_query, preferred_element_type=jnp.float32).astype(jnp.bfloat16)
    coarse_key = jnp.dot(normed, w_key, preferred_element_type=jnp.float32).astype(jnp.bfloat16)
    coarse_value = jnp.dot(normed, w_value, preferred_element_type=jnp.float32).astype(jnp.bfloat16)
    coarse_mix = coarse_attention(coarse_query, coarse_key, coarse_value)
    coarse_out = (pooled_wide + jnp.dot(coarse_mix, w_coarse_out, preferred_element_type=jnp.float32)).astype(jnp.bfloat16)
    lifted = jnp.repeat(coarse_out, POOL, axis=0)
    return (fine_state.astype(jnp.float32) + lifted.astype(jnp.float32)).astype(jnp.bfloat16)
```

```python
import functools
import math

import jax
import jax.numpy as jnp
from jax import lax
from jax.experimental import pallas as pl
from jax.experimental.pallas import tpu as pltpu
from jax.sharding import PartitionSpec as P

HE = 128
WIN = 512
POOL = 8
NEG = -1e30
LOG2E = math.log2(math.e)
SCALE = 1.0 / math.sqrt(HE)
BF = jnp.bfloat16
F32 = jnp.float32
TRANS = (((1,), (1,)), ((), ()))
MESH = pl.DeviceIdType.MESH
NX, NY, NZ, NC = 4, 4, 16, 2
NP = NX * NY * NC


def vmem_spec():
    return pl.BlockSpec(memory_space=pltpu.VMEM)


def any_spec():
    return pl.BlockSpec(memory_space=pl.ANY)


def place():
    outer = lax.axis_index("outer")
    inner = lax.axis_index("inner")
    x = (outer % 2) * 2 + inner // 8
    return x, (inner // 2) % NY, outer // 2, inner % NC


def device_at(x, y, z, c):
    return (z * 2 + x // 2, (x % 2) * 8 + y * 2 + c)


def device_of(pos):
    pos = (pos + 512) % 512
    return (pos // 16, pos % 16)


def slot_of(x, y, c):
    return x * 8 + y * 2 + c


def greet(devices):
    barrier = pltpu.get_barrier_semaphore()
    for d in devices:
        pl.semaphore_signal(barrier, inc=1, device_id=d, device_id_type=MESH)
    pl.semaphore_wait(barrier, len(devices))


def plane_neighbours():
    x, y, z, c = place()
    return [
        device_at((x + 1) % NX, y, z, c),
        device_at((x + 3) % NX, y, z, c),
        device_at(x, (y + 1) % NY, z, c),
        device_at(x, (y + 3) % NY, z, c),
        device_at(x, y, z, 1 - c),
    ]


class Sends:
    def __init__(self, send_sem, recv_sem, base=0):
        self.send_sem, self.recv_sem, self.next = send_sem, recv_sem, base
        self.started = []

    def new(self):
        self.next += 1
        return self.next - 1

    def copy(self, k, src, dst, to):
        return pltpu.make_async_remote_copy(
            src_ref=src,
            dst_ref=dst,
            send_sem=self.send_sem.at[k],
            recv_sem=self.recv_sem.at[k],
            device_id=to,
            device_id_type=MESH,
        )

    def start(self, k, src, dst, to):
        c = self.copy(k, src, dst, to)
        c.start()
        self.started.append(c)

    def arrived(self, k, dst, to):
        self.copy(k, dst, dst, to).wait_recv()

    def drain(self):
        for c in self.started:
            c.wait_send()
        self.started = []


PLANE_COPIES = 71


def plane_gather(sends, src, dst, local_sem):
    x, y, z, c = place()
    rows = src.shape[0]
    quarter = rows // 4

    def xy(axis, off):
        return ((x + off) % NX, y) if axis == 0 else (x, (y + off) % NY)

    def near(axis, off):
        px, py = xy(axis, off)
        return device_at(px, py, z, c)

    def at(axis, a, b):
        if axis == 0:
            return slot_of((x + a) % NX, (y + b) % NY, c)
        return slot_of((x + b) % NX, (y + a) % NY, c)

    partner = device_at(x, y, z, 1 - c)
    halves = []
    for first in (0, 1):
        lo = first * 2 * quarter
        halves.append(
            dict(
                first=first,
                whole=pl.ds(lo, 2 * quarter),
                q0=pl.ds(lo, quarter),
                q1=pl.ds(lo + quarter, quarter),
                k={},
            )
        )
    for h in halves:
        for name in ("r1", "l1", "r2", "l2"):
            h["k"][name] = sends.new()
        for j in (0, -1, 1, 2):
            for name in ("r1", "l1", "r2", "l2"):
                h["k"][name, j] = sends.new()
        for j in (0, -1, 1, 2):
            for i in (0, -1, 1, 2):
                if (i, j) != (0, 0):
                    h["k"]["p", j, i] = sends.new()
    own_pair = sends.new()
    mine = slot_of(x, y, c)
    theirs = slot_of(x, y, 1 - c)
    local = pltpu.make_async_copy(src, dst.at[mine], local_sem)

    def to_partner(h, j, i):
        s = at(h["first"], j, i)
        sends.start(h["k"]["p", j, i], dst.at[s, h["whole"]], dst.at[s, h["whole"]], partner)

    for h in halves:
        a = h["first"]
        for name, off in (("r1", 1), ("l1", -1)):
            sends.start(
                h["k"][name], src.at[h["whole"]], dst.at[mine, h["whole"]], near(a, off % 4)
            )
    for h in halves:
        b = 1 - h["first"]
        for name, off in (("r1", 1), ("l1", -1)):
            sends.start(
                h["k"][name, 0], src.at[h["whole"]], dst.at[mine, h["whole"]], near(b, off % 4)
            )
    sends.start(own_pair, src, dst.at[mine], partner)
    local.start()
    yield

    def second(h, j):
        s = at(h["first"], j, 0)
        for name, off in (("r1", 1), ("l1", -1)):
            sends.start(
                h["k"][name, j],
                dst.at[s, h["whole"]],
                dst.at[s, h["whole"]],
                near(1 - h["first"], off % 4),
            )
        to_partner(h, j, 0)

    for h in halves:
        a = h["first"]
        for name, fwd, off, part in (("r1", "r2", -1, "q0"), ("l1", "l2", 1, "q1")):
            s = at(a, off, 0)
            sends.arrived(h["k"][name], dst.at[s, h["whole"]], near(a, off % 4))
            sends.start(
                h["k"][fwd], dst.at[s, h[part]], dst.at[s, h[part]], near(a, (-off) % 4)
            )
    for h in halves:
        for off in (-1, 1):
            second(h, off)
    yield

    def relay(h, j):
        b = 1 - h["first"]
        for name, fwd, off, part in (("r1", "r2", -1, "q0"), ("l1", "l2", 1, "q1")):
            s = at(h["first"], j, off)
            sends.arrived(h["k"][name, j], dst.at[s, h["whole"]], near(b, off % 4))
            sends.start(
                h["k"][fwd, j], dst.at[s, h[part]], dst.at[s, h[part]], near(b, (-off) % 4)
            )
            to_partner(h, j, off)

    for h in halves:
        relay(h, 0)
    yield
    for h in halves:
        a = h["first"]
        s = at(a, 2, 0)
        sends.arrived(h["k"]["r2"], dst.at[s, h["q0"]], near(a, 3))
        sends.arrived(h["k"]["l2"], dst.at[s, h["q1"]], near(a, 1))
        second(h, 2)
    yield

    def last(h, j):
        b = 1 - h["first"]
        s = at(h["first"], j, 2)
        sends.arrived(h["k"]["r2", j], dst.at[s, h["q0"]], near(b, 3))
        sends.arrived(h["k"]["l2", j], dst.at[s, h["q1"]], near(b, 1))
        to_partner(h, j, 2)

    for j in (-1, 1):
        for h in halves:
            relay(h, j)
    for h in halves:
        last(h, 0)
    yield
    for h in halves:
        relay(h, 2)
    for j in (-1, 1):
        for h in halves:
            last(h, j)
    yield
    for h in halves:
        last(h, 2)
    local.wait()
    sends.arrived(own_pair, dst.at[theirs], partner)
    for h in halves:
        for j in (0, -1, 1, 2):
            for i in (0, -1, 1, 2):
                if (i, j) != (0, 0):
                    s = at(h["first"], j, i) + 1 - 2 * c
                    sends.arrived(h["k"]["p", j, i], dst.at[s, h["whole"]], partner)
    yield


def run_all(steps):
    for _ in steps:
        pass


def gather_kernel(src_ref, dst_ref, local_sem, send_sem, recv_sem):
    greet(plane_neighbours())
    sends = Sends(send_sem, recv_sem)
    run_all(plane_gather(sends, src_ref, dst_ref, local_sem))
    sends.drain()


def gathered_in_plane(block, collective_id):
    return pl.pallas_call(
        gather_kernel,
        out_shape=jax.ShapeDtypeStruct((NP, *block.shape), block.dtype),
        in_specs=[any_spec()],
        out_specs=any_spec(),
        scratch_shapes=[
            pltpu.SemaphoreType.DMA,
            pltpu.SemaphoreType.DMA((PLANE_COPIES,)),
            pltpu.SemaphoreType.DMA((PLANE_COPIES,)),
        ],
        compiler_params=pltpu.CompilerParams(
            collective_id=collective_id, has_side_effects=True, vmem_limit_bytes=16 << 20
        ),
        name=f"plane_gather_{collective_id}",
    )(block)


def halo_kernel(k_ref, v_ref, kp_ref, vp_ref, send_sem, recv_sem):
    x, y, z, c = place()
    pos = lax.axis_index("outer") * 16 + lax.axis_index("inner")
    rows = k_ref.shape[0]
    short = WIN - 2 * rows
    ahead, behind = device_of(pos + 2), device_of(pos - 2)
    partner = device_at(x, y, z, 1 - c)
    greet([ahead, behind, partner, device_of(pos + 3), device_of(pos - 3)])
    sends = Sends(send_sem, recv_sem)
    pairs = ((k_ref, kp_ref), (v_ref, vp_ref))
    mid, end = pl.ds(short, rows), pl.ds(short + rows, rows)
    head, tail = pl.ds(0, short), pl.ds(rows - short, short)
    for n, (own, prev) in enumerate(pairs):
        sends.start(n, own, prev.at[mid], ahead)

    def put(n, src, dst, to):
        sends.copy(n, src, dst, to).start()

    for n, (own, prev) in enumerate(pairs):

        @pl.when(c == 0)
        def _():
            put(2 + n, own, prev.at[end], partner)

        @pl.when(c == 1)
        def _():
            put(4 + n, own.at[tail], prev.at[head], device_of(pos + 3))

    for n, (own, prev) in enumerate(pairs):
        sends.arrived(n, prev.at[mid], behind)

        @pl.when(c == 0)
        def _():
            put(4 + n, prev.at[pl.ds(rows, short)], prev.at[head], partner)

        @pl.when(c == 1)
        def _():
            put(2 + n, prev.at[mid], prev.at[end], partner)

    for n, (own, prev) in enumerate(pairs):
        sends.copy(2 + n, own, prev.at[end], partner).wait_send()
        sends.copy(4 + n, own.at[tail], prev.at[head], partner).wait_send()
        sends.arrived(2 + n, prev.at[end], partner)
        sends.arrived(4 + n, prev.at[head], partner)
    sends.drain()


def halo(k, v):
    width = k.shape[1]
    return pl.pallas_call(
        halo_kernel,
        out_shape=[jax.ShapeDtypeStruct((WIN, width), BF)] * 2,
        in_specs=[any_spec()] * 2,
        out_specs=[any_spec()] * 2,
        scratch_shapes=[pltpu.SemaphoreType.DMA((6,)), pltpu.SemaphoreType.DMA((6,))],
        compiler_params=pltpu.CompilerParams(
            collective_id=1, has_side_effects=True, vmem_limit_bytes=16 << 20
        ),
        name="halo",
    )(k, v)


def fine_kernel(
    x_ref, q_ref, k_ref, v_ref, kp_ref, vp_ref, w_ref, gain_ref,
    state_ref, pooled_ref, normed_ref,
    mix_ref, edge_out, edge_in, send_sem, recv_sem,
):
    rows = q_ref.shape[0]
    heads = q_ref.shape[1] // HE
    position = lax.axis_index("outer") * 16 + lax.axis_index("inner")
    greet([device_of(position + 1), device_of(position - 1)])
    t_prev = lax.broadcasted_iota(jnp.int32, (rows, WIN), 0)
    u_prev = lax.broadcasted_iota(jnp.int32, (rows, WIN), 1)
    ok_prev = (u_prev > t_prev) & (position * rows - WIN + u_prev >= 0)
    t_own = lax.broadcasted_iota(jnp.int32, (rows, rows), 0)
    u_own = lax.broadcasted_iota(jnp.int32, (rows, rows), 1)
    ok_own = u_own <= t_own
    for h in range(heads):
        cols = slice(h * HE, (h + 1) * HE)
        q = q_ref[:, cols]
        s_prev = lax.dot_general(q, kp_ref[:, cols], TRANS, preferred_element_type=F32) * SCALE
        s_own = lax.dot_general(q, k_ref[:, cols], TRANS, preferred_element_type=F32) * SCALE
        s_prev = jnp.where(ok_prev, s_prev, NEG)
        s_own = jnp.where(ok_own, s_own, NEG)
        top = jnp.maximum(
            jnp.max(s_prev, axis=-1, keepdims=True), jnp.max(s_own, axis=-1, keepdims=True)
        )
        p_prev = jnp.exp(s_prev - top)
        p_own = jnp.exp(s_own - top)
        total = jnp.sum(p_prev, axis=-1, keepdims=True) + jnp.sum(p_own, axis=-1, keepdims=True)
        mixed = jnp.dot(p_prev.astype(BF), vp_ref[:, cols], preferred_element_type=F32)
        mixed += jnp.dot(p_own.astype(BF), v_ref[:, cols], preferred_element_type=F32)
        mix_ref[:, cols] = (mixed / total).astype(BF)
    width = x_ref.shape[1]
    half = w_ref.shape[1]
    per = w_ref.shape[2]

    @pl.loop(0, NP // 2)
    def _(n):
        at = pl.ds(pl.multiple_of(n * per, per), per)
        prod = jnp.dot(mix_ref[:, :half], w_ref[n], preferred_element_type=F32)
        prod += jnp.dot(mix_ref[:, half:], w_ref[n + NP // 2], preferred_element_type=F32)
        state_ref[:, at] = (x_ref[:, at].astype(F32) + prod).astype(BF)

    edge_out[...] = state_ref[rows - POOL :, :]
    send = pltpu.make_async_remote_copy(
        src_ref=edge_out,
        dst_ref=edge_in,
        send_sem=send_sem,
        recv_sem=recv_sem,
        device_id=device_of(position + 1),
        device_id_type=MESH,
    )
    send.start()
    groups = state_ref[...].astype(F32).reshape(rows // POOL, POOL, width)
    first = groups[:, 0, :]
    rest = jnp.sum(groups[:, 1:, :], axis=1)
    send.wait()
    edge = jnp.sum(edge_in[...].astype(F32)[1:, :], axis=0, keepdims=True)
    edge = jnp.where(position == 0, 0.0, edge)
    before = jnp.concatenate([edge, rest[: rows // POOL - 1, :]], axis=0)
    pooled = ((before + first) / POOL).astype(BF)
    pooled_ref[...] = pooled
    wide = pooled.astype(F32)
    moment = jnp.mean(wide * wide, axis=-1, keepdims=True)
    normed_ref[...] = (wide * lax.rsqrt(moment + 1e-06) * gain_ref[...]).astype(BF)


def fine_stage(x, q, k, v, kp, vp, w, gain):
    rows, width = x.shape
    coarse = jax.ShapeDtypeStruct((rows // POOL, width), BF)
    return pl.pallas_call(
        fine_kernel,
        out_shape=[jax.ShapeDtypeStruct((rows, width), BF), coarse, coarse],
        in_specs=[vmem_spec()] * 8,
        out_specs=[vmem_spec()] * 3,
        scratch_shapes=[
            pltpu.VMEM(q.shape, BF),
            pltpu.VMEM((POOL, width), BF),
            pltpu.VMEM((POOL, width), BF),
            pltpu.SemaphoreType.DMA,
            pltpu.SemaphoreType.DMA,
        ],
        compiler_params=pltpu.CompilerParams(
            collective_id=2, has_side_effects=True, vmem_limit_bytes=40 << 20
        ),
        name="fine",
    )(x, q, k, v, kp, vp, w, gain.reshape(1, width))


ZCHUNK = 8


def z_gather_kernel(src_ref, dst_ref, local_sem, send_sem, recv_sem):
    x, y, z, c = place()
    up, down = device_at(x, y, (z + 1) % NZ, c), device_at(x, y, (z + NZ - 1) % NZ, c)
    greet([up, down])
    sends = Sends(send_sem, recv_sem)
    chunks = src_ref.shape[0] // ZCHUNK
    local = pltpu.make_async_copy(src_ref, dst_ref.at[z], local_sem)
    local.start()
    count_up, count_down = NZ // 2, NZ // 2 - 1
    for s in range(count_up + 1):
        for part in range(chunks):
            at = pl.ds(part * ZCHUNK, ZCHUNK)
            for sign, count, base, to, origin in (
                (-1, count_up, 0, up, down),
                (1, count_down, count_up * chunks, down, up),
            ):
                if s > count:
                    continue
                held = (z + sign * s + NZ) % NZ
                if s > 0:
                    sends.arrived(base + (s - 1) * chunks + part, dst_ref.at[held, at], origin)
                if s < count:
                    src = src_ref.at[at] if s == 0 else dst_ref.at[held, at]
                    sends.start(base + s * chunks + part, src, dst_ref.at[held, at], to)
    local.wait()
    sends.drain()


def gathered_along_z(block):
    chunks = block.shape[0] // ZCHUNK
    count = (NZ - 1) * chunks
    return pl.pallas_call(
        z_gather_kernel,
        out_shape=jax.ShapeDtypeStruct((NZ, *block.shape), block.dtype),
        in_specs=[any_spec()],
        out_specs=any_spec(),
        scratch_shapes=[
            pltpu.SemaphoreType.DMA,
            pltpu.SemaphoreType.DMA((count,)),
            pltpu.SemaphoreType.DMA((count,)),
        ],
        compiler_params=pltpu.CompilerParams(
            collective_id=3, has_side_effects=True, vmem_limit_bytes=16 << 20
        ),
        name="z_gather",
    )(block)


def z_exchange_kernel(src_ref, dst_ref, local_sem, send_sem, recv_sem):
    x, y, z, c = place()
    others = [device_at(x, y, (z + d) % NZ, c) for d in range(1, NZ)]
    greet(others)
    sends = Sends(send_sem, recv_sem)
    local = pltpu.make_async_copy(src_ref.at[z], dst_ref.at[z], local_sem)
    local.start()
    for d in (8, 7, 9, 6, 10, 5, 11, 4, 12, 3, 13, 2, 14, 1, 15):
        sends.start(d - 1, src_ref.at[(z + d) % NZ], dst_ref.at[z], others[d - 1])
    local.wait()
    for d in range(1, NZ):
        origin = (z + NZ - d) % NZ
        sends.arrived(d - 1, dst_ref.at[origin], device_at(x, y, origin, c))
    sends.drain()


def exchanged_along_z(blocks):
    return pl.pallas_call(
        z_exchange_kernel,
        out_shape=jax.ShapeDtypeStruct(blocks.shape, blocks.dtype),
        in_specs=[any_spec()],
        out_specs=any_spec(),
        scratch_shapes=[
            pltpu.SemaphoreType.DMA,
            pltpu.SemaphoreType.DMA((NZ - 1,)),
            pltpu.SemaphoreType.DMA((NZ - 1,)),
        ],
        compiler_params=pltpu.CompilerParams(
            collective_id=4, has_side_effects=True, vmem_limit_bytes=16 << 20
        ),
        name="z_exchange",
    )(blocks)


def scatter_kernel(src_ref, dst_ref, local_sem, send_sem, recv_sem):
    outer = lax.axis_index("outer")
    inner = lax.axis_index("inner")
    head = outer // 2
    others = [(outer, (inner + d) % 16) for d in range(1, 16)]
    greet(others)
    sends = Sends(send_sem, recv_sem)

    @pl.when(inner == head)
    def _():
        local = pltpu.make_async_copy(src_ref.at[inner], dst_ref, local_sem)
        local.start()
        for d in range(1, 16):
            to = (inner + d) % 16
            pltpu.make_async_remote_copy(
                src_ref=src_ref.at[to],
                dst_ref=dst_ref,
                send_sem=send_sem.at[d - 1],
                recv_sem=recv_sem,
                device_id=(outer, to),
                device_id_type=MESH,
            ).start()
        local.wait()
        for d in range(1, 16):
            pltpu.make_async_copy(src_ref.at[0], src_ref.at[0], send_sem.at[d - 1]).wait()

    @pl.when(inner != head)
    def _():
        pltpu.make_async_copy(dst_ref, dst_ref, recv_sem).wait()


def scattered_from_head(pieces):
    return pl.pallas_call(
        scatter_kernel,
        out_shape=jax.ShapeDtypeStruct(pieces.shape[1:], pieces.dtype),
        in_specs=[any_spec()],
        out_specs=any_spec(),
        scratch_shapes=[
            pltpu.SemaphoreType.DMA,
            pltpu.SemaphoreType.DMA((15,)),
            pltpu.SemaphoreType.DMA,
        ],
        compiler_params=pltpu.CompilerParams(
            collective_id=5, has_side_effects=True, vmem_limit_bytes=16 << 20
        ),
        name="scatter",
    )(pieces)


def coarse_kernel(q_ref, kv_ref, out_ref, top_ref, acc_ref):
    x, y, z, c = place()
    me = slot_of(x, y, c)
    count = q_ref.shape[0]
    per = count // NZ
    factor = SCALE * LOG2E
    top_ref[...] = jnp.full(top_ref.shape, NEG, F32)
    acc_ref[...] = jnp.zeros(acc_ref.shape, F32)
    ones = jnp.ones((count, HE), BF)
    t = lax.broadcasted_iota(jnp.int32, (count, count), 0)
    u = lax.broadcasted_iota(jnp.int32, (count, count), 1)
    t_plane, u_plane = t // per, u // per

    @pl.loop(0, NP)
    def _(d):
        s = lax.dot_general(
            q_ref[...], kv_ref[d, :, :HE], TRANS, preferred_element_type=F32
        ) * factor
        reach = jnp.where(d < me, t_plane * per + per - 1, jnp.where(d == me, t, t_plane * per - 1))
        s = jnp.where(u <= reach, s, NEG)
        old = top_ref[...]
        new = jnp.maximum(old, jnp.max(s, axis=-1, keepdims=True))
        p = jnp.where(u <= reach, jnp.exp2(s - new), 0.0).astype(BF)
        wide = jnp.concatenate([kv_ref[d, :, HE:], ones], axis=1)
        acc_ref[...] = acc_ref[...] * jnp.exp2(old - new) + jnp.dot(
            p, wide, preferred_element_type=F32
        )
        top_ref[...] = new

    out_ref[...] = (acc_ref[:, :HE] / acc_ref[:, HE:]).astype(BF)


def coarse_stage(q, kv):
    return pl.pallas_call(
        coarse_kernel,
        out_shape=jax.ShapeDtypeStruct(q.shape, BF),
        in_specs=[vmem_spec()] * 2,
        out_specs=vmem_spec(),
        scratch_shapes=[
            pltpu.VMEM((q.shape[0], 1), F32),
            pltpu.VMEM((q.shape[0], 2 * HE), F32),
        ],
        compiler_params=pltpu.CompilerParams(vmem_limit_bytes=40 << 20),
        name="coarse",
    )(q, kv)


def on_device(
    fine_input,
    fine_query,
    fine_key,
    fine_value,
    w_fine_out,
    norm_gain,
    w_query,
    w_key,
    w_value,
    w_coarse_out,
):
    rows, width = fine_input.shape
    copy = lax.axis_index("outer") % 2

    def half_of(w):
        size = w.shape[0] // 2
        return lax.dynamic_slice_in_dim(w, copy * size, size, 0)

    kp, vp = halo(fine_key, fine_value)
    w_fine = gathered_in_plane(half_of(w_fine_out), 6)
    w_out = gathered_in_plane(half_of(w_coarse_out), 7)
    joined = jnp.concatenate([w_query, w_key, w_value], axis=1)
    head_width = joined.shape[1]
    piece = scattered_from_head(half_of(joined).reshape(16, -1, head_width))
    w_head = gathered_in_plane(piece, 8).reshape(width, head_width)
    state, pooled, normed = fine_stage(
        fine_input, fine_query, fine_key, fine_value, kp, vp, w_fine, norm_gain
    )
    tokens = gathered_along_z(normed).reshape(-1, width)
    proj = jnp.dot(tokens, w_head, preferred_element_type=F32).astype(BF)
    kv = gathered_in_plane(proj[:, HE:], 9)
    mix = coarse_stage(proj[:, :HE], kv)
    heads = exchanged_along_z(mix.reshape(NZ, -1, HE))
    heads = heads.reshape(NZ, rows // POOL, 2, HE // 2).transpose(1, 2, 0, 3)
    head_total = jnp.dot(
        heads.reshape(rows // POOL, -1), w_out.reshape(-1, width), preferred_element_type=F32
    )
    coarse_out = (pooled.astype(F32) + head_total).astype(BF)
    groups = state.reshape(rows // POOL, POOL, width).astype(F32)
    lifted = groups + coarse_out.astype(F32)[:, None, :]
    return lifted.reshape(rows, width).astype(BF)


def solution(mesh):
    placed = (
        P(("outer", "inner"), None),
        P(("outer", "inner"), None),
        P(("outer", "inner"), None),
        P(("outer", "inner"), None),
        P(None, "inner"),
        P(),
        P(None, "inner"),
        P(None, "inner"),
        P(None, "inner"),
        P("inner", None),
    )
    return jax.shard_map(
        on_device,
        mesh=mesh,
        in_specs=placed,
        out_specs=P(("outer", "inner"), None),
        check_vma=False,
    )
```

```python
import functools
import math

import jax
import jax.numpy as jnp
from jax import lax
from jax.experimental import pallas as pl
from jax.experimental.pallas import tpu as pltpu
from jax.sharding import PartitionSpec as P

HE = 128
WIN = 512
POOL = 8
NEG = -1e30
LOG2E = math.log2(math.e)
SCALE = 1.0 / math.sqrt(HE)
BF = jnp.bfloat16
F32 = jnp.float32
TRANS = (((1,), (1,)), ((), ()))
MESH = pl.DeviceIdType.MESH
NX, NY, NZ, NC = 4, 4, 16, 2
NP = NX * NY * NC


def vmem_spec():
    return pl.BlockSpec(memory_space=pltpu.VMEM)


def any_spec():
    return pl.BlockSpec(memory_space=pl.ANY)


def place():
    outer = lax.axis_index("outer")
    inner = lax.axis_index("inner")
    x = (outer % 2) * 2 + inner // 8
    return x, (inner // 2) % NY, outer // 2, inner % NC


def device_at(x, y, z, c):
    return (z * 2 + x // 2, (x % 2) * 8 + y * 2 + c)


def device_of(pos):
    pos = (pos + 512) % 512
    return (pos // 16, pos % 16)


def slot_of(x, y, c):
    return x * 8 + y * 2 + c


def greet(devices):
    barrier = pltpu.get_barrier_semaphore()
    for d in devices:
        pl.semaphore_signal(barrier, inc=1, device_id=d, device_id_type=MESH)
    pl.semaphore_wait(barrier, len(devices))


def plane_neighbours():
    x, y, z, c = place()
    return [
        device_at((x + 1) % NX, y, z, c),
        device_at((x + 3) % NX, y, z, c),
        device_at(x, (y + 1) % NY, z, c),
        device_at(x, (y + 3) % NY, z, c),
        device_at(x, y, z, 1 - c),
    ]


class Sends:
    def __init__(self, send_sem, recv_sem, base=0):
        self.send_sem, self.recv_sem, self.next = send_sem, recv_sem, base
        self.started = []

    def new(self):
        self.next += 1
        return self.next - 1

    def copy(self, k, src, dst, to):
        return pltpu.make_async_remote_copy(
            src_ref=src,
            dst_ref=dst,
            send_sem=self.send_sem.at[k],
            recv_sem=self.recv_sem.at[k],
            device_id=to,
            device_id_type=MESH,
        )

    def start(self, k, src, dst, to):
        c = self.copy(k, src, dst, to)
        c.start()
        self.started.append(c)

    def arrived(self, k, dst, to):
        self.copy(k, dst, dst, to).wait_recv()

    def drain(self):
        for c in self.started:
            c.wait_send()
        self.started = []


def plane_copies(firsts):
    return 35 * len(firsts) + 1


def plane_gather(sends, src, dst, local_sem, firsts=(0, 1)):
    x, y, z, c = place()
    part = src.shape[0] // len(firsts)

    def near(axis, off):
        if axis == 0:
            return device_at((x + off) % NX, y, z, c)
        return device_at(x, (y + off) % NY, z, c)

    def at(axis, a, b):
        if axis == 0:
            return slot_of((x + a) % NX, (y + b) % NY, c)
        return slot_of((x + b) % NX, (y + a) % NY, c)

    partner = device_at(x, y, z, 1 - c)
    halves = []
    for n, first in enumerate(firsts):
        lo = n * part
        h = dict(first=first, whole=pl.ds(lo, part), k={})
        h["q0"] = pl.ds(lo, part // 2)
        h["q1"] = pl.ds(lo + part // 2, part // 2)
        for name in ("r1", "l1", "r2", "l2"):
            h["k"][name] = sends.new()
        for j in (0, -1, 1, 2):
            for name in ("r1", "l1", "r2", "l2"):
                h["k"][name, j] = sends.new()
        for j in (0, -1, 1, 2):
            for i in (0, -1, 1, 2):
                if (i, j) != (0, 0):
                    h["k"]["p", j, i] = sends.new()
        halves.append(h)
    own_pair = sends.new()
    mine = slot_of(x, y, c)
    theirs = slot_of(x, y, 1 - c)
    local = pltpu.make_async_copy(src, dst.at[mine], local_sem)

    def to_partner(h, j, i):
        s = at(h["first"], j, i)
        sends.start(h["k"]["p", j, i], dst.at[s, h["whole"]], dst.at[s, h["whole"]], partner)

    for second_axis in (False, True):
        for h in halves:
            a = 1 - h["first"] if second_axis else h["first"]
            for name, off in (("r1", 1), ("l1", -1)):
                k = h["k"][(name, 0) if second_axis else name]
                sends.start(k, src.at[h["whole"]], dst.at[mine, h["whole"]], near(a, off % 4))
    sends.start(own_pair, src, dst.at[mine], partner)
    local.start()
    yield

    def second(h, j):
        s = at(h["first"], j, 0)
        for name, off in (("r1", 1), ("l1", -1)):
            sends.start(
                h["k"][name, j],
                dst.at[s, h["whole"]],
                dst.at[s, h["whole"]],
                near(1 - h["first"], off % 4),
            )
        to_partner(h, j, 0)

    directions = (("r1", "r2", -1, "q0"), ("l1", "l2", 1, "q1"))
    for h in halves:
        a = h["first"]
        for name, fwd, off, q in directions:
            s = at(a, off, 0)
            sends.arrived(h["k"][name], dst.at[s, h["whole"]], near(a, off % 4))
            sends.start(h["k"][fwd], dst.at[s, h[q]], dst.at[s, h[q]], near(a, (-off) % 4))
    for h in halves:
        for off in (-1, 1):
            second(h, off)
    yield

    def relay(h, j):
        b = 1 - h["first"]
        for name, fwd, off, q in directions:
            s = at(h["first"], j, off)
            sends.arrived(h["k"][name, j], dst.at[s, h["whole"]], near(b, off % 4))
            sends.start(h["k"][fwd, j], dst.at[s, h[q]], dst.at[s, h[q]], near(b, (-off) % 4))
            to_partner(h, j, off)

    for h in halves:
        relay(h, 0)
    yield
    for h in halves:
        a = h["first"]
        s = at(a, 2, 0)
        sends.arrived(h["k"]["r2"], dst.at[s, h["q0"]], near(a, 3))
        sends.arrived(h["k"]["l2"], dst.at[s, h["q1"]], near(a, 1))
        second(h, 2)
    yield

    def last(h, j):
        b = 1 - h["first"]
        s = at(h["first"], j, 2)
        sends.arrived(h["k"]["r2", j], dst.at[s, h["q0"]], near(b, 3))
        sends.arrived(h["k"]["l2", j], dst.at[s, h["q1"]], near(b, 1))
        to_partner(h, j, 2)

    for j in (-1, 1):
        for h in halves:
            relay(h, j)
    for h in halves:
        last(h, 0)
    yield
    for h in halves:
        relay(h, 2)
    for j in (-1, 1):
        for h in halves:
            last(h, j)
    yield
    for h in halves:
        last(h, 2)
    local.wait()
    sends.arrived(own_pair, dst.at[theirs], partner)
    for h in halves:
        for j in (0, -1, 1, 2):
            for i in (0, -1, 1, 2):
                if (i, j) != (0, 0):
                    s = at(h["first"], j, i) + 1 - 2 * c
                    sends.arrived(h["k"]["p", j, i], dst.at[s, h["whole"]], partner)
    yield


def run_all(steps):
    for _ in steps:
        pass


HALO_COPIES = 8
W_FIRSTS = (1,)


def halo_copies(sends, k_ref, v_ref, kp_ref, vp_ref, relay_ref):
    x, y, z, c = place()
    pos = lax.axis_index("outer") * 16 + lax.axis_index("inner")
    rows = k_ref.shape[0]
    short = WIN - 2 * rows
    ahead, behind = device_of(pos + 2), device_of(pos - 2)
    partner = device_at(x, y, z, 1 - c)
    down, up = device_at(x, (y + 3) % NY, z, c), device_at(x, (y + 1) % NY, z, c)
    relay_to = relay_target()
    pairs = ((k_ref, kp_ref), (v_ref, vp_ref))
    mid, end = pl.ds(short, rows), pl.ds(short + rows, rows)
    head, tail = pl.ds(0, short), pl.ds(rows - short, short)

    def put(n, src, dst, to):
        sends.copy(n, src, dst, to).start()

    for n, (own, prev) in enumerate(pairs):
        put(n, own, prev.at[mid], ahead)

        @pl.when(c == 0)
        def _():
            put(2 + n, own, prev.at[end], partner)

        @pl.when(c == 1)
        def _():
            put(6 + n, own.at[tail], relay_ref.at[n], down)

        yield

    for n, (own, prev) in enumerate(pairs):

        @pl.when(c == 1)
        def _():
            sends.copy(6 + n, relay_ref.at[n], relay_ref.at[n], up).wait_recv()
            put(4 + n, relay_ref.at[n], prev.at[head], relay_to)

        yield
    for n, (own, prev) in enumerate(pairs):
        sends.arrived(n, prev.at[mid], behind)

        @pl.when(c == 0)
        def _():
            put(4 + n, prev.at[pl.ds(rows, short)], prev.at[head], partner)

        @pl.when(c == 1)
        def _():
            put(2 + n, prev.at[mid], prev.at[end], partner)

        yield
    for n, (own, prev) in enumerate(pairs):
        sends.arrived(2 + n, prev.at[end], partner)
        sends.arrived(4 + n, prev.at[head], partner)
        sends.copy(n, own, prev.at[mid], ahead).wait_send()
        sends.copy(2 + n, own, prev.at[end], partner).wait_send()
        sends.copy(4 + n, own.at[tail], prev.at[head], partner).wait_send()

        @pl.when(c == 1)
        def _():
            sends.copy(6 + n, own.at[tail], relay_ref.at[n], down).wait_send()

    yield


def relay_target():
    x, y, z, c = place()
    pos = lax.axis_index("outer") * 16 + lax.axis_index("inner")
    above_o, above_i = device_at(x, (y + 1) % NY, z, 1)
    to_o, to_i = device_of(above_o * 16 + above_i + 3)
    from_o, from_i = device_of(pos - 3)
    fx, fy, fz = (from_o % 2) * 2 + from_i // 8, (from_i // 2) % NY, from_o // 2
    by_o, by_i = device_at(fx, (fy + 3) % NY, fz, 1)
    return jnp.where(c == 1, to_o, by_o), jnp.where(c == 1, to_i, by_i)


def fine_kernel(
    x_ref, q_ref, k_ref, v_ref, w_src, gain_ref,
    state_ref, pooled_ref, normed_ref,
    mix_ref, edge_out, edge_in, kp_ref, vp_ref, relay_ref, w_ref, local_sem, send_sem, recv_sem,
):
    rows = q_ref.shape[0]
    heads = q_ref.shape[1] // HE
    position = lax.axis_index("outer") * 16 + lax.axis_index("inner")
    greet(
        plane_neighbours()
        + [device_of(position + d) for d in (2, -2, 1, -1)]
        + [relay_target()]
    )
    sends = Sends(send_sem, recv_sem, HALO_COPIES)
    weights = plane_gather(sends, w_src, w_ref, local_sem, W_FIRSTS)
    rows_before = halo_copies(sends, k_ref, v_ref, kp_ref, vp_ref, relay_ref)
    next(weights)
    next(rows_before)
    next(weights)
    next(rows_before)
    next(weights)
    run_all(rows_before)
    next(weights)
    t_prev = lax.broadcasted_iota(jnp.int32, (rows, WIN), 0)
    u_prev = lax.broadcasted_iota(jnp.int32, (rows, WIN), 1)
    ok_prev = (u_prev > t_prev) & (position * rows - WIN + u_prev >= 0)
    t_own = lax.broadcasted_iota(jnp.int32, (rows, rows), 0)
    u_own = lax.broadcasted_iota(jnp.int32, (rows, rows), 1)
    ok_own = u_own <= t_own
    for h in range(heads):
        cols = slice(h * HE, (h + 1) * HE)
        q = q_ref[:, cols]
        s_prev = lax.dot_general(q, kp_ref[:, cols], TRANS, preferred_element_type=F32) * SCALE
        s_own = lax.dot_general(q, k_ref[:, cols], TRANS, preferred_element_type=F32) * SCALE
        s_prev = jnp.where(ok_prev, s_prev, NEG)
        s_own = jnp.where(ok_own, s_own, NEG)
        top = jnp.maximum(
            jnp.max(s_prev, axis=-1, keepdims=True), jnp.max(s_own, axis=-1, keepdims=True)
        )
        p_prev = jnp.exp(s_prev - top)
        p_own = jnp.exp(s_own - top)
        total = jnp.sum(p_prev, axis=-1, keepdims=True) + jnp.sum(p_own, axis=-1, keepdims=True)
        mixed = jnp.dot(p_prev.astype(BF), vp_ref[:, cols], preferred_element_type=F32)
        mixed += jnp.dot(p_own.astype(BF), v_ref[:, cols], preferred_element_type=F32)
        mix_ref[:, cols] = (mixed / total).astype(BF)
        if h in (1, 3):
            next(weights)
    run_all(weights)
    width = x_ref.shape[1]
    half = w_ref.shape[1]
    per = w_ref.shape[2]

    @pl.loop(0, NP // 2)
    def _(n):
        at = pl.ds(pl.multiple_of(n * per, per), per)
        prod = jnp.dot(mix_ref[:, :half], w_ref[n], preferred_element_type=F32)
        prod += jnp.dot(mix_ref[:, half:], w_ref[n + NP // 2], preferred_element_type=F32)
        state_ref[:, at] = (x_ref[:, at].astype(F32) + prod).astype(BF)

    edge_out[...] = state_ref[rows - POOL :, :]
    send = pltpu.make_async_remote_copy(
        src_ref=edge_out,
        dst_ref=edge_in,
        send_sem=send_sem.at[EDGE_COPY],
        recv_sem=recv_sem.at[EDGE_COPY],
        device_id=device_of(position + 1),
        device_id_type=MESH,
    )
    send.start()
    groups = state_ref[...].astype(F32).reshape(rows // POOL, POOL, width)
    first = groups[:, 0, :]
    rest = jnp.sum(groups[:, 1:, :], axis=1)
    send.wait()
    edge = jnp.sum(edge_in[...].astype(F32)[1:, :], axis=0, keepdims=True)
    edge = jnp.where(position == 0, 0.0, edge)
    before = jnp.concatenate([edge, rest[: rows // POOL - 1, :]], axis=0)
    pooled = ((before + first) / POOL).astype(BF)
    pooled_ref[...] = pooled
    wide = pooled.astype(F32)
    moment = jnp.mean(wide * wide, axis=-1, keepdims=True)
    normed_ref[...] = (wide * lax.rsqrt(moment + 1e-06) * gain_ref[...]).astype(BF)
    sends.drain()


EDGE_COPY = HALO_COPIES + plane_copies(W_FIRSTS)


def fine_stage(x, q, k, v, w_half, gain):
    rows, width = x.shape
    coarse = jax.ShapeDtypeStruct((rows // POOL, width), BF)
    return pl.pallas_call(
        fine_kernel,
        out_shape=[jax.ShapeDtypeStruct((rows, width), BF), coarse, coarse],
        in_specs=[vmem_spec()] * 6,
        out_specs=[vmem_spec()] * 3,
        scratch_shapes=[
            pltpu.VMEM(q.shape, BF),
            pltpu.VMEM((POOL, width), BF),
            pltpu.VMEM((POOL, width), BF),
            pltpu.VMEM((WIN, k.shape[1]), BF),
            pltpu.VMEM((WIN, k.shape[1]), BF),
            pltpu.VMEM((2, WIN - 2 * rows, k.shape[1]), BF),
            pltpu.VMEM((NP, *w_half.shape), BF),
            pltpu.SemaphoreType.DMA,
            pltpu.SemaphoreType.DMA((EDGE_COPY + 1,)),
            pltpu.SemaphoreType.DMA((EDGE_COPY + 1,)),
        ],
        compiler_params=pltpu.CompilerParams(
            collective_id=2, has_side_effects=True, vmem_limit_bytes=40 << 20
        ),
        name="fine",
    )(x, q, k, v, w_half, gain.reshape(1, width))


ZCHUNK = 8
HEAD_FIRSTS = (0, 1)


def z_copies(rows):
    return (NZ - 1) * (rows // ZCHUNK)


def z_gather(sends, src_ref, dst_ref, local_sem):
    x, y, z, c = place()
    up, down = device_at(x, y, (z + 1) % NZ, c), device_at(x, y, (z + NZ - 1) % NZ, c)
    chunks = src_ref.shape[0] // ZCHUNK
    first = sends.next
    sends.next += z_copies(src_ref.shape[0])
    count_up, count_down = NZ // 2, NZ // 2 - 1
    local = pltpu.make_async_copy(src_ref, dst_ref.at[z], local_sem)
    for s in range(count_up + 1):
        for part in range(chunks):
            at = pl.ds(part * ZCHUNK, ZCHUNK)
            for sign, count, base, to, origin in (
                (-1, count_up, first, up, down),
                (1, count_down, first + count_up * chunks, down, up),
            ):
                if s > count:
                    continue
                held = (z + sign * s + NZ) % NZ
                if s > 0:
                    sends.arrived(base + (s - 1) * chunks + part, dst_ref.at[held, at], origin)
                if s < count:
                    src = src_ref.at[at] if s == 0 else dst_ref.at[held, at]
                    sends.start(base + s * chunks + part, src, dst_ref.at[held, at], to)
        if s == 0:
            local.start()
        if s == count_up:
            local.wait()
        yield


def scatter(src_ref, dst_ref, local_sem, send_sem, recv_sem):
    outer = lax.axis_index("outer")
    inner = lax.axis_index("inner")
    head = outer // 2

    @pl.when(inner == head)
    def _():
        pltpu.make_async_copy(src_ref.at[inner], dst_ref, local_sem).start()
        for d in range(1, 16):
            to = (inner + d) % 16
            pltpu.make_async_remote_copy(
                src_ref=src_ref.at[to],
                dst_ref=dst_ref,
                send_sem=send_sem.at[d - 1],
                recv_sem=recv_sem,
                device_id=(outer, to),
                device_id_type=MESH,
            ).start()

    yield

    @pl.when(inner == head)
    def _():
        pltpu.make_async_copy(src_ref.at[inner], dst_ref, local_sem).wait()
        for d in range(1, 16):
            pltpu.make_async_copy(src_ref.at[0], src_ref.at[0], send_sem.at[d - 1]).wait()

    @pl.when(inner != head)
    def _():
        pltpu.make_async_copy(dst_ref, dst_ref, recv_sem).wait()

    yield


def middle_kernel(
    normed_ref, pieces_ref, w_src, tokens_ref, head_ref, w_ref,
    piece_ref, local_sem, scatter_send, scatter_recv, send_sem, recv_sem,
):
    x, y, z, c = place()
    outer = lax.axis_index("outer")
    inner = lax.axis_index("inner")
    ends = [device_at(x, y, (z + 1) % NZ, c), device_at(x, y, (z + NZ - 1) % NZ, c)]
    greet(plane_neighbours() + ends + [(outer, (inner + d) % 16) for d in range(1, 16)])
    sends = Sends(send_sem, recv_sem)
    along = z_gather(sends, normed_ref, tokens_ref, local_sem.at[0])
    pieces = scatter(pieces_ref, piece_ref, local_sem.at[1], scatter_send, scatter_recv)
    head = plane_gather(sends, piece_ref, head_ref, local_sem.at[2], HEAD_FIRSTS)
    out = plane_gather(sends, w_src, w_ref, local_sem.at[3])
    next(along)
    next(pieces)
    next(out)
    next(along)
    next(along)
    next(pieces)
    next(head)
    next(out)
    next(along)
    next(head)
    next(out)
    next(along)
    next(head)
    next(out)
    next(along)
    next(head)
    next(out)
    next(along)
    next(head)
    next(out)
    next(along)
    next(head)
    next(along)
    run_all(head)
    run_all(out)
    sends.drain()


def middle_stage(normed, pieces, w_half):
    count = z_copies(normed.shape[0]) + plane_copies(HEAD_FIRSTS) + plane_copies((0, 1))
    return pl.pallas_call(
        middle_kernel,
        out_shape=[
            jax.ShapeDtypeStruct((NZ, *normed.shape), BF),
            jax.ShapeDtypeStruct((NP, *pieces.shape[1:]), BF),
            jax.ShapeDtypeStruct((NP, *w_half.shape), BF),
        ],
        in_specs=[any_spec()] * 3,
        out_specs=[any_spec()] * 3,
        scratch_shapes=[
            pltpu.VMEM(pieces.shape[1:], BF),
            pltpu.SemaphoreType.DMA((4,)),
            pltpu.SemaphoreType.DMA((15,)),
            pltpu.SemaphoreType.DMA,
            pltpu.SemaphoreType.DMA((count,)),
            pltpu.SemaphoreType.DMA((count,)),
        ],
        compiler_params=pltpu.CompilerParams(
            collective_id=3, has_side_effects=True, vmem_limit_bytes=16 << 20
        ),
        name="middle",
    )(normed, pieces, w_half)


KEY_GROUP = 8
PLANE_GROUP = 4


def coarse_kernel(
    proj_ref, out_ref,
    kv_ref, top_ref, acc_ref, mix_ref, heads_ref, local_sem, send_sem, recv_sem,
):
    x, y, z, c = place()
    others = [device_at(x, y, (z + d) % NZ, c) for d in range(1, NZ)]
    greet(plane_neighbours() + others)
    sends = Sends(send_sem, recv_sem, NZ - 1)
    run_all(plane_gather(sends, proj_ref.at[:, HE:], kv_ref, local_sem))
    me = slot_of(x, y, c)
    count = proj_ref.shape[0]
    per = count // NZ
    step = PLANE_GROUP * per
    factor = SCALE * LOG2E
    top_ref[...] = jnp.full(top_ref.shape, NEG, F32)
    acc_ref[...] = jnp.zeros(acc_ref.shape, F32)
    width = KEY_GROUP * step
    ones = jnp.ones((width, HE), BF)
    t = lax.broadcasted_iota(jnp.int32, (step, 1), 0)
    u = lax.broadcasted_iota(jnp.int32, (1, width), 1)
    t_order = (t // per * NP + me) * 32 + t % per
    u_order = (u % step // per * NP + u // step) * 32 + u % per

    @pl.loop(0, NP // KEY_GROUP)
    def _(g):
        some = pl.ds(g * KEY_GROUP, KEY_GROUP)
        allowed = u_order <= t_order - g * (KEY_GROUP * 32)
        for n in range(NZ // PLANE_GROUP):
            lo = n * step
            keys = kv_ref[some, lo : lo + step, :HE].reshape(width, HE)
            values = kv_ref[some, lo : lo + step, HE:].reshape(width, HE)
            s = lax.dot_general(
                proj_ref[lo:, :HE], keys, TRANS, preferred_element_type=F32
            ) * factor
            edge = jnp.where(allowed, s[:step], NEG)
            s = jnp.concatenate([edge, s[step:]], axis=0) if lo + step < count else edge
            old = top_ref[lo:, :]
            new = jnp.maximum(old, jnp.max(s, axis=-1, keepdims=True))
            p = jnp.exp2(s - new).astype(BF)
            wide = jnp.concatenate([values, ones], axis=1)
            acc_ref[lo:, :] = acc_ref[lo:, :] * jnp.exp2(old - new) + jnp.dot(
                p, wide, preferred_element_type=F32
            )
            top_ref[lo:, :] = new

    mix_ref[...] = (acc_ref[:, :HE] / acc_ref[:, HE:]).astype(BF).reshape(mix_ref.shape)
    for d in (8, 7, 9, 6, 10, 5, 11, 4, 12, 3, 13, 2, 14, 1, 15):
        sends.start(d - 1, mix_ref.at[(z + d) % NZ], heads_ref.at[z], others[d - 1])
    heads_ref[z] = mix_ref[z]
    for d in range(1, NZ):
        origin = (z + NZ - d) % NZ
        sends.arrived(d - 1, heads_ref.at[origin], others[NZ - d - 1])
    sends.drain()
    out_ref[...] = heads_ref[...]


def coarse_stage(proj):
    rows = proj.shape[0]
    count = NZ - 1 + plane_copies((0, 1))
    return pl.pallas_call(
        coarse_kernel,
        out_shape=jax.ShapeDtypeStruct((NZ, rows // NZ, HE), BF),
        in_specs=[vmem_spec()],
        out_specs=vmem_spec(),
        scratch_shapes=[
            pltpu.VMEM((NP, rows, 2 * HE), BF),
            pltpu.VMEM((rows, 1), F32),
            pltpu.VMEM((rows, 2 * HE), F32),
            pltpu.VMEM((NZ, rows // NZ, HE), BF),
            pltpu.VMEM((NZ, rows // NZ, HE), BF),
            pltpu.SemaphoreType.DMA,
            pltpu.SemaphoreType.DMA((count,)),
            pltpu.SemaphoreType.DMA((count,)),
        ],
        compiler_params=pltpu.CompilerParams(
            collective_id=4, has_side_effects=True, vmem_limit_bytes=40 << 20
        ),
        name="coarse",
    )(proj)


def on_device(
    fine_input,
    fine_query,
    fine_key,
    fine_value,
    w_fine_out,
    norm_gain,
    w_query,
    w_key,
    w_value,
    w_coarse_out,
):
    rows, width = fine_input.shape
    copy = lax.axis_index("outer") % 2

    def half_of(w):
        size = w.shape[0] // 2
        return lax.dynamic_slice_in_dim(w, copy * size, size, 0)

    state, pooled, normed = fine_stage(
        fine_input, fine_query, fine_key, fine_value, half_of(w_fine_out), norm_gain
    )
    joined = jnp.concatenate([half_of(w_query), half_of(w_key), half_of(w_value)], axis=1)
    pieces = joined.reshape(16, -1, joined.shape[1])
    tokens, w_head, w_out = middle_stage(normed, pieces, half_of(w_coarse_out))
    proj = jnp.dot(
        tokens.reshape(-1, width), w_head.reshape(width, -1), preferred_element_type=F32
    ).astype(BF)
    heads = coarse_stage(proj)
    heads = heads.reshape(NZ, rows // POOL, 2, HE // 2).transpose(1, 2, 0, 3)
    head_total = jnp.dot(
        heads.reshape(rows // POOL, -1), w_out.reshape(-1, width), preferred_element_type=F32
    )
    coarse_out = (pooled.astype(F32) + head_total).astype(BF)
    groups = state.reshape(rows // POOL, POOL, width).astype(F32)
    lifted = groups + coarse_out.astype(F32)[:, None, :]
    return lifted.reshape(rows, width).astype(BF)


def solution(mesh):
    placed = (
        P(("outer", "inner"), None),
        P(("outer", "inner"), None),
        P(("outer", "inner"), None),
        P(("outer", "inner"), None),
        P(None, "inner"),
        P(),
        P(None, "inner"),
        P(None, "inner"),
        P(None, "inner"),
        P("inner", None),
    )
    return jax.shard_map(
        on_device,
        mesh=mesh,
        in_specs=placed,
        out_specs=P(("outer", "inner"), None),
        check_vma=False,
    )
```

```python
import functools
import math

import jax
import jax.numpy as jnp
from jax import lax
from jax.experimental import pallas as pl
from jax.experimental.pallas import tpu as pltpu
from jax.sharding import PartitionSpec as P

HE = 128
WIN = 512
POOL = 8
NEG = -1e30
LOG2E = math.log2(math.e)
SCALE = 1.0 / math.sqrt(HE)
BF = jnp.bfloat16
F32 = jnp.float32
TRANS = (((1,), (1,)), ((), ()))
MESH = pl.DeviceIdType.MESH
NX, NY, NZ, NC = 4, 4, 16, 2
NP = NX * NY * NC


def vmem_spec():
    return pl.BlockSpec(memory_space=pltpu.VMEM)


def any_spec():
    return pl.BlockSpec(memory_space=pl.ANY)


def hbm_spec():
    return pl.BlockSpec(memory_space=pltpu.HBM)


def in_hbm(a):
    return pltpu.with_memory_space_constraint(a, pltpu.HBM)


def place():
    outer = lax.axis_index("outer")
    inner = lax.axis_index("inner")
    x = (outer % 2) * 2 + inner // 8
    return x, (inner // 2) % NY, outer // 2, inner % NC


def device_at(x, y, z, c):
    return (z * 2 + x // 2, (x % 2) * 8 + y * 2 + c)


def device_of(pos):
    pos = (pos + 512) % 512
    return (pos // 16, pos % 16)


def slot_of(x, y, c):
    return x * 8 + y * 2 + c


def greet(devices):
    barrier = pltpu.get_barrier_semaphore()
    for d in devices:
        pl.semaphore_signal(barrier, inc=1, device_id=d, device_id_type=MESH)
    pl.semaphore_wait(barrier, len(devices))


def plane_neighbours():
    x, y, z, c = place()
    return [
        device_at((x + 1) % NX, y, z, c),
        device_at((x + 3) % NX, y, z, c),
        device_at(x, (y + 1) % NY, z, c),
        device_at(x, (y + 3) % NY, z, c),
        device_at(x, y, z, 1 - c),
    ]


class Sends:
    def __init__(self, send_sem, recv_sem, base=0):
        self.send_sem, self.recv_sem, self.next = send_sem, recv_sem, base
        self.started = []

    def new(self):
        self.next += 1
        return self.next - 1

    def copy(self, k, src, dst, to):
        return pltpu.make_async_remote_copy(
            src_ref=src,
            dst_ref=dst,
            send_sem=self.send_sem.at[k],
            recv_sem=self.recv_sem.at[k],
            device_id=to,
            device_id_type=MESH,
        )

    def start(self, k, src, dst, to):
        c = self.copy(k, src, dst, to)
        c.start()
        self.started.append(c)

    def arrived(self, k, dst, to):
        self.copy(k, dst, dst, to).wait_recv()

    def drain(self):
        for c in self.started:
            c.wait_send()
        self.started = []


def plane_copies(firsts):
    return 35 * len(firsts) + 1


def plane_gather(sends, src, dst, local_sem, firsts=(0, 1)):
    x, y, z, c = place()
    part = src.shape[0] // len(firsts)

    def near(axis, off):
        if axis == 0:
            return device_at((x + off) % NX, y, z, c)
        return device_at(x, (y + off) % NY, z, c)

    def at(axis, a, b):
        if axis == 0:
            return slot_of((x + a) % NX, (y + b) % NY, c)
        return slot_of((x + b) % NX, (y + a) % NY, c)

    partner = device_at(x, y, z, 1 - c)
    halves = []
    for n, first in enumerate(firsts):
        lo = n * part
        h = dict(first=first, whole=pl.ds(lo, part), k={})
        h["q0"] = pl.ds(lo, part // 2)
        h["q1"] = pl.ds(lo + part // 2, part // 2)
        for name in ("r1", "l1", "r2", "l2"):
            h["k"][name] = sends.new()
        for j in (0, -1, 1, 2):
            for name in ("r1", "l1", "r2", "l2"):
                h["k"][name, j] = sends.new()
        for j in (0, -1, 1, 2):
            for i in (0, -1, 1, 2):
                if (i, j) != (0, 0):
                    h["k"]["p", j, i] = sends.new()
        halves.append(h)
    own_pair = sends.new()
    mine = slot_of(x, y, c)
    theirs = slot_of(x, y, 1 - c)
    local = pltpu.make_async_copy(src, dst.at[mine], local_sem)

    def to_partner(h, j, i):
        s = at(h["first"], j, i)
        sends.start(h["k"]["p", j, i], dst.at[s, h["whole"]], dst.at[s, h["whole"]], partner)

    for second_axis in (False, True):
        for h in halves:
            a = 1 - h["first"] if second_axis else h["first"]
            for name, off in (("r1", 1), ("l1", -1)):
                k = h["k"][(name, 0) if second_axis else name]
                sends.start(k, src.at[h["whole"]], dst.at[mine, h["whole"]], near(a, off % 4))
    sends.start(own_pair, src, dst.at[mine], partner)
    local.start()
    yield

    def second(h, j):
        s = at(h["first"], j, 0)
        for name, off in (("r1", 1), ("l1", -1)):
            sends.start(
                h["k"][name, j],
                dst.at[s, h["whole"]],
                dst.at[s, h["whole"]],
                near(1 - h["first"], off % 4),
            )
        to_partner(h, j, 0)

    directions = (("r1", "r2", -1, "q0"), ("l1", "l2", 1, "q1"))
    for h in halves:
        a = h["first"]
        for name, fwd, off, q in directions:
            s = at(a, off, 0)
            sends.arrived(h["k"][name], dst.at[s, h["whole"]], near(a, off % 4))
            sends.start(h["k"][fwd], dst.at[s, h[q]], dst.at[s, h[q]], near(a, (-off) % 4))
    for h in halves:
        for off in (-1, 1):
            second(h, off)
    yield

    def relay(h, j):
        b = 1 - h["first"]
        for name, fwd, off, q in directions:
            s = at(h["first"], j, off)
            sends.arrived(h["k"][name, j], dst.at[s, h["whole"]], near(b, off % 4))
            sends.start(h["k"][fwd, j], dst.at[s, h[q]], dst.at[s, h[q]], near(b, (-off) % 4))
            to_partner(h, j, off)

    for h in halves:
        relay(h, 0)
    yield
    for h in halves:
        a = h["first"]
        s = at(a, 2, 0)
        sends.arrived(h["k"]["r2"], dst.at[s, h["q0"]], near(a, 3))
        sends.arrived(h["k"]["l2"], dst.at[s, h["q1"]], near(a, 1))
        second(h, 2)
    yield

    def last(h, j):
        b = 1 - h["first"]
        s = at(h["first"], j, 2)
        sends.arrived(h["k"]["r2", j], dst.at[s, h["q0"]], near(b, 3))
        sends.arrived(h["k"]["l2", j], dst.at[s, h["q1"]], near(b, 1))
        to_partner(h, j, 2)

    for j in (-1, 1):
        for h in halves:
            relay(h, j)
    for h in halves:
        last(h, 0)
    yield
    for h in halves:
        relay(h, 2)
    for j in (-1, 1):
        for h in halves:
            last(h, j)
    yield
    for h in halves:
        last(h, 2)
    local.wait()
    sends.arrived(own_pair, dst.at[theirs], partner)
    for h in halves:
        for j in (0, -1, 1, 2):
            for i in (0, -1, 1, 2):
                if (i, j) != (0, 0):
                    s = at(h["first"], j, i) + 1 - 2 * c
                    sends.arrived(h["k"]["p", j, i], dst.at[s, h["whole"]], partner)
    yield


def run_all(steps):
    for _ in steps:
        pass


HALO_COPIES = 8
W_FIRSTS = (1,)
HEAD_FIRSTS = (1,)


def halo_copies(sends, k_ref, v_ref, kp_ref, vp_ref, relay_ref):
    x, y, z, c = place()
    pos = lax.axis_index("outer") * 16 + lax.axis_index("inner")
    rows = k_ref.shape[0]
    short = WIN - 2 * rows
    ahead, behind = device_of(pos + 2), device_of(pos - 2)
    partner = device_at(x, y, z, 1 - c)
    down, up = device_at(x, (y + 3) % NY, z, c), device_at(x, (y + 1) % NY, z, c)
    relay_to = relay_target()
    pairs = ((k_ref, kp_ref), (v_ref, vp_ref))
    mid, end = pl.ds(short, rows), pl.ds(short + rows, rows)
    head, tail = pl.ds(0, short), pl.ds(rows - short, short)

    def put(n, src, dst, to):
        sends.copy(n, src, dst, to).start()

    for n, (own, prev) in enumerate(pairs):
        put(n, own, prev.at[mid], ahead)

        @pl.when(c == 0)
        def _():
            put(2 + n, own, prev.at[end], partner)

        @pl.when(c == 1)
        def _():
            put(6 + n, own.at[tail], relay_ref.at[n], down)

        yield

    for n, (own, prev) in enumerate(pairs):

        @pl.when(c == 1)
        def _():
            sends.copy(6 + n, relay_ref.at[n], relay_ref.at[n], up).wait_recv()
            put(4 + n, relay_ref.at[n], prev.at[head], relay_to)

        yield
    for n, (own, prev) in enumerate(pairs):
        sends.arrived(n, prev.at[mid], behind)

        @pl.when(c == 0)
        def _():
            put(4 + n, prev.at[pl.ds(rows, short)], prev.at[head], partner)

        @pl.when(c == 1)
        def _():
            put(2 + n, prev.at[mid], prev.at[end], partner)

        yield
    for n, (own, prev) in enumerate(pairs):
        sends.arrived(2 + n, prev.at[end], partner)
        sends.arrived(4 + n, prev.at[head], partner)
        sends.copy(n, own, prev.at[mid], ahead).wait_send()
        sends.copy(2 + n, own, prev.at[end], partner).wait_send()
        sends.copy(4 + n, own.at[tail], prev.at[head], partner).wait_send()

        @pl.when(c == 1)
        def _():
            sends.copy(6 + n, own.at[tail], relay_ref.at[n], down).wait_send()

    yield


def relay_target():
    x, y, z, c = place()
    pos = lax.axis_index("outer") * 16 + lax.axis_index("inner")
    above_o, above_i = device_at(x, (y + 1) % NY, z, 1)
    to_o, to_i = device_of(above_o * 16 + above_i + 3)
    from_o, from_i = device_of(pos - 3)
    fx, fy, fz = (from_o % 2) * 2 + from_i // 8, (from_i // 2) % NY, from_o // 2
    by_o, by_i = device_at(fx, (fy + 3) % NY, fz, 1)
    return jnp.where(c == 1, to_o, by_o), jnp.where(c == 1, to_i, by_i)


def fine_kernel(
    gain_ref, x_src, q_src, k_src, v_src, w_src, wq_ref, wk_ref, wv_ref,
    state_ref, pooled_ref, normed_ref, head_ref,
    x_ref, q_ref, k_ref, v_ref,
    mix_ref, edge_out, edge_in, kp_ref, vp_ref, relay_ref, w_ref, piece_ref,
    load_sem, local_sem, scatter_send, scatter_recv, send_sem, recv_sem,
):
    rows = q_ref.shape[0]
    heads = q_ref.shape[1] // HE
    outer = lax.axis_index("outer")
    inner = lax.axis_index("inner")
    position = outer * 16 + inner
    greet(
        plane_neighbours()
        + [device_of(position + d) for d in (2, -2, 1, -1)]
        + [relay_target()]
        + [(outer, (inner + d) % 16) for d in range(1, 16)]
    )
    sends = Sends(send_sem, recv_sem, HALO_COPIES)
    weights = plane_gather(sends, half_rows(w_src), w_ref, local_sem.at[0], W_FIRSTS)
    head = plane_gather(sends, piece_ref, head_ref, local_sem.at[1], HEAD_FIRSTS)
    pieces = scatter((wq_ref, wk_ref, wv_ref), piece_ref, local_sem.at[pl.ds(2, 3)], scatter_send, scatter_recv)
    rows_before = halo_copies(sends, k_src, v_src, kp_ref, vp_ref, relay_ref)
    next(weights)
    next(rows_before)
    next(pieces)
    loads = [
        pltpu.make_async_copy(src, dst, load_sem.at[n])
        for n, (src, dst) in enumerate(
            ((q_src, q_ref), (k_src, k_ref), (v_src, v_ref), (x_src, x_ref))
        )
    ]
    for load in loads:
        load.start()
    next(weights)
    next(rows_before)
    next(weights)
    next(rows_before)
    next(weights)
    next(rows_before)
    next(pieces)
    next(head)
    next(weights)
    next(rows_before)
    next(head)
    next(weights)
    next(rows_before)
    next(head)
    run_all(rows_before)
    for load in loads:
        load.wait()
    t_prev = lax.broadcasted_iota(jnp.int32, (rows, WIN), 0)
    u_prev = lax.broadcasted_iota(jnp.int32, (rows, WIN), 1)
    ok_prev = (u_prev > t_prev) & (position * rows - WIN + u_prev >= 0)
    t_own = lax.broadcasted_iota(jnp.int32, (rows, rows), 0)
    u_own = lax.broadcasted_iota(jnp.int32, (rows, rows), 1)
    ok_own = u_own <= t_own
    for h in range(heads):
        cols = slice(h * HE, (h + 1) * HE)
        q = q_ref[:, cols]
        s_prev = lax.dot_general(q, kp_ref[:, cols], TRANS, preferred_element_type=F32) * SCALE
        s_own = lax.dot_general(q, k_ref[:, cols], TRANS, preferred_element_type=F32) * SCALE
        s_prev = jnp.where(ok_prev, s_prev, NEG)
        s_own = jnp.where(ok_own, s_own, NEG)
        top = jnp.maximum(
            jnp.max(s_prev, axis=-1, keepdims=True), jnp.max(s_own, axis=-1, keepdims=True)
        )
        p_prev = jnp.exp(s_prev - top)
        p_own = jnp.exp(s_own - top)
        total = jnp.sum(p_prev, axis=-1, keepdims=True) + jnp.sum(p_own, axis=-1, keepdims=True)
        mixed = jnp.dot(p_prev.astype(BF), vp_ref[:, cols], preferred_element_type=F32)
        mixed += jnp.dot(p_own.astype(BF), v_ref[:, cols], preferred_element_type=F32)
        mix_ref[:, cols] = (mixed / total).astype(BF)
        if h in (1, 3, 5):
            next(head)
    run_all(weights)
    width = x_ref.shape[1]
    half = w_ref.shape[1]
    per = w_ref.shape[2]

    @pl.loop(0, NP // 4)
    def _(m):
        n = 2 * m
        at = pl.ds(pl.multiple_of(n * per, 2 * per), 2 * per)
        upper = jnp.concatenate([w_ref[n], w_ref[n + 1]], axis=1)
        lower = jnp.concatenate([w_ref[n + NP // 2], w_ref[n + 1 + NP // 2]], axis=1)
        prod = jnp.dot(mix_ref[:, :half], upper, preferred_element_type=F32)
        prod += jnp.dot(mix_ref[:, half:], lower, preferred_element_type=F32)
        state_ref[:, at] = (x_ref[:, at].astype(F32) + prod).astype(BF)

    edge_out[...] = state_ref[rows - POOL :, :]
    send = pltpu.make_async_remote_copy(
        src_ref=edge_out,
        dst_ref=edge_in,
        send_sem=send_sem.at[EDGE_COPY],
        recv_sem=recv_sem.at[EDGE_COPY],
        device_id=device_of(position + 1),
        device_id_type=MESH,
    )
    send.start()
    groups = state_ref[...].astype(F32).reshape(rows // POOL, POOL, width)
    first = groups[:, 0, :]
    rest = jnp.sum(groups[:, 1:, :], axis=1)
    send.wait()
    edge = jnp.sum(edge_in[...].astype(F32)[1:, :], axis=0, keepdims=True)
    edge = jnp.where(position == 0, 0.0, edge)
    before = jnp.concatenate([edge, rest[: rows // POOL - 1, :]], axis=0)
    pooled = ((before + first) / POOL).astype(BF)
    pooled_ref[...] = pooled
    wide = pooled.astype(F32)
    moment = jnp.mean(wide * wide, axis=-1, keepdims=True)
    normed_ref[...] = (wide * lax.rsqrt(moment + 1e-06) * gain_ref[...]).astype(BF)
    run_all(head)
    sends.drain()


EDGE_COPY = HALO_COPIES + plane_copies(W_FIRSTS) + plane_copies(HEAD_FIRSTS)


def fine_stage(x, q, k, v, gain, w, *head_weights):
    rows, width = x.shape
    coarse = jax.ShapeDtypeStruct((rows // POOL, width), BF)
    piece = (width // NP, len(head_weights) * HE)
    return pl.pallas_call(
        fine_kernel,
        out_shape=[
            jax.ShapeDtypeStruct((rows, width), BF),
            coarse,
            coarse,
            jax.ShapeDtypeStruct((NP, *piece), BF),
        ],
        in_specs=[vmem_spec()] + [hbm_spec()] * 8,
        out_specs=[vmem_spec()] * 3 + [any_spec()],
        scratch_shapes=[
            *[pltpu.VMEM(a.shape, BF) for a in (x, q, k, v)],
            pltpu.VMEM(q.shape, BF),
            pltpu.VMEM((POOL, width), BF),
            pltpu.VMEM((POOL, width), BF),
            pltpu.VMEM((WIN, k.shape[1]), BF),
            pltpu.VMEM((WIN, k.shape[1]), BF),
            pltpu.VMEM((2, WIN - 2 * rows, k.shape[1]), BF),
            pltpu.VMEM((NP, w.shape[0] // 2, w.shape[1]), BF),
            pltpu.VMEM(piece, BF),
            pltpu.SemaphoreType.DMA((4,)),
            pltpu.SemaphoreType.DMA((5,)),
            pltpu.SemaphoreType.DMA((3, 15)),
            pltpu.SemaphoreType.DMA((3,)),
            pltpu.SemaphoreType.DMA((EDGE_COPY + 1,)),
            pltpu.SemaphoreType.DMA((EDGE_COPY + 1,)),
        ],
        compiler_params=pltpu.CompilerParams(
            collective_id=2, has_side_effects=True, vmem_limit_bytes=32 << 20
        ),
        name="fine",
    )(gain.reshape(1, width), *[in_hbm(a) for a in (x, q, k, v, w, *head_weights)])


ZCHUNK = 8


def z_copies(rows):
    return (NZ - 1) * (rows // ZCHUNK)


LEAP = 4


def z_gather(sends, src_ref, dst_ref, local_sem):
    x, y, z, c = place()
    chunks = src_ref.shape[0] // ZCHUNK
    first = sends.next
    sends.next += z_copies(src_ref.shape[0])
    ways = ((1, NZ // 2, first), (-1, NZ // 2 - 1, first + NZ // 2 * chunks))
    local = pltpu.make_async_copy(src_ref, dst_ref.at[z], local_sem)

    def far(d):
        return device_at(x, y, (z + d + NZ) % NZ, c)

    def reach(d, direct):
        return LEAP if direct else 1

    def send(d, part, way):
        sign, count, base = way
        if d > count:
            return
        at = pl.ds(part * ZCHUNK, ZCHUNK)
        own = d in (1, LEAP)
        held = z if own else (z - sign * (d - 1) + NZ) % NZ
        src = src_ref.at[at] if own else dst_ref.at[held, at]
        sends.start(
            base + (d - 1) * chunks + part, src, dst_ref.at[held, at], far(sign * reach(d, d == LEAP))
        )

    def receive(d, part, way):
        sign, count, base = way
        if d > count:
            return
        at = pl.ds(part * ZCHUNK, ZCHUNK)
        held = (z - sign * d + NZ) % NZ
        sends.arrived(
            base + (d - 1) * chunks + part, dst_ref.at[held, at], far(-sign * reach(d, d == LEAP))
        )

    for d in (1, LEAP):
        for part in range(chunks):
            for way in ways:
                send(d, part, way)
    local.start()
    yield
    for d in (1, 4, 2, 5, 3, 6, 7, 8):
        for part in range(chunks):
            for way in ways:
                receive(d, part, way)
                if d + 1 not in (LEAP, NZ // 2 + 1):
                    send(d + 1, part, way)
        if d == NZ // 2:
            local.wait()
        yield


def scatter(weights, dst_ref, local_sem, send_sem, recv_sem):
    outer = lax.axis_index("outer")
    inner = lax.axis_index("inner")
    head = outer // 2
    rows = dst_ref.shape[0]
    base = (outer % 2) * (16 * rows)
    columns = [pl.ds(n * HE, HE) for n in range(len(weights))]

    def rows_of(w, to):
        return w.at[pl.ds(pl.multiple_of(base + to * rows, rows), rows)]

    def to_self(n, w):
        return pltpu.make_async_copy(rows_of(w, inner), dst_ref.at[:, columns[n]], local_sem.at[n])

    @pl.when(inner == head)
    def _():
        for n, w in enumerate(weights):
            to_self(n, w).start()
        for d in range(1, 16):
            to = (inner + d) % 16
            for n, w in enumerate(weights):
                pltpu.make_async_remote_copy(
                    src_ref=rows_of(w, to),
                    dst_ref=dst_ref.at[:, columns[n]],
                    send_sem=send_sem.at[n, d - 1],
                    recv_sem=recv_sem.at[n],
                    device_id=(outer, to),
                    device_id_type=MESH,
                ).start()

    yield

    @pl.when(inner == head)
    def _():
        for n, w in enumerate(weights):
            to_self(n, w).wait()
            for d in range(1, 16):
                piece = rows_of(w, 0)
                pltpu.make_async_copy(piece, piece, send_sem.at[n, d - 1]).wait()

    @pl.when(inner != head)
    def _():
        for n in range(len(weights)):
            piece = dst_ref.at[:, columns[n]]
            pltpu.make_async_copy(piece, piece, recv_sem.at[n]).wait()

    yield


def half_rows(w_ref):
    size = w_ref.shape[0] // 2
    copy = lax.axis_index("outer") % 2
    return w_ref.at[pl.ds(pl.multiple_of(copy * size, size), size)]


def middle_kernel(
    normed_ref, w_src, tokens_ref, w_ref, local_sem, send_sem, recv_sem
):
    x, y, z, c = place()
    greet(plane_neighbours() + [device_at(x, y, (z + d + NZ) % NZ, c) for d in (1, -1, LEAP, -LEAP)])
    sends = Sends(send_sem, recv_sem)
    along = z_gather(sends, normed_ref, tokens_ref, local_sem.at[0])
    out = plane_gather(sends, half_rows(w_src), w_ref, local_sem.at[1])
    for steps in (1, 2, 2, 1, 2, 1):
        for _ in range(steps):
            next(along)
        next(out)
    run_all(out)
    sends.drain()


def middle_stage(normed, w):
    count = z_copies(normed.shape[0]) + plane_copies((0, 1))
    return pl.pallas_call(
        middle_kernel,
        out_shape=[
            jax.ShapeDtypeStruct((NZ, *normed.shape), BF),
            jax.ShapeDtypeStruct((NP, w.shape[0] // 2, w.shape[1]), BF),
        ],
        in_specs=[any_spec(), hbm_spec()],
        out_specs=[any_spec(), hbm_spec()],
        scratch_shapes=[
            pltpu.SemaphoreType.DMA((2,)),
            pltpu.SemaphoreType.DMA((count,)),
            pltpu.SemaphoreType.DMA((count,)),
        ],
        compiler_params=pltpu.CompilerParams(
            collective_id=3, has_side_effects=True, vmem_limit_bytes=16 << 20
        ),
        name="middle",
    )(normed, w)


KEY_GROUP = 8
PLANE_GROUP = 4


def coarse_kernel(
    proj_ref, pooled_ref, w_src, out_ref,
    kv_ref, top_ref, acc_ref, mix_ref, heads_ref, w_ref, local_sem, w_sem, send_sem, recv_sem,
):
    x, y, z, c = place()
    others = [device_at(x, y, (z + d) % NZ, c) for d in range(1, NZ)]
    greet(plane_neighbours() + others)
    sends = Sends(send_sem, recv_sem, NZ - 1)
    gather = plane_gather(sends, proj_ref.at[:, HE:], kv_ref, local_sem)
    me = slot_of(x, y, c)
    count = proj_ref.shape[0]
    per = count // NZ
    step = PLANE_GROUP * per
    factor = SCALE * LOG2E
    top_ref[...] = jnp.full(top_ref.shape, NEG, F32)
    acc_ref[...] = jnp.zeros(acc_ref.shape, F32)
    width = KEY_GROUP * step
    ones = jnp.ones((width, HE), BF)
    t = lax.broadcasted_iota(jnp.int32, (step, 1), 0)
    u = lax.broadcasted_iota(jnp.int32, (1, width), 1)
    t_order = (t // per * NP + me) * 32 + t % per
    u_order = u % step // per * (NP * 32) + u % per

    def attend(slots):
        order = u_order
        for i, slot in enumerate(slots):
            order = jnp.where(u // step == i, order + slot * 32, order)
        allowed = order <= t_order
        for n in range(NZ // PLANE_GROUP):
            lo = n * step
            keys = jnp.concatenate([kv_ref[d, lo : lo + step, :HE] for d in slots], axis=0)
            values = jnp.concatenate([kv_ref[d, lo : lo + step, HE:] for d in slots], axis=0)
            s = lax.dot_general(
                proj_ref[lo:, :HE], keys, TRANS, preferred_element_type=F32
            ) * factor
            edge = jnp.where(allowed, s[:step], NEG)
            s = jnp.concatenate([edge, s[step:]], axis=0) if lo + step < count else edge
            old = top_ref[lo:, :]
            new = jnp.maximum(old, jnp.max(s, axis=-1, keepdims=True))
            p = jnp.exp2(s - new).astype(BF)
            wide = jnp.concatenate([values, ones], axis=1)
            acc_ref[lo:, :] = acc_ref[lo:, :] * jnp.exp2(old - new) + jnp.dot(
                p, wide, preferred_element_type=F32
            )
            top_ref[lo:, :] = new

    def slots_at(offsets, core):
        return [slot_of((x + a) % NX, (y + b) % NY, core) for a, b in offsets]

    early = [(0, 1), (0, 3), (1, 0), (3, 0), (1, 1), (1, 3), (3, 1), (3, 3)]
    late = [(0, 0), (0, 2), (2, 0), (2, 1), (2, 3), (1, 2), (3, 2), (2, 2)]
    next(gather)
    inners = w_ref.shape[0]
    loads = [
        pltpu.make_async_copy(w_src.at[pl.ds(n * inners, inners)], w_ref.at[:, n], w_sem.at[n])
        for n in range(w_ref.shape[1])
    ]
    for load in loads:
        load.start()
    for _ in range(5):
        next(gather)
    attend(slots_at(early, c))
    run_all(gather)
    attend(slots_at(late, c))
    attend(slots_at(early, 1 - c))
    attend(slots_at(late, 1 - c))
    mix_ref[...] = (acc_ref[:, :HE] / acc_ref[:, HE:]).astype(BF).reshape(mix_ref.shape)
    for d in (8, 7, 9, 6, 10, 5, 11, 4, 12, 3, 13, 2, 14, 1, 15):
        sends.start(d - 1, mix_ref.at[(z + d) % NZ], heads_ref.at[z], others[d - 1])
    heads_ref[z] = mix_ref[z]
    for d in range(1, NZ):
        origin = (z + NZ - d) % NZ
        sends.arrived(d - 1, heads_ref.at[origin], others[NZ - d - 1])
    sends.drain()
    for load in loads:
        load.wait()
    total = pooled_ref[...].astype(F32)
    depth = 2 * HE
    for n in range(NZ // 2):
        two = jnp.concatenate([heads_ref[2 * n], heads_ref[2 * n + 1]], axis=1)
        w = w_ref[2 * n : 2 * n + 2].reshape(depth, total.shape[1])
        total += jnp.dot(two, w, preferred_element_type=F32)
    out_ref[...] = total.astype(BF)


def coarse_stage(proj, pooled, w):
    rows = proj.shape[0]
    count = NZ - 1 + plane_copies((0, 1))
    return pl.pallas_call(
        coarse_kernel,
        out_shape=jax.ShapeDtypeStruct(pooled.shape, BF),
        in_specs=[vmem_spec(), vmem_spec(), hbm_spec()],
        out_specs=vmem_spec(),
        scratch_shapes=[
            pltpu.VMEM((NP, rows, 2 * HE), BF),
            pltpu.VMEM((rows, 1), F32),
            pltpu.VMEM((rows, 2 * HE), F32),
            pltpu.VMEM((NZ, rows // NZ, HE), BF),
            pltpu.VMEM((NZ, rows // NZ, HE), BF),
            pltpu.VMEM((NP // 2, 2, *w.shape[1:]), BF),
            pltpu.SemaphoreType.DMA,
            pltpu.SemaphoreType.DMA((2,)),
            pltpu.SemaphoreType.DMA((count,)),
            pltpu.SemaphoreType.DMA((count,)),
        ],
        compiler_params=pltpu.CompilerParams(
            collective_id=4, has_side_effects=True, vmem_limit_bytes=36 << 20
        ),
        name="coarse",
    )(proj, pooled, w)


def on_device(
    fine_input,
    fine_query,
    fine_key,
    fine_value,
    w_fine_out,
    norm_gain,
    w_query,
    w_key,
    w_value,
    w_coarse_out,
):
    rows, width = fine_input.shape
    state, pooled, normed, w_head = fine_stage(
        fine_input, fine_query, fine_key, fine_value, norm_gain, w_fine_out, w_query, w_key, w_value
    )
    tokens, w_out = middle_stage(normed, w_coarse_out)
    proj = jnp.dot(
        tokens.reshape(-1, width), w_head.reshape(width, -1), preferred_element_type=F32
    ).astype(BF)
    coarse_out = coarse_stage(proj, pooled, w_out)
    groups = state.reshape(rows // POOL, POOL, width).astype(F32)
    lifted = groups + coarse_out.astype(F32)[:, None, :]
    return lifted.reshape(rows, width).astype(BF)


def solution(mesh):
    placed = (
        P(("outer", "inner"), None),
        P(("outer", "inner"), None),
        P(("outer", "inner"), None),
        P(("outer", "inner"), None),
        P(None, "inner"),
        P(),
        P(None, "inner"),
        P(None, "inner"),
        P(None, "inner"),
        P("inner", None),
    )
    return jax.shard_map(
        on_device,
        mesh=mesh,
        in_specs=placed,
        out_specs=P(("outer", "inner"), None),
        check_vma=False,
    )
```

```python
import functools
import math

import jax
import jax.numpy as jnp
from jax import lax
from jax.experimental import pallas as pl
from jax.experimental.pallas import tpu as pltpu
from jax.sharding import PartitionSpec as P

HE = 128
WIN = 512
POOL = 8
NEG = -1e30
LOG2E = math.log2(math.e)
SCALE = 1.0 / math.sqrt(HE)
BF = jnp.bfloat16
F32 = jnp.float32
TRANS = (((1,), (1,)), ((), ()))
MESH = pl.DeviceIdType.MESH
NX, NY, NZ, NC = 4, 4, 16, 2
NP = NX * NY * NC


def vmem_spec():
    return pl.BlockSpec(memory_space=pltpu.VMEM)


def any_spec():
    return pl.BlockSpec(memory_space=pl.ANY)


def hbm_spec():
    return pl.BlockSpec(memory_space=pltpu.HBM)


def in_hbm(a):
    return pltpu.with_memory_space_constraint(a, pltpu.HBM)


def place():
    outer = lax.axis_index("outer")
    inner = lax.axis_index("inner")
    x = (outer % 2) * 2 + inner // 8
    return x, (inner // 2) % NY, outer // 2, inner % NC


def device_at(x, y, z, c):
    return (z * 2 + x // 2, (x % 2) * 8 + y * 2 + c)


def device_of(pos):
    pos = (pos + 512) % 512
    return (pos // 16, pos % 16)


def slot_of(x, y, c):
    return x * 8 + y * 2 + c


def greet(devices):
    barrier = pltpu.get_barrier_semaphore()
    for d in devices:
        pl.semaphore_signal(barrier, inc=1, device_id=d, device_id_type=MESH)
    pl.semaphore_wait(barrier, len(devices))


def plane_neighbours():
    x, y, z, c = place()
    return [
        device_at((x + 1) % NX, y, z, c),
        device_at((x + 3) % NX, y, z, c),
        device_at(x, (y + 1) % NY, z, c),
        device_at(x, (y + 3) % NY, z, c),
        device_at(x, y, z, 1 - c),
    ]


class Sends:
    def __init__(self, send_sem, recv_sem, base=0):
        self.send_sem, self.recv_sem, self.next = send_sem, recv_sem, base
        self.started = []

    def new(self):
        self.next += 1
        return self.next - 1

    def copy(self, k, src, dst, to):
        return pltpu.make_async_remote_copy(
            src_ref=src,
            dst_ref=dst,
            send_sem=self.send_sem.at[k],
            recv_sem=self.recv_sem.at[k],
            device_id=to,
            device_id_type=MESH,
        )

    def start(self, k, src, dst, to):
        c = self.copy(k, src, dst, to)
        c.start()
        self.started.append(c)

    def arrived(self, k, dst, to):
        self.copy(k, dst, dst, to).wait_recv()

    def drain(self):
        for c in self.started:
            c.wait_send()
        self.started = []


def plane_copies(firsts):
    return 35 * len(firsts) + 1


def plane_gather(sends, src, dst, local_sem, firsts=(0, 1)):
    x, y, z, c = place()
    part = src.shape[0] // len(firsts)

    def near(axis, off):
        if axis == 0:
            return device_at((x + off) % NX, y, z, c)
        return device_at(x, (y + off) % NY, z, c)

    def at(axis, a, b):
        if axis == 0:
            return slot_of((x + a) % NX, (y + b) % NY, c)
        return slot_of((x + b) % NX, (y + a) % NY, c)

    partner = device_at(x, y, z, 1 - c)
    halves = []
    for n, first in enumerate(firsts):
        lo = n * part
        h = dict(first=first, whole=pl.ds(lo, part), k={})
        h["q0"] = pl.ds(lo, part // 2)
        h["q1"] = pl.ds(lo + part // 2, part // 2)
        for name in ("r1", "l1", "r2", "l2"):
            h["k"][name] = sends.new()
        for j in (0, -1, 1, 2):
            for name in ("r1", "l1", "r2", "l2"):
                h["k"][name, j] = sends.new()
        for j in (0, -1, 1, 2):
            for i in (0, -1, 1, 2):
                if (i, j) != (0, 0):
                    h["k"]["p", j, i] = sends.new()
        halves.append(h)
    own_pair = sends.new()
    mine = slot_of(x, y, c)
    theirs = slot_of(x, y, 1 - c)
    local = pltpu.make_async_copy(src, dst.at[mine], local_sem)

    def to_partner(h, j, i):
        s = at(h["first"], j, i)
        sends.start(h["k"]["p", j, i], dst.at[s, h["whole"]], dst.at[s, h["whole"]], partner)

    for second_axis in (False, True):
        for h in halves:
            a = 1 - h["first"] if second_axis else h["first"]
            for name, off in (("r1", 1), ("l1", -1)):
                k = h["k"][(name, 0) if second_axis else name]
                sends.start(k, src.at[h["whole"]], dst.at[mine, h["whole"]], near(a, off % 4))
    sends.start(own_pair, src, dst.at[mine], partner)
    local.start()
    yield

    def second(h, j):
        s = at(h["first"], j, 0)
        for name, off in (("r1", 1), ("l1", -1)):
            sends.start(
                h["k"][name, j],
                dst.at[s, h["whole"]],
                dst.at[s, h["whole"]],
                near(1 - h["first"], off % 4),
            )
        to_partner(h, j, 0)

    directions = (("r1", "r2", -1, "q0"), ("l1", "l2", 1, "q1"))
    for h in halves:
        a = h["first"]
        for name, fwd, off, q in directions:
            s = at(a, off, 0)
            sends.arrived(h["k"][name], dst.at[s, h["whole"]], near(a, off % 4))
            sends.start(h["k"][fwd], dst.at[s, h[q]], dst.at[s, h[q]], near(a, (-off) % 4))
    for h in halves:
        for off in (-1, 1):
            second(h, off)
    yield

    def relay(h, j):
        b = 1 - h["first"]
        for name, fwd, off, q in directions:
            s = at(h["first"], j, off)
            sends.arrived(h["k"][name, j], dst.at[s, h["whole"]], near(b, off % 4))
            sends.start(h["k"][fwd, j], dst.at[s, h[q]], dst.at[s, h[q]], near(b, (-off) % 4))
            to_partner(h, j, off)

    for h in halves:
        relay(h, 0)
    yield
    for h in halves:
        a = h["first"]
        s = at(a, 2, 0)
        sends.arrived(h["k"]["r2"], dst.at[s, h["q0"]], near(a, 3))
        sends.arrived(h["k"]["l2"], dst.at[s, h["q1"]], near(a, 1))
        second(h, 2)
    yield

    def last(h, j):
        b = 1 - h["first"]
        s = at(h["first"], j, 2)
        sends.arrived(h["k"]["r2", j], dst.at[s, h["q0"]], near(b, 3))
        sends.arrived(h["k"]["l2", j], dst.at[s, h["q1"]], near(b, 1))
        to_partner(h, j, 2)

    for j in (-1, 1):
        for h in halves:
            relay(h, j)
    for h in halves:
        last(h, 0)
    yield
    for h in halves:
        relay(h, 2)
    for j in (-1, 1):
        for h in halves:
            last(h, j)
    yield
    for h in halves:
        last(h, 2)
    local.wait()
    sends.arrived(own_pair, dst.at[theirs], partner)
    for h in halves:
        for j in (0, -1, 1, 2):
            for i in (0, -1, 1, 2):
                if (i, j) != (0, 0):
                    s = at(h["first"], j, i) + 1 - 2 * c
                    sends.arrived(h["k"]["p", j, i], dst.at[s, h["whole"]], partner)
    yield


def run_all(steps):
    for _ in steps:
        pass


HALO_PARTS = 4
HALO_COPIES = 4 * HALO_PARTS
W_FIRSTS = (1,)


def halo_copies(sends, k_ref, v_ref, kp_ref, vp_ref, relay_ref):
    x, y, z, c = place()
    pos = lax.axis_index("outer") * 16 + lax.axis_index("inner")
    rows = k_ref.shape[0]
    short = WIN - 2 * rows
    ahead, behind = device_of(pos + 2), device_of(pos - 2)
    partner = device_at(x, y, z, 1 - c)
    down, up = device_at(x, (y + 3) % NY, z, c), device_at(x, (y + 1) % NY, z, c)
    relay_to = relay_target()
    half = k_ref.shape[1] // 2
    pairs = [
        (own.at[:, pl.ds(lo, half)], prev.at[:, pl.ds(lo, half)])
        for lo in (0, half)
        for own, prev in ((k_ref, kp_ref), (v_ref, vp_ref))
    ]
    count = len(pairs)
    mid, end = pl.ds(short, rows), pl.ds(short + rows, rows)
    head, tail = pl.ds(0, short), pl.ds(rows - short, short)

    def put(n, src, dst, to):
        sends.copy(n, src, dst, to).start()

    for n, (own, prev) in enumerate(pairs):
        put(n, own, prev.at[mid], ahead)

        @pl.when(c == 0)
        def _():
            put(count + n, own, prev.at[end], partner)

        @pl.when(c == 1)
        def _():
            put(3 * count + n, own.at[tail], relay_ref.at[n], down)

        yield

    for n, (own, prev) in enumerate(pairs):

        @pl.when(c == 1)
        def _():
            sends.copy(3 * count + n, relay_ref.at[n], relay_ref.at[n], up).wait_recv()
            put(2 * count + n, relay_ref.at[n], prev.at[head], relay_to)

        yield
    for group in (range(count // 2), range(count // 2, count)):
        for n in group:
            own, prev = pairs[n]
            sends.arrived(n, prev.at[mid], behind)

            @pl.when(c == 0)
            def _():
                put(2 * count + n, prev.at[pl.ds(rows, short)], prev.at[head], partner)

            @pl.when(c == 1)
            def _():
                put(count + n, prev.at[mid], prev.at[end], partner)

            yield
        for n in group:
            own, prev = pairs[n]
            sends.arrived(count + n, prev.at[end], partner)
            sends.arrived(2 * count + n, prev.at[head], partner)
            sends.copy(n, own, prev.at[mid], ahead).wait_send()
            sends.copy(count + n, own, prev.at[end], partner).wait_send()
            sends.copy(2 * count + n, own.at[tail], prev.at[head], partner).wait_send()

            @pl.when(c == 1)
            def _():
                sends.copy(3 * count + n, own.at[tail], relay_ref.at[n], down).wait_send()

            yield


def relay_target():
    x, y, z, c = place()
    pos = lax.axis_index("outer") * 16 + lax.axis_index("inner")
    above_o, above_i = device_at(x, (y + 1) % NY, z, 1)
    to_o, to_i = device_of(above_o * 16 + above_i + 3)
    from_o, from_i = device_of(pos - 3)
    fx, fy, fz = (from_o % 2) * 2 + from_i // 8, (from_i // 2) % NY, from_o // 2
    by_o, by_i = device_at(fx, (fy + 3) % NY, fz, 1)
    return jnp.where(c == 1, to_o, by_o), jnp.where(c == 1, to_i, by_i)


def fine_kernel(
    gain_ref, x_src, q_src, k_src, v_src, w_src,
    state_ref, pooled_ref, normed_ref,
    x_ref, q_ref, k_ref, v_ref, mix_ref, edge_out, edge_in, kp_ref, vp_ref, relay_ref, w_ref,
    load_sem, local_sem, send_sem, recv_sem,
):
    rows = q_ref.shape[0]
    heads = q_ref.shape[1] // HE
    position = lax.axis_index("outer") * 16 + lax.axis_index("inner")
    greet(
        plane_neighbours()
        + [device_of(position + d) for d in (2, -2, 1, -1)]
        + [relay_target()]
    )
    sends = Sends(send_sem, recv_sem, HALO_COPIES)
    weights = plane_gather(sends, half_rows(w_src), w_ref, local_sem, W_FIRSTS)
    before_rows = halo_copies(sends, k_src, v_src, kp_ref, vp_ref, relay_ref)
    loads = [
        pltpu.make_async_copy(src, dst, load_sem.at[n])
        for n, (src, dst) in enumerate(
            ((q_src, q_ref), (k_src, k_ref), (v_src, v_ref), (x_src, x_ref))
        )
    ]
    next(weights)
    next(before_rows)
    next(before_rows)
    for load in loads:
        load.start()
    for steps in (weights, before_rows, before_rows, weights, before_rows, before_rows, weights):
        next(steps)
    for steps in (before_rows,) * 4 + (weights,) + (before_rows,) * 2:
        next(steps)
    for load in loads:
        load.wait()
    between = {0: (weights,), 1: (before_rows,), 2: (before_rows,), 3: (before_rows,) * 2, 5: (weights,)}
    t_prev = lax.broadcasted_iota(jnp.int32, (rows, WIN), 0)
    u_prev = lax.broadcasted_iota(jnp.int32, (rows, WIN), 1)
    ok_prev = (u_prev > t_prev) & (position * rows - WIN + u_prev >= 0)
    t_own = lax.broadcasted_iota(jnp.int32, (rows, rows), 0)
    u_own = lax.broadcasted_iota(jnp.int32, (rows, rows), 1)
    ok_own = u_own <= t_own
    for h in range(heads):
        cols = slice(h * HE, (h + 1) * HE)
        q = q_ref[:, cols]
        s_prev = lax.dot_general(q, kp_ref[:, cols], TRANS, preferred_element_type=F32) * SCALE
        s_own = lax.dot_general(q, k_ref[:, cols], TRANS, preferred_element_type=F32) * SCALE
        s_prev = jnp.where(ok_prev, s_prev, NEG)
        s_own = jnp.where(ok_own, s_own, NEG)
        top = jnp.maximum(
            jnp.max(s_prev, axis=-1, keepdims=True), jnp.max(s_own, axis=-1, keepdims=True)
        )
        p_prev = jnp.exp(s_prev - top)
        p_own = jnp.exp(s_own - top)
        total = jnp.sum(p_prev, axis=-1, keepdims=True) + jnp.sum(p_own, axis=-1, keepdims=True)
        mixed = jnp.dot(p_prev.astype(BF), vp_ref[:, cols], preferred_element_type=F32)
        mixed += jnp.dot(p_own.astype(BF), v_ref[:, cols], preferred_element_type=F32)
        mix_ref[:, cols] = (mixed / total).astype(BF)
        for steps in between.get(h, ()):
            next(steps)
    width = x_ref.shape[1]
    half = w_ref.shape[1]
    per = w_ref.shape[2]

    @pl.loop(0, NP // 4)
    def _(m):
        n = 2 * m
        at = pl.ds(pl.multiple_of(n * per, 2 * per), 2 * per)
        upper = jnp.concatenate([w_ref[n], w_ref[n + 1]], axis=1)
        lower = jnp.concatenate([w_ref[n + NP // 2], w_ref[n + 1 + NP // 2]], axis=1)
        prod = jnp.dot(mix_ref[:, :half], upper, preferred_element_type=F32)
        prod += jnp.dot(mix_ref[:, half:], lower, preferred_element_type=F32)
        state_ref[:, at] = (x_ref[:, at].astype(F32) + prod).astype(BF)

    edge_out[...] = state_ref[rows - POOL :, :]
    send = pltpu.make_async_remote_copy(
        src_ref=edge_out,
        dst_ref=edge_in,
        send_sem=send_sem.at[EDGE_COPY],
        recv_sem=recv_sem.at[EDGE_COPY],
        device_id=device_of(position + 1),
        device_id_type=MESH,
    )
    send.start()
    groups = state_ref[...].astype(F32).reshape(rows // POOL, POOL, width)
    first = groups[:, 0, :]
    rest = jnp.sum(groups[:, 1:, :], axis=1)
    send.wait()
    edge = jnp.sum(edge_in[...].astype(F32)[1:, :], axis=0, keepdims=True)
    edge = jnp.where(position == 0, 0.0, edge)
    before = jnp.concatenate([edge, rest[: rows // POOL - 1, :]], axis=0)
    pooled = ((before + first) / POOL).astype(BF)
    pooled_ref[...] = pooled
    wide = pooled.astype(F32)
    moment = jnp.mean(wide * wide, axis=-1, keepdims=True)
    normed_ref[...] = (wide * lax.rsqrt(moment + 1e-06) * gain_ref[...]).astype(BF)
    sends.drain()


EDGE_COPY = HALO_COPIES + plane_copies(W_FIRSTS)


def fine_stage(x, q, k, v, gain, w):
    rows, width = x.shape
    coarse = jax.ShapeDtypeStruct((rows // POOL, width), BF)
    return pl.pallas_call(
        fine_kernel,
        out_shape=[jax.ShapeDtypeStruct((rows, width), BF), coarse, coarse],
        in_specs=[vmem_spec()] + [hbm_spec()] * 5,
        out_specs=[vmem_spec()] * 3,
        scratch_shapes=[
            *[pltpu.VMEM(a.shape, BF) for a in (x, q, k, v)],
            pltpu.VMEM(q.shape, BF),
            pltpu.VMEM((POOL, width), BF),
            pltpu.VMEM((POOL, width), BF),
            pltpu.VMEM((WIN, k.shape[1]), BF),
            pltpu.VMEM((WIN, k.shape[1]), BF),
            pltpu.VMEM((HALO_PARTS, WIN - 2 * rows, k.shape[1] // 2), BF),
            pltpu.VMEM((NP, w.shape[0] // 2, w.shape[1]), BF),
            pltpu.SemaphoreType.DMA((4,)),
            pltpu.SemaphoreType.DMA,
            pltpu.SemaphoreType.DMA((EDGE_COPY + 1,)),
            pltpu.SemaphoreType.DMA((EDGE_COPY + 1,)),
        ],
        compiler_params=pltpu.CompilerParams(
            collective_id=2, has_side_effects=True, vmem_limit_bytes=32 << 20
        ),
        name="fine",
    )(gain.reshape(1, width), *[in_hbm(a) for a in (x, q, k, v, w)])


ZCHUNK = 8


def z_copies(rows):
    return (NZ - 1) * (rows // ZCHUNK)


def z_gather(sends, src_ref, dst_ref, local_sem):
    x, y, z, c = place()
    up, down = device_at(x, y, (z + 1) % NZ, c), device_at(x, y, (z + NZ - 1) % NZ, c)
    chunks = src_ref.shape[0] // ZCHUNK
    first = sends.next
    sends.next += z_copies(src_ref.shape[0])
    count_up, count_down = NZ // 2, NZ // 2 - 1
    local = pltpu.make_async_copy(src_ref, dst_ref.at[z], local_sem)
    for s in range(count_up + 1):
        for part in range(chunks):
            at = pl.ds(part * ZCHUNK, ZCHUNK)
            for sign, count, base, to, origin in (
                (-1, count_up, first, up, down),
                (1, count_down, first + count_up * chunks, down, up),
            ):
                if s > count:
                    continue
                held = (z + sign * s + NZ) % NZ
                if s > 0:
                    sends.arrived(base + (s - 1) * chunks + part, dst_ref.at[held, at], origin)
                if s < count:
                    src = src_ref.at[at] if s == 0 else dst_ref.at[held, at]
                    sends.start(base + s * chunks + part, src, dst_ref.at[held, at], to)
        if s == 0:
            local.start()
        if s == count_up:
            local.wait()
        yield


def scatter(weights, dst_ref, local_sem, send_sem, recv_sem):
    outer = lax.axis_index("outer")
    inner = lax.axis_index("inner")
    head = outer // 2
    rows = dst_ref.shape[0]
    base = (outer % 2) * (16 * rows)
    columns = [pl.ds(n * HE, HE) for n in range(len(weights))]

    def rows_of(w, to):
        return w.at[pl.ds(pl.multiple_of(base + to * rows, rows), rows)]

    def to_self(n, w):
        return pltpu.make_async_copy(rows_of(w, inner), dst_ref.at[:, columns[n]], local_sem.at[n])

    @pl.when(inner == head)
    def _():
        for n, w in enumerate(weights):
            to_self(n, w).start()
        for d in range(1, 16):
            to = (inner + d) % 16
            for n, w in enumerate(weights):
                pltpu.make_async_remote_copy(
                    src_ref=rows_of(w, to),
                    dst_ref=dst_ref.at[:, columns[n]],
                    send_sem=send_sem.at[n, d - 1],
                    recv_sem=recv_sem.at[n],
                    device_id=(outer, to),
                    device_id_type=MESH,
                ).start()

    yield

    @pl.when(inner == head)
    def _():
        for n, w in enumerate(weights):
            to_self(n, w).wait()
            for d in range(1, 16):
                piece = rows_of(w, 0)
                pltpu.make_async_copy(piece, piece, send_sem.at[n, d - 1]).wait()

    @pl.when(inner != head)
    def _():
        for n in range(len(weights)):
            piece = dst_ref.at[:, columns[n]]
            pltpu.make_async_copy(piece, piece, recv_sem.at[n]).wait()

    yield


def half_rows(w_ref):
    size = w_ref.shape[0] // 2
    copy = lax.axis_index("outer") % 2
    return w_ref.at[pl.ds(pl.multiple_of(copy * size, size), size)]


PIECE_COPIES = 32


def to_all_of_plane(sends, src, dst, local_sem):
    x, y, z, c = place()
    partner = device_at(x, y, z, 1 - c)
    mine = slot_of(x, y, c)
    first = sends.next
    sends.next += PIECE_COPIES
    offsets = [(a, b) for a in range(NX) for b in range(NY)]
    local = pltpu.make_async_copy(src, dst.at[mine], local_sem)
    local.start()
    for n, (a, b) in enumerate(offsets):
        to = device_at((x + a) % NX, (y + b) % NY, z, c) if n else partner
        sends.start(first + n, src, dst.at[mine], to)
    yield
    for n, (a, b) in enumerate(offsets):
        if n:
            px, py = (x + NX - a) % NX, (y + NY - b) % NY
            s = slot_of(px, py, c)
            sends.arrived(first + n, dst.at[s], device_at(px, py, z, c))
            sends.start(first + len(offsets) + n, dst.at[s], dst.at[s], partner)
    yield
    local.wait()
    sends.arrived(first, dst.at[slot_of(x, y, 1 - c)], partner)
    for n, (a, b) in enumerate(offsets):
        if n:
            s = slot_of((x + NX - a) % NX, (y + NY - b) % NY, 1 - c)
            sends.arrived(first + len(offsets) + n, dst.at[s], partner)
    yield


def middle_kernel(
    normed_ref, w_src, wq_ref, wk_ref, wv_ref, tokens_ref, w_ref, head_ref,
    piece_ref, local_sem, scatter_send, scatter_recv, send_sem, recv_sem,
):
    x, y, z, c = place()
    outer = lax.axis_index("outer")
    inner = lax.axis_index("inner")
    plane = [(a, b) for a in range(NX) for b in range(NY)][1:]
    greet(
        [device_at((x + a) % NX, (y + b) % NY, z, c) for a, b in plane]
        + [device_at(x, y, z, 1 - c)]
        + [device_at(x, y, (z + d + NZ) % NZ, c) for d in (1, -1)]
        + [(outer, (inner + d) % 16) for d in range(1, 16)]
    )
    sends = Sends(send_sem, recv_sem)
    along = z_gather(sends, normed_ref, tokens_ref, local_sem.at[0])
    out = plane_gather(sends, half_rows(w_src), w_ref, local_sem.at[1])
    pieces = scatter((wq_ref, wk_ref, wv_ref), piece_ref, local_sem.at[pl.ds(2, 3)], scatter_send, scatter_recv)
    head = to_all_of_plane(sends, piece_ref, head_ref, local_sem.at[5])
    order = (along, pieces, out, along, along, pieces, head, out, along, out, along, out, along, out)
    for steps in order + (along, head, along, out, along, head, out):
        next(steps)
    sends.drain()


def middle_stage(normed, w, *head_weights):
    count = z_copies(normed.shape[0]) + plane_copies((0, 1)) + PIECE_COPIES
    piece = (normed.shape[1] // NP, len(head_weights) * HE)
    return pl.pallas_call(
        middle_kernel,
        out_shape=[
            jax.ShapeDtypeStruct((NZ, *normed.shape), BF),
            jax.ShapeDtypeStruct((NP, w.shape[0] // 2, w.shape[1]), BF),
            jax.ShapeDtypeStruct((NP, *piece), BF),
        ],
        in_specs=[any_spec()] + [hbm_spec()] * 4,
        out_specs=[any_spec(), hbm_spec(), any_spec()],
        scratch_shapes=[
            pltpu.VMEM(piece, BF),
            pltpu.SemaphoreType.DMA((6,)),
            pltpu.SemaphoreType.DMA((3, 15)),
            pltpu.SemaphoreType.DMA((3,)),
            pltpu.SemaphoreType.DMA((count,)),
            pltpu.SemaphoreType.DMA((count,)),
        ],
        compiler_params=pltpu.CompilerParams(
            collective_id=3, has_side_effects=True, vmem_limit_bytes=16 << 20
        ),
        name="middle",
    )(normed, *[in_hbm(a) for a in (w, *head_weights)])


PLANE_GROUP = 4
STATS = 3


def coarse_kernel(
    proj_ref, pooled_ref, w_src, out_ref,
    kv_ref, q_ref, top_ref, acc_ref, part_out, part_in, mix_ref, heads_ref, w_ref,
    w_sem, send_sem, recv_sem,
):
    x, y, z, c = place()
    others = [device_at(x, y, (z + d) % NZ, c) for d in range(1, NZ)]
    along_x = [device_at((x + d) % NX, y, z, c) for d in range(NX)]
    along_y = [device_at(x, (y + d) % NY, z, c) for d in range(NY)]
    partner = device_at(x, y, z, 1 - c)
    greet(along_x[1:] + along_y[1:] + [partner] + others)
    sends = Sends(send_sem, recv_sem)
    base_k, base_p, base_q, base_o, base_z = 0, 4, 8, 12, 16
    own_kv = proj_ref.at[:, HE:]
    own_q = proj_ref.at[:, :HE]
    mine = y * NC + c
    for d in (2, 1, 3):
        sends.start(base_k + d, own_kv, kv_ref.at[mine], along_y[d])
        sends.start(base_q + d, own_q, q_ref.at[d], along_x[d])
    sends.start(base_p, own_kv, kv_ref.at[mine], partner)
    kv_ref[mine] = proj_ref[:, HE:]
    q_ref[0] = proj_ref[:, :HE]
    inners = w_ref.shape[0]
    loads = [
        pltpu.make_async_copy(w_src.at[pl.ds(n * inners, inners)], w_ref.at[:, n], w_sem.at[n])
        for n in range(w_ref.shape[1])
    ]
    for load in loads:
        load.start()
    for d in (1, 3, 2):
        s = (y + NY - d) % NY * NC + c
        sends.arrived(base_k + d, kv_ref.at[s], along_y[NY - d])
        sends.start(base_p + d, kv_ref.at[s], kv_ref.at[s], partner)
    sends.arrived(base_p, kv_ref.at[y * NC + 1 - c], partner)
    for d in (1, 3, 2):
        sends.arrived(base_p + d, kv_ref.at[(y + NY - d) % NY * NC + 1 - c], partner)
    count = proj_ref.shape[0]
    per = count // NZ
    step = PLANE_GROUP * per
    factor = SCALE * LOG2E
    side = NY * NC
    width = side * step
    ones = jnp.ones((width, HE), BF)
    t = lax.broadcasted_iota(jnp.int32, (step, 1), 0)
    u = lax.broadcasted_iota(jnp.int32, (1, width), 1)
    t_order = t // per * (NP * 32) + t % per
    u_order = (u % step // per * NP + u // step) * 32 + u % per
    lane = lax.broadcasted_iota(jnp.int32, (count, HE), 1)

    def attend(d):
        owner = slot_of((x + NX - d) % NX, y, c)
        allowed = u_order <= t_order + (owner - side * x) * 32
        for n in range(NZ // PLANE_GROUP):
            lo = n * step
            keys = kv_ref[:, lo : lo + step, :HE].reshape(width, HE)
            values = kv_ref[:, lo : lo + step, HE:].reshape(width, HE)
            s = lax.dot_general(
                q_ref[d, lo:, :], keys, TRANS, preferred_element_type=F32
            ) * factor
            edge = jnp.where(allowed, s[:step], NEG)
            s = jnp.concatenate([edge, s[step:]], axis=0) if lo + step < count else edge
            best = jnp.max(s, axis=-1, keepdims=True)
            wide = jnp.concatenate([values, ones], axis=1)
            if n == 0:
                top_ref[...] = best
                acc_ref[...] = jnp.dot(
                    jnp.exp2(s - best).astype(BF), wide, preferred_element_type=F32
                )
            else:
                old = top_ref[lo:, :]
                new = jnp.maximum(old, best)
                acc_ref[lo:, :] = acc_ref[lo:, :] * jnp.exp2(old - new) + jnp.dot(
                    jnp.exp2(s - new).astype(BF), wide, preferred_element_type=F32
                )
                top_ref[lo:, :] = new
        weight = top_ref[...] + jnp.log2(acc_ref[:, HE:])
        return acc_ref[:, :HE] / acc_ref[:, HE:], weight

    for d in (2, 1, 3):
        sends.arrived(base_q + d, q_ref.at[d], along_x[NX - d])
        mixed, weight = attend(d)
        high = weight.astype(BF).astype(F32)
        middle = (weight - high).astype(BF).astype(F32)
        low = weight - high - middle
        pieces = jnp.where(lane < 32, high, jnp.where(lane < 64, middle, low))
        part_out[d, :, :HE] = mixed.astype(BF)
        part_out[d, :, HE:] = pieces.astype(BF)
        sends.start(base_o + d, part_out.at[d], part_in.at[d], along_x[NX - d])
    mixed, weight = attend(0)
    parts = [(mixed, weight)]
    for d in (2, 1, 3):
        sends.arrived(base_o + d, part_in.at[d], along_x[d])
        got = part_in[d, :, HE:].astype(F32)
        weight = sum(got[:, 32 * n : 32 * n + 1] for n in range(STATS))
        parts.append((part_in[d, :, :HE].astype(F32), weight + jnp.zeros((count, HE), F32)))
    best = functools.reduce(jnp.maximum, [w for _, w in parts])
    total, mixed = 0.0, 0.0
    for m, w in parts:
        share = jnp.exp2(w - best)
        total += share
        mixed += share * m
    mix_ref[...] = (mixed / total).astype(BF).reshape(mix_ref.shape)
    for d in (8, 7, 9, 6, 10, 5, 11, 4, 12, 3, 13, 2, 14, 1, 15):
        sends.start(base_z + d, mix_ref.at[(z + d) % NZ], heads_ref.at[z], others[d - 1])
    heads_ref[z] = mix_ref[z]
    for load in loads:
        load.wait()
    for d in range(1, NZ):
        origin = (z + NZ - d) % NZ
        sends.arrived(base_z + d, heads_ref.at[origin], others[NZ - d - 1])
    sends.drain()
    total = pooled_ref[...].astype(F32)
    depth = 2 * HE
    for n in range(NZ // 2):
        two = jnp.concatenate([heads_ref[2 * n], heads_ref[2 * n + 1]], axis=1)
        w = w_ref[2 * n : 2 * n + 2].reshape(depth, total.shape[1])
        total += jnp.dot(two, w, preferred_element_type=F32)
    out_ref[...] = total.astype(BF)


def coarse_stage(proj, pooled, w):
    rows = proj.shape[0]
    count = 16 + NZ
    heads = pltpu.VMEM((NZ, rows // NZ, HE), BF)
    parts = pltpu.VMEM((NX, rows, 2 * HE), BF)
    return pl.pallas_call(
        coarse_kernel,
        out_shape=jax.ShapeDtypeStruct(pooled.shape, BF),
        in_specs=[vmem_spec(), vmem_spec(), hbm_spec()],
        out_specs=vmem_spec(),
        scratch_shapes=[
            pltpu.VMEM((NY * NC, rows, 2 * HE), BF),
            pltpu.VMEM((NX, rows, HE), BF),
            pltpu.VMEM((rows, 1), F32),
            pltpu.VMEM((rows, 2 * HE), F32),
            parts,
            parts,
            heads,
            heads,
            pltpu.VMEM((NP // 2, 2, *w.shape[1:]), BF),
            pltpu.SemaphoreType.DMA((2,)),
            pltpu.SemaphoreType.DMA((count,)),
            pltpu.SemaphoreType.DMA((count,)),
        ],
        compiler_params=pltpu.CompilerParams(
            collective_id=4, has_side_effects=True, vmem_limit_bytes=36 << 20
        ),
        name="coarse",
    )(proj, pooled, w)


def on_device(
    fine_input,
    fine_query,
    fine_key,
    fine_value,
    w_fine_out,
    norm_gain,
    w_query,
    w_key,
    w_value,
    w_coarse_out,
):
    rows, width = fine_input.shape
    state, pooled, normed = fine_stage(
        fine_input, fine_query, fine_key, fine_value, norm_gain, w_fine_out
    )
    tokens, w_out, w_head = middle_stage(normed, w_coarse_out, w_query, w_key, w_value)
    proj = jnp.dot(
        tokens.reshape(-1, width), w_head.reshape(width, -1), preferred_element_type=F32
    ).astype(BF)
    coarse_out = coarse_stage(proj, pooled, w_out)
    groups = state.reshape(rows // POOL, POOL, width).astype(F32)
    lifted = groups + coarse_out.astype(F32)[:, None, :]
    return lifted.reshape(rows, width).astype(BF)


def solution(mesh):
    placed = (
        P(("outer", "inner"), None),
        P(("outer", "inner"), None),
        P(("outer", "inner"), None),
        P(("outer", "inner"), None),
        P(None, "inner"),
        P(),
        P(None, "inner"),
        P(None, "inner"),
        P(None, "inner"),
        P("inner", None),
    )
    return jax.shard_map(
        on_device,
        mesh=mesh,
        in_specs=placed,
        out_specs=P(("outer", "inner"), None),
        check_vma=False,
    )
```

```python
import functools
import math

import jax
import jax.numpy as jnp
from jax import lax
from jax.experimental import pallas as pl
from jax.experimental.pallas import tpu as pltpu
from jax.sharding import PartitionSpec as P

HE = 128
WIN = 512
POOL = 8
NEG = -1e30
LOG2E = math.log2(math.e)
SCALE = 1.0 / math.sqrt(HE)
BF = jnp.bfloat16
F32 = jnp.float32
TRANS = (((1,), (1,)), ((), ()))
MESH = pl.DeviceIdType.MESH
NX, NY, NZ, NC = 4, 4, 16, 2
NP = NX * NY * NC


def vmem_spec():
    return pl.BlockSpec(memory_space=pltpu.VMEM)


def any_spec():
    return pl.BlockSpec(memory_space=pl.ANY)


def hbm_spec():
    return pl.BlockSpec(memory_space=pltpu.HBM)


def in_hbm(a):
    return pltpu.with_memory_space_constraint(a, pltpu.HBM)


def place():
    outer = lax.axis_index("outer")
    inner = lax.axis_index("inner")
    x = (outer % 2) * 2 + inner // 8
    return x, (inner // 2) % NY, outer // 2, inner % NC


def device_at(x, y, z, c):
    return (z * 2 + x // 2, (x % 2) * 8 + y * 2 + c)


def device_of(pos):
    pos = (pos + 512) % 512
    return (pos // 16, pos % 16)


def slot_of(x, y, c):
    return x * 8 + y * 2 + c


def greet(devices):
    barrier = pltpu.get_barrier_semaphore()
    for d in devices:
        pl.semaphore_signal(barrier, inc=1, device_id=d, device_id_type=MESH)
    pl.semaphore_wait(barrier, len(devices))


def plane_neighbours():
    x, y, z, c = place()
    return [
        device_at((x + 1) % NX, y, z, c),
        device_at((x + 3) % NX, y, z, c),
        device_at(x, (y + 1) % NY, z, c),
        device_at(x, (y + 3) % NY, z, c),
        device_at(x, y, z, 1 - c),
    ]


class Sends:
    def __init__(self, send_sem, recv_sem, base=0):
        self.send_sem, self.recv_sem, self.next = send_sem, recv_sem, base
        self.started = []

    def new(self):
        self.next += 1
        return self.next - 1

    def copy(self, k, src, dst, to):
        return pltpu.make_async_remote_copy(
            src_ref=src,
            dst_ref=dst,
            send_sem=self.send_sem.at[k],
            recv_sem=self.recv_sem.at[k],
            device_id=to,
            device_id_type=MESH,
        )

    def start(self, k, src, dst, to):
        c = self.copy(k, src, dst, to)
        c.start()
        self.started.append(c)

    def arrived(self, k, dst, to):
        self.copy(k, dst, dst, to).wait_recv()

    def drain(self):
        for c in self.started:
            c.wait_send()
        self.started = []


def plane_copies(firsts):
    return 35 * len(firsts) + 1


def plane_gather(sends, src, dst, local_sem, firsts=(0, 1)):
    x, y, z, c = place()
    part = src.shape[0] // len(firsts)

    def near(axis, off):
        if axis == 0:
            return device_at((x + off) % NX, y, z, c)
        return device_at(x, (y + off) % NY, z, c)

    def at(axis, a, b):
        if axis == 0:
            return slot_of((x + a) % NX, (y + b) % NY, c)
        return slot_of((x + b) % NX, (y + a) % NY, c)

    partner = device_at(x, y, z, 1 - c)
    halves = []
    for n, first in enumerate(firsts):
        lo = n * part
        h = dict(first=first, whole=pl.ds(lo, part), k={})
        h["q0"] = pl.ds(lo, part // 2)
        h["q1"] = pl.ds(lo + part // 2, part // 2)
        for name in ("r1", "l1", "r2", "l2"):
            h["k"][name] = sends.new()
        for j in (0, -1, 1, 2):
            for name in ("r1", "l1", "r2", "l2"):
                h["k"][name, j] = sends.new()
        for j in (0, -1, 1, 2):
            for i in (0, -1, 1, 2):
                if (i, j) != (0, 0):
                    h["k"]["p", j, i] = sends.new()
        halves.append(h)
    own_pair = sends.new()
    mine = slot_of(x, y, c)
    theirs = slot_of(x, y, 1 - c)
    local = pltpu.make_async_copy(src, dst.at[mine], local_sem)

    def to_partner(h, j, i):
        s = at(h["first"], j, i)
        sends.start(h["k"]["p", j, i], dst.at[s, h["whole"]], dst.at[s, h["whole"]], partner)

    for second_axis in (False, True):
        for h in halves:
            a = 1 - h["first"] if second_axis else h["first"]
            for name, off in (("r1", 1), ("l1", -1)):
                k = h["k"][(name, 0) if second_axis else name]
                sends.start(k, src.at[h["whole"]], dst.at[mine, h["whole"]], near(a, off % 4))
    sends.start(own_pair, src, dst.at[mine], partner)
    local.start()
    yield

    def second(h, j):
        s = at(h["first"], j, 0)
        for name, off in (("r1", 1), ("l1", -1)):
            sends.start(
                h["k"][name, j],
                dst.at[s, h["whole"]],
                dst.at[s, h["whole"]],
                near(1 - h["first"], off % 4),
            )
        to_partner(h, j, 0)

    directions = (("r1", "r2", -1, "q0"), ("l1", "l2", 1, "q1"))
    for h in halves:
        a = h["first"]
        for name, fwd, off, q in directions:
            s = at(a, off, 0)
            sends.arrived(h["k"][name], dst.at[s, h["whole"]], near(a, off % 4))
            sends.start(h["k"][fwd], dst.at[s, h[q]], dst.at[s, h[q]], near(a, (-off) % 4))
    for h in halves:
        for off in (-1, 1):
            second(h, off)
    yield

    def relay(h, j):
        b = 1 - h["first"]
        for name, fwd, off, q in directions:
            s = at(h["first"], j, off)
            sends.arrived(h["k"][name, j], dst.at[s, h["whole"]], near(b, off % 4))
            sends.start(h["k"][fwd, j], dst.at[s, h[q]], dst.at[s, h[q]], near(b, (-off) % 4))
            to_partner(h, j, off)

    for h in halves:
        relay(h, 0)
    yield
    for h in halves:
        a = h["first"]
        s = at(a, 2, 0)
        sends.arrived(h["k"]["r2"], dst.at[s, h["q0"]], near(a, 3))
        sends.arrived(h["k"]["l2"], dst.at[s, h["q1"]], near(a, 1))
        second(h, 2)
    yield

    def last(h, j):
        b = 1 - h["first"]
        s = at(h["first"], j, 2)
        sends.arrived(h["k"]["r2", j], dst.at[s, h["q0"]], near(b, 3))
        sends.arrived(h["k"]["l2", j], dst.at[s, h["q1"]], near(b, 1))
        to_partner(h, j, 2)

    for j in (-1, 1):
        for h in halves:
            relay(h, j)
    for h in halves:
        last(h, 0)
    yield
    for h in halves:
        relay(h, 2)
    for j in (-1, 1):
        for h in halves:
            last(h, j)
    yield
    for h in halves:
        last(h, 2)
    local.wait()
    sends.arrived(own_pair, dst.at[theirs], partner)
    for h in halves:
        for j in (0, -1, 1, 2):
            for i in (0, -1, 1, 2):
                if (i, j) != (0, 0):
                    s = at(h["first"], j, i) + 1 - 2 * c
                    sends.arrived(h["k"]["p", j, i], dst.at[s, h["whole"]], partner)
    yield


def run_all(steps):
    for _ in steps:
        pass


HALO_PARTS = 4
HALO_COPIES = 4 * HALO_PARTS
W_FIRSTS = (1,)


def halo_copies(sends, k_ref, v_ref, kp_ref, vp_ref, relay_ref):
    x, y, z, c = place()
    pos = lax.axis_index("outer") * 16 + lax.axis_index("inner")
    rows = k_ref.shape[0]
    short = WIN - 2 * rows
    ahead, behind = device_of(pos + 2), device_of(pos - 2)
    partner = device_at(x, y, z, 1 - c)
    down, up = device_at(x, (y + 3) % NY, z, c), device_at(x, (y + 1) % NY, z, c)
    relay_to = relay_target()
    half = k_ref.shape[1] // 2
    pairs = [
        (own.at[:, pl.ds(lo, half)], prev.at[:, pl.ds(lo, half)])
        for lo in (0, half)
        for own, prev in ((k_ref, kp_ref), (v_ref, vp_ref))
    ]
    count = len(pairs)
    mid, end = pl.ds(short, rows), pl.ds(short + rows, rows)
    head, tail = pl.ds(0, short), pl.ds(rows - short, short)

    def put(n, src, dst, to):
        sends.copy(n, src, dst, to).start()

    for n, (own, prev) in enumerate(pairs):
        put(n, own, prev.at[mid], ahead)

        @pl.when(c == 0)
        def _():
            put(count + n, own, prev.at[end], partner)

        @pl.when(c == 1)
        def _():
            put(3 * count + n, own.at[tail], relay_ref.at[n], down)

        yield

    for n, (own, prev) in enumerate(pairs):

        @pl.when(c == 1)
        def _():
            sends.copy(3 * count + n, relay_ref.at[n], relay_ref.at[n], up).wait_recv()
            put(2 * count + n, relay_ref.at[n], prev.at[head], relay_to)

        yield
    for group in (range(count // 2), range(count // 2, count)):
        for n in group:
            own, prev = pairs[n]
            sends.arrived(n, prev.at[mid], behind)

            @pl.when(c == 0)
            def _():
                put(2 * count + n, prev.at[pl.ds(rows, short)], prev.at[head], partner)

            @pl.when(c == 1)
            def _():
                put(count + n, prev.at[mid], prev.at[end], partner)

            yield
        for n in group:
            own, prev = pairs[n]
            sends.arrived(count + n, prev.at[end], partner)
            sends.arrived(2 * count + n, prev.at[head], partner)
            sends.copy(n, own, prev.at[mid], ahead).wait_send()
            sends.copy(count + n, own, prev.at[end], partner).wait_send()
            sends.copy(2 * count + n, own.at[tail], prev.at[head], partner).wait_send()

            @pl.when(c == 1)
            def _():
                sends.copy(3 * count + n, own.at[tail], relay_ref.at[n], down).wait_send()

            yield


def relay_target():
    x, y, z, c = place()
    pos = lax.axis_index("outer") * 16 + lax.axis_index("inner")
    above_o, above_i = device_at(x, (y + 1) % NY, z, 1)
    to_o, to_i = device_of(above_o * 16 + above_i + 3)
    from_o, from_i = device_of(pos - 3)
    fx, fy, fz = (from_o % 2) * 2 + from_i // 8, (from_i // 2) % NY, from_o // 2
    by_o, by_i = device_at(fx, (fy + 3) % NY, fz, 1)
    return jnp.where(c == 1, to_o, by_o), jnp.where(c == 1, to_i, by_i)


def fine_kernel(
    gain_ref, x_src, q_src, k_src, v_src, w_src,
    state_ref, pooled_ref, normed_ref,
    x_ref, q_ref, k_ref, v_ref, mix_ref, edge_out, edge_in, kp_ref, vp_ref, relay_ref, w_ref,
    load_sem, local_sem, send_sem, recv_sem,
):
    rows = q_ref.shape[0]
    heads = q_ref.shape[1] // HE
    position = lax.axis_index("outer") * 16 + lax.axis_index("inner")
    greet(
        plane_neighbours()
        + [device_of(position + d) for d in (2, -2, 1, -1)]
        + [relay_target()]
    )
    sends = Sends(send_sem, recv_sem, HALO_COPIES)
    weights = plane_gather(sends, half_rows(w_src), w_ref, local_sem, W_FIRSTS)
    before_rows = halo_copies(sends, k_src, v_src, kp_ref, vp_ref, relay_ref)
    loads = [
        pltpu.make_async_copy(src, dst, load_sem.at[n])
        for n, (src, dst) in enumerate(
            ((q_src, q_ref), (k_src, k_ref), (v_src, v_ref), (x_src, x_ref))
        )
    ]
    next(weights)
    next(before_rows)
    next(before_rows)
    for load in loads:
        load.start()
    for steps in (weights, before_rows, before_rows, weights, before_rows, before_rows, weights):
        next(steps)
    for steps in (before_rows,) * 4 + (weights,) + (before_rows,) * 2:
        next(steps)
    for load in loads:
        load.wait()
    between = {0: (weights,), 1: (before_rows,), 2: (before_rows,), 3: (before_rows,) * 2, 5: (weights,)}
    t_prev = lax.broadcasted_iota(jnp.int32, (rows, WIN), 0)
    u_prev = lax.broadcasted_iota(jnp.int32, (rows, WIN), 1)
    ok_prev = (u_prev > t_prev) & (position * rows - WIN + u_prev >= 0)
    t_own = lax.broadcasted_iota(jnp.int32, (rows, rows), 0)
    u_own = lax.broadcasted_iota(jnp.int32, (rows, rows), 1)
    ok_own = u_own <= t_own
    for h in range(heads):
        cols = slice(h * HE, (h + 1) * HE)
        q = q_ref[:, cols]
        s_prev = lax.dot_general(q, kp_ref[:, cols], TRANS, preferred_element_type=F32) * SCALE
        s_own = lax.dot_general(q, k_ref[:, cols], TRANS, preferred_element_type=F32) * SCALE
        s_prev = jnp.where(ok_prev, s_prev, NEG)
        s_own = jnp.where(ok_own, s_own, NEG)
        top = jnp.maximum(
            jnp.max(s_prev, axis=-1, keepdims=True), jnp.max(s_own, axis=-1, keepdims=True)
        )
        p_prev = jnp.exp(s_prev - top)
        p_own = jnp.exp(s_own - top)
        total = jnp.sum(p_prev, axis=-1, keepdims=True) + jnp.sum(p_own, axis=-1, keepdims=True)
        mixed = jnp.dot(p_prev.astype(BF), vp_ref[:, cols], preferred_element_type=F32)
        mixed += jnp.dot(p_own.astype(BF), v_ref[:, cols], preferred_element_type=F32)
        mix_ref[:, cols] = (mixed / total).astype(BF)
        for steps in between.get(h, ()):
            next(steps)
    width = x_ref.shape[1]
    half = w_ref.shape[1]
    per = w_ref.shape[2]

    @pl.loop(0, NP // 4)
    def _(m):
        n = 2 * m
        at = pl.ds(pl.multiple_of(n * per, 2 * per), 2 * per)
        upper = jnp.concatenate([w_ref[n], w_ref[n + 1]], axis=1)
        lower = jnp.concatenate([w_ref[n + NP // 2], w_ref[n + 1 + NP // 2]], axis=1)
        prod = jnp.dot(mix_ref[:, :half], upper, preferred_element_type=F32)
        prod += jnp.dot(mix_ref[:, half:], lower, preferred_element_type=F32)
        state_ref[:, at] = (x_ref[:, at].astype(F32) + prod).astype(BF)

    edge_out[...] = state_ref[rows - POOL :, :]
    send = pltpu.make_async_remote_copy(
        src_ref=edge_out,
        dst_ref=edge_in,
        send_sem=send_sem.at[EDGE_COPY],
        recv_sem=recv_sem.at[EDGE_COPY],
        device_id=device_of(position + 1),
        device_id_type=MESH,
    )
    send.start()
    groups = state_ref[...].astype(F32).reshape(rows // POOL, POOL, width)
    first = groups[:, 0, :]
    rest = jnp.sum(groups[:, 1:, :], axis=1)
    send.wait()
    edge = jnp.sum(edge_in[...].astype(F32)[1:, :], axis=0, keepdims=True)
    edge = jnp.where(position == 0, 0.0, edge)
    before = jnp.concatenate([edge, rest[: rows // POOL - 1, :]], axis=0)
    pooled = ((before + first) / POOL).astype(BF)
    pooled_ref[...] = pooled
    wide = pooled.astype(F32)
    moment = jnp.mean(wide * wide, axis=-1, keepdims=True)
    normed_ref[...] = (wide * lax.rsqrt(moment + 1e-06) * gain_ref[...]).astype(BF)
    sends.drain()


EDGE_COPY = HALO_COPIES + plane_copies(W_FIRSTS)


def fine_stage(x, q, k, v, gain, w):
    rows, width = x.shape
    coarse = jax.ShapeDtypeStruct((rows // POOL, width), BF)
    return pl.pallas_call(
        fine_kernel,
        out_shape=[jax.ShapeDtypeStruct((rows, width), BF), coarse, coarse],
        in_specs=[vmem_spec()] + [hbm_spec()] * 5,
        out_specs=[vmem_spec()] * 3,
        scratch_shapes=[
            *[pltpu.VMEM(a.shape, BF) for a in (x, q, k, v)],
            pltpu.VMEM(q.shape, BF),
            pltpu.VMEM((POOL, width), BF),
            pltpu.VMEM((POOL, width), BF),
            pltpu.VMEM((WIN, k.shape[1]), BF),
            pltpu.VMEM((WIN, k.shape[1]), BF),
            pltpu.VMEM((HALO_PARTS, WIN - 2 * rows, k.shape[1] // 2), BF),
            pltpu.VMEM((NP, w.shape[0] // 2, w.shape[1]), BF),
            pltpu.SemaphoreType.DMA((4,)),
            pltpu.SemaphoreType.DMA,
            pltpu.SemaphoreType.DMA((EDGE_COPY + 1,)),
            pltpu.SemaphoreType.DMA((EDGE_COPY + 1,)),
        ],
        compiler_params=pltpu.CompilerParams(
            collective_id=2, has_side_effects=True, vmem_limit_bytes=32 << 20
        ),
        name="fine",
    )(gain.reshape(1, width), *[in_hbm(a) for a in (x, q, k, v, w)])


ZCHUNK = 8


def z_copies(rows):
    return (NZ - 1) * (rows // ZCHUNK)


def z_gather(sends, src_ref, dst_ref, local_sem):
    x, y, z, c = place()
    up, down = device_at(x, y, (z + 1) % NZ, c), device_at(x, y, (z + NZ - 1) % NZ, c)
    chunks = src_ref.shape[0] // ZCHUNK
    first = sends.next
    sends.next += z_copies(src_ref.shape[0])
    count_up, count_down = NZ // 2, NZ // 2 - 1
    local = pltpu.make_async_copy(src_ref, dst_ref.at[z], local_sem)
    for s in range(count_up + 1):
        for part in range(chunks):
            at = pl.ds(part * ZCHUNK, ZCHUNK)
            for sign, count, base, to, origin in (
                (-1, count_up, first, up, down),
                (1, count_down, first + count_up * chunks, down, up),
            ):
                if s > count:
                    continue
                held = (z + sign * s + NZ) % NZ
                if s > 0:
                    sends.arrived(base + (s - 1) * chunks + part, dst_ref.at[held, at], origin)
                if s < count:
                    src = src_ref.at[at] if s == 0 else dst_ref.at[held, at]
                    sends.start(base + s * chunks + part, src, dst_ref.at[held, at], to)
        if s == 0:
            local.start()
        if s == count_up:
            local.wait()
        yield


def scatter(weights, dst_ref, local_sem, send_sem, recv_sem):
    outer = lax.axis_index("outer")
    inner = lax.axis_index("inner")
    head = outer // 2
    rows = dst_ref.shape[0]
    base = (outer % 2) * (16 * rows)
    columns = [pl.ds(n * HE, HE) for n in range(len(weights))]

    def rows_of(w, to):
        return w.at[pl.ds(pl.multiple_of(base + to * rows, rows), rows)]

    def to_self(n, w):
        return pltpu.make_async_copy(rows_of(w, inner), dst_ref.at[:, columns[n]], local_sem.at[n])

    @pl.when(inner == head)
    def _():
        for n, w in enumerate(weights):
            to_self(n, w).start()
        for d in range(1, 16):
            to = (inner + d) % 16
            for n, w in enumerate(weights):
                pltpu.make_async_remote_copy(
                    src_ref=rows_of(w, to),
                    dst_ref=dst_ref.at[:, columns[n]],
                    send_sem=send_sem.at[n, d - 1],
                    recv_sem=recv_sem.at[n],
                    device_id=(outer, to),
                    device_id_type=MESH,
                ).start()

    yield

    @pl.when(inner == head)
    def _():
        for n, w in enumerate(weights):
            to_self(n, w).wait()
            for d in range(1, 16):
                piece = rows_of(w, 0)
                pltpu.make_async_copy(piece, piece, send_sem.at[n, d - 1]).wait()

    @pl.when(inner != head)
    def _():
        for n in range(len(weights)):
            piece = dst_ref.at[:, columns[n]]
            pltpu.make_async_copy(piece, piece, recv_sem.at[n]).wait()

    yield


def half_rows(w_ref):
    size = w_ref.shape[0] // 2
    copy = lax.axis_index("outer") % 2
    return w_ref.at[pl.ds(pl.multiple_of(copy * size, size), size)]


PIECE_COPIES = 32


def to_all_of_plane(sends, src, dst, local_sem):
    x, y, z, c = place()
    partner = device_at(x, y, z, 1 - c)
    mine = slot_of(x, y, c)
    first = sends.next
    sends.next += PIECE_COPIES
    offsets = [(a, b) for a in range(NX) for b in range(NY)]
    local = pltpu.make_async_copy(src, dst.at[mine], local_sem)
    local.start()
    for n, (a, b) in enumerate(offsets):
        to = device_at((x + a) % NX, (y + b) % NY, z, c) if n else partner
        sends.start(first + n, src, dst.at[mine], to)
    yield
    for n, (a, b) in enumerate(offsets):
        if n:
            px, py = (x + NX - a) % NX, (y + NY - b) % NY
            s = slot_of(px, py, c)
            sends.arrived(first + n, dst.at[s], device_at(px, py, z, c))
            sends.start(first + len(offsets) + n, dst.at[s], dst.at[s], partner)
    yield
    local.wait()
    sends.arrived(first, dst.at[slot_of(x, y, 1 - c)], partner)
    for n, (a, b) in enumerate(offsets):
        if n:
            s = slot_of((x + NX - a) % NX, (y + NY - b) % NY, 1 - c)
            sends.arrived(first + len(offsets) + n, dst.at[s], partner)
    yield


PLANE_GROUP = 4
STATS = 3


def coarse_kernel(
    normed_ref, pooled_ref, w_src, wq_ref, wk_ref, wv_ref, out_ref,
    tokens_ref, w_ref, head_ref, piece_ref, proj_ref,
    kv_ref, q_ref, top_ref, acc_ref, part_out, part_in, mix_ref, heads_ref,
    local_sem, scatter_send, scatter_recv, send_sem, recv_sem,
):
    x, y, z, c = place()
    outer = lax.axis_index("outer")
    inner = lax.axis_index("inner")
    plane = [(a, b) for a in range(NX) for b in range(NY)][1:]
    others = [device_at(x, y, (z + d) % NZ, c) for d in range(1, NZ)]
    along_x = [device_at((x + d) % NX, y, z, c) for d in range(NX)]
    along_y = [device_at(x, (y + d) % NY, z, c) for d in range(NY)]
    partner = device_at(x, y, z, 1 - c)
    greet(
        [device_at((x + a) % NX, (y + b) % NY, z, c) for a, b in plane]
        + [partner]
        + others
        + [(outer, (inner + d) % 16) for d in range(1, 16)]
    )
    base_k, base_p, base_q, base_o, base_z = 0, 4, 8, 12, 16
    sends = Sends(send_sem, recv_sem, base_z + NZ)
    along = z_gather(sends, normed_ref, tokens_ref, local_sem.at[0])
    out = plane_gather(sends, half_rows(w_src), w_ref, local_sem.at[1])
    pieces = scatter((wq_ref, wk_ref, wv_ref), piece_ref, local_sem.at[pl.ds(2, 3)], scatter_send, scatter_recv)
    head = to_all_of_plane(sends, piece_ref, head_ref, local_sem.at[5])
    order = (along, pieces, out, along, along, pieces, head, out, along, out, along, out, along, out)
    for steps in order + (along, head, along, along, head):
        next(steps)
    count = proj_ref.shape[0]
    deep = tokens_ref.shape[2]
    proj_ref[...] = jnp.dot(
        tokens_ref[...].reshape(count, deep),
        head_ref[...].reshape(deep, proj_ref.shape[1]),
        preferred_element_type=F32,
    ).astype(BF)
    own_kv = proj_ref.at[:, HE:]
    own_q = proj_ref.at[:, :HE]
    mine = y * NC + c
    for d in (2, 1, 3):
        sends.start(base_k + d, own_kv, kv_ref.at[mine], along_y[d])
        sends.start(base_q + d, own_q, q_ref.at[d], along_x[d])
    sends.start(base_p, own_kv, kv_ref.at[mine], partner)
    kv_ref[mine] = proj_ref[:, HE:]
    q_ref[0] = proj_ref[:, :HE]
    next(out)
    for d in (1, 3, 2):
        s = (y + NY - d) % NY * NC + c
        sends.arrived(base_k + d, kv_ref.at[s], along_y[NY - d])
        sends.start(base_p + d, kv_ref.at[s], kv_ref.at[s], partner)
    sends.arrived(base_p, kv_ref.at[y * NC + 1 - c], partner)
    for d in (1, 3, 2):
        sends.arrived(base_p + d, kv_ref.at[(y + NY - d) % NY * NC + 1 - c], partner)
    per = count // NZ
    step = PLANE_GROUP * per
    factor = SCALE * LOG2E
    side = NY * NC
    width = side * step
    ones = jnp.ones((width, HE), BF)
    t = lax.broadcasted_iota(jnp.int32, (step, 1), 0)
    u = lax.broadcasted_iota(jnp.int32, (1, width), 1)
    t_order = t // per * (NP * 32) + t % per
    u_order = (u % step // per * NP + u // step) * 32 + u % per
    lane = lax.broadcasted_iota(jnp.int32, (count, HE), 1)

    def attend(d):
        owner = slot_of((x + NX - d) % NX, y, c)
        allowed = u_order <= t_order + (owner - side * x) * 32
        for n in range(NZ // PLANE_GROUP):
            lo = n * step
            keys = kv_ref[:, lo : lo + step, :HE].reshape(width, HE)
            values = kv_ref[:, lo : lo + step, HE:].reshape(width, HE)
            s = lax.dot_general(
                q_ref[d, lo:, :], keys, TRANS, preferred_element_type=F32
            ) * factor
            edge = jnp.where(allowed, s[:step], NEG)
            s = jnp.concatenate([edge, s[step:]], axis=0) if lo + step < count else edge
            best = jnp.max(s, axis=-1, keepdims=True)
            wide = jnp.concatenate([values, ones], axis=1)
            if n == 0:
                top_ref[...] = best
                acc_ref[...] = jnp.dot(
                    jnp.exp2(s - best).astype(BF), wide, preferred_element_type=F32
                )
            else:
                old = top_ref[lo:, :]
                new = jnp.maximum(old, best)
                acc_ref[lo:, :] = acc_ref[lo:, :] * jnp.exp2(old - new) + jnp.dot(
                    jnp.exp2(s - new).astype(BF), wide, preferred_element_type=F32
                )
                top_ref[lo:, :] = new
        weight = top_ref[...] + jnp.log2(acc_ref[:, HE:])
        return acc_ref[:, :HE] / acc_ref[:, HE:], weight

    for d in (2, 1, 3):
        sends.arrived(base_q + d, q_ref.at[d], along_x[NX - d])
        mixed, weight = attend(d)
        high = weight.astype(BF).astype(F32)
        middle = (weight - high).astype(BF).astype(F32)
        low = weight - high - middle
        pieces = jnp.where(lane < 32, high, jnp.where(lane < 64, middle, low))
        part_out[d, :, :HE] = mixed.astype(BF)
        part_out[d, :, HE:] = pieces.astype(BF)
        sends.start(base_o + d, part_out.at[d], part_in.at[d], along_x[NX - d])
    mixed, weight = attend(0)
    parts = [(mixed, weight)]
    for d in (2, 1, 3):
        sends.arrived(base_o + d, part_in.at[d], along_x[d])
        got = part_in[d, :, HE:].astype(F32)
        weight = sum(got[:, 32 * n : 32 * n + 1] for n in range(STATS))
        parts.append((part_in[d, :, :HE].astype(F32), weight + jnp.zeros((count, HE), F32)))
    best = functools.reduce(jnp.maximum, [w for _, w in parts])
    total, mixed = 0.0, 0.0
    for m, w in parts:
        share = jnp.exp2(w - best)
        total += share
        mixed += share * m
    mix_ref[...] = (mixed / total).astype(BF).reshape(mix_ref.shape)
    for d in (8, 7, 9, 6, 10, 5, 11, 4, 12, 3, 13, 2, 14, 1, 15):
        sends.start(base_z + d, mix_ref.at[(z + d) % NZ], heads_ref.at[z], others[d - 1])
    heads_ref[z] = mix_ref[z]
    next(out)
    for d in range(1, NZ):
        origin = (z + NZ - d) % NZ
        sends.arrived(base_z + d, heads_ref.at[origin], others[NZ - d - 1])
    sends.drain()
    total = pooled_ref[...].astype(F32)
    for n in range(NZ // 2):
        two = jnp.concatenate([heads_ref[2 * n], heads_ref[2 * n + 1]], axis=1)
        rows = [w_ref[h + half] for h in (2 * n, 2 * n + 1) for half in (0, NP // 2)]
        w = jnp.concatenate(rows, axis=0)
        total += jnp.dot(two, w, preferred_element_type=F32)
    out_ref[...] = total.astype(BF)


def coarse_stage(normed, pooled, w, *head_weights):
    width = normed.shape[1]
    rows = NZ * normed.shape[0]
    count = 16 + NZ + z_copies(normed.shape[0]) + plane_copies((0, 1)) + PIECE_COPIES
    piece = (width // NP, len(head_weights) * HE)
    heads = pltpu.VMEM((NZ, rows // NZ, HE), BF)
    parts = pltpu.VMEM((NX, rows, 2 * HE), BF)
    return pl.pallas_call(
        coarse_kernel,
        out_shape=jax.ShapeDtypeStruct(pooled.shape, BF),
        in_specs=[vmem_spec(), vmem_spec()] + [hbm_spec()] * 4,
        out_specs=vmem_spec(),
        scratch_shapes=[
            pltpu.VMEM((NZ, *normed.shape), BF),
            pltpu.VMEM((NP, w.shape[0] // 2, width), BF),
            pltpu.VMEM((NP, *piece), BF),
            pltpu.VMEM(piece, BF),
            pltpu.VMEM((rows, piece[1]), BF),
            pltpu.VMEM((NY * NC, rows, 2 * HE), BF),
            pltpu.VMEM((NX, rows, HE), BF),
            pltpu.VMEM((rows, 1), F32),
            pltpu.VMEM((rows, 2 * HE), F32),
            parts,
            parts,
            heads,
            heads,
            pltpu.SemaphoreType.DMA((6,)),
            pltpu.SemaphoreType.DMA((3, 15)),
            pltpu.SemaphoreType.DMA((3,)),
            pltpu.SemaphoreType.DMA((count,)),
            pltpu.SemaphoreType.DMA((count,)),
        ],
        compiler_params=pltpu.CompilerParams(
            collective_id=4, has_side_effects=True, vmem_limit_bytes=40 << 20
        ),
        name="coarse",
    )(normed, pooled, *[in_hbm(a) for a in (w, *head_weights)])


def on_device(
    fine_input,
    fine_query,
    fine_key,
    fine_value,
    w_fine_out,
    norm_gain,
    w_query,
    w_key,
    w_value,
    w_coarse_out,
):
    rows, width = fine_input.shape
    state, pooled, normed = fine_stage(
        fine_input, fine_query, fine_key, fine_value, norm_gain, w_fine_out
    )
    coarse_out = coarse_stage(normed, pooled, w_coarse_out, w_query, w_key, w_value)
    groups = state.reshape(rows // POOL, POOL, width).astype(F32)
    lifted = groups + coarse_out.astype(F32)[:, None, :]
    return lifted.reshape(rows, width).astype(BF)


def solution(mesh):
    placed = (
        P(("outer", "inner"), None),
        P(("outer", "inner"), None),
        P(("outer", "inner"), None),
        P(("outer", "inner"), None),
        P(None, "inner"),
        P(),
        P(None, "inner"),
        P(None, "inner"),
        P(None, "inner"),
        P("inner", None),
    )
    return jax.shard_map(
        on_device,
        mesh=mesh,
        in_specs=placed,
        out_specs=P(("outer", "inner"), None),
        check_vma=False,
    )
```

```python
import functools
import math

import jax
import jax.numpy as jnp
from jax import lax
from jax.experimental import pallas as pl
from jax.experimental.pallas import tpu as pltpu
from jax.sharding import PartitionSpec as P

HE = 128
WIN = 512
POOL = 8
NEG = -1e30
LOG2E = math.log2(math.e)
SCALE = 1.0 / math.sqrt(HE)
BF = jnp.bfloat16
F32 = jnp.float32
TRANS = (((1,), (1,)), ((), ()))
MESH = pl.DeviceIdType.MESH
NX, NY, NZ, NC = 4, 4, 16, 2
NP = NX * NY * NC


def vmem_spec():
    return pl.BlockSpec(memory_space=pltpu.VMEM)


def any_spec():
    return pl.BlockSpec(memory_space=pl.ANY)


def hbm_spec():
    return pl.BlockSpec(memory_space=pltpu.HBM)


def in_hbm(a):
    return pltpu.with_memory_space_constraint(a, pltpu.HBM)


def place():
    outer = lax.axis_index("outer")
    inner = lax.axis_index("inner")
    x = (outer % 2) * 2 + inner // 8
    return x, (inner // 2) % NY, outer // 2, inner % NC


def device_at(x, y, z, c):
    return (z * 2 + x // 2, (x % 2) * 8 + y * 2 + c)


def device_of(pos):
    pos = (pos + 512) % 512
    return (pos // 16, pos % 16)


def slot_of(x, y, c):
    return x * 8 + y * 2 + c


def greet(devices):
    barrier = pltpu.get_barrier_semaphore()
    for d in devices:
        pl.semaphore_signal(barrier, inc=1, device_id=d, device_id_type=MESH)
    pl.semaphore_wait(barrier, len(devices))


def plane_neighbours():
    x, y, z, c = place()
    return [
        device_at((x + 1) % NX, y, z, c),
        device_at((x + 3) % NX, y, z, c),
        device_at(x, (y + 1) % NY, z, c),
        device_at(x, (y + 3) % NY, z, c),
        device_at(x, y, z, 1 - c),
    ]


class Sends:
    def __init__(self, send_sem, recv_sem, base=0):
        self.send_sem, self.recv_sem, self.next = send_sem, recv_sem, base
        self.started = []

    def new(self):
        self.next += 1
        return self.next - 1

    def copy(self, k, src, dst, to):
        return pltpu.make_async_remote_copy(
            src_ref=src,
            dst_ref=dst,
            send_sem=self.send_sem.at[k],
            recv_sem=self.recv_sem.at[k],
            device_id=to,
            device_id_type=MESH,
        )

    def start(self, k, src, dst, to):
        c = self.copy(k, src, dst, to)
        c.start()
        self.started.append(c)

    def arrived(self, k, dst, to):
        self.copy(k, dst, dst, to).wait_recv()

    def drain(self):
        for c in self.started:
            c.wait_send()
        self.started = []


def plane_copies(firsts):
    return 35 * len(firsts) + 1


def plane_gather(sends, src, dst, local_sem, firsts=(0, 1)):
    x, y, z, c = place()
    part = src.shape[0] // len(firsts)

    def near(axis, off):
        if axis == 0:
            return device_at((x + off) % NX, y, z, c)
        return device_at(x, (y + off) % NY, z, c)

    def at(axis, a, b):
        if axis == 0:
            return slot_of((x + a) % NX, (y + b) % NY, c)
        return slot_of((x + b) % NX, (y + a) % NY, c)

    partner = device_at(x, y, z, 1 - c)
    halves = []
    for n, first in enumerate(firsts):
        lo = n * part
        h = dict(first=first, whole=pl.ds(lo, part), k={})
        h["q0"] = pl.ds(lo, part // 2)
        h["q1"] = pl.ds(lo + part // 2, part // 2)
        for name in ("r1", "l1", "r2", "l2"):
            h["k"][name] = sends.new()
        for j in (0, -1, 1, 2):
            for name in ("r1", "l1", "r2", "l2"):
                h["k"][name, j] = sends.new()
        for j in (0, -1, 1, 2):
            for i in (0, -1, 1, 2):
                if (i, j) != (0, 0):
                    h["k"]["p", j, i] = sends.new()
        halves.append(h)
    own_pair = sends.new()
    mine = slot_of(x, y, c)
    theirs = slot_of(x, y, 1 - c)
    local = pltpu.make_async_copy(src, dst.at[mine], local_sem)

    def to_partner(h, j, i):
        s = at(h["first"], j, i)
        sends.start(h["k"]["p", j, i], dst.at[s, h["whole"]], dst.at[s, h["whole"]], partner)

    for second_axis in (False, True):
        for h in halves:
            a = 1 - h["first"] if second_axis else h["first"]
            for name, off in (("r1", 1), ("l1", -1)):
                k = h["k"][(name, 0) if second_axis else name]
                sends.start(k, src.at[h["whole"]], dst.at[mine, h["whole"]], near(a, off % 4))
    sends.start(own_pair, src, dst.at[mine], partner)
    local.start()
    yield

    def second(h, j):
        s = at(h["first"], j, 0)
        for name, off in (("r1", 1), ("l1", -1)):
            sends.start(
                h["k"][name, j],
                dst.at[s, h["whole"]],
                dst.at[s, h["whole"]],
                near(1 - h["first"], off % 4),
            )
        to_partner(h, j, 0)

    directions = (("r1", "r2", -1, "q0"), ("l1", "l2", 1, "q1"))
    for h in halves:
        a = h["first"]
        for name, fwd, off, q in directions:
            s = at(a, off, 0)
            sends.arrived(h["k"][name], dst.at[s, h["whole"]], near(a, off % 4))
            sends.start(h["k"][fwd], dst.at[s, h[q]], dst.at[s, h[q]], near(a, (-off) % 4))
    for h in halves:
        for off in (-1, 1):
            second(h, off)
    yield

    def relay(h, j):
        b = 1 - h["first"]
        for name, fwd, off, q in directions:
            s = at(h["first"], j, off)
            sends.arrived(h["k"][name, j], dst.at[s, h["whole"]], near(b, off % 4))
            sends.start(h["k"][fwd, j], dst.at[s, h[q]], dst.at[s, h[q]], near(b, (-off) % 4))
            to_partner(h, j, off)

    for h in halves:
        relay(h, 0)
    yield
    for h in halves:
        a = h["first"]
        s = at(a, 2, 0)
        sends.arrived(h["k"]["r2"], dst.at[s, h["q0"]], near(a, 3))
        sends.arrived(h["k"]["l2"], dst.at[s, h["q1"]], near(a, 1))
        second(h, 2)
    yield

    def last(h, j):
        b = 1 - h["first"]
        s = at(h["first"], j, 2)
        sends.arrived(h["k"]["r2", j], dst.at[s, h["q0"]], near(b, 3))
        sends.arrived(h["k"]["l2", j], dst.at[s, h["q1"]], near(b, 1))
        to_partner(h, j, 2)

    for j in (-1, 1):
        for h in halves:
            relay(h, j)
    for h in halves:
        last(h, 0)
    yield
    for h in halves:
        relay(h, 2)
    for j in (-1, 1):
        for h in halves:
            last(h, j)
    yield
    for h in halves:
        last(h, 2)
    local.wait()
    sends.arrived(own_pair, dst.at[theirs], partner)
    for h in halves:
        for j in (0, -1, 1, 2):
            for i in (0, -1, 1, 2):
                if (i, j) != (0, 0):
                    s = at(h["first"], j, i) + 1 - 2 * c
                    sends.arrived(h["k"]["p", j, i], dst.at[s, h["whole"]], partner)
    yield


def run_all(steps):
    for _ in steps:
        pass


HALO_PARTS = 4
HALO_COPIES = 4 * HALO_PARTS
W_FIRSTS = (1,)


def halo_copies(sends, k_ref, v_ref, kp_ref, vp_ref, relay_ref):
    x, y, z, c = place()
    pos = lax.axis_index("outer") * 16 + lax.axis_index("inner")
    rows = k_ref.shape[0]
    short = WIN - 2 * rows
    ahead, behind = device_of(pos + 2), device_of(pos - 2)
    partner = device_at(x, y, z, 1 - c)
    down, up = device_at(x, (y + 3) % NY, z, c), device_at(x, (y + 1) % NY, z, c)
    relay_to = relay_target()
    half = k_ref.shape[1] // 2
    pairs = [
        (own.at[:, pl.ds(lo, half)], prev.at[:, pl.ds(lo, half)])
        for lo in (0, half)
        for own, prev in ((k_ref, kp_ref), (v_ref, vp_ref))
    ]
    count = len(pairs)
    mid, end = pl.ds(short, rows), pl.ds(short + rows, rows)
    head, tail = pl.ds(0, short), pl.ds(rows - short, short)

    def put(n, src, dst, to):
        sends.copy(n, src, dst, to).start()

    for n, (own, prev) in enumerate(pairs):
        put(n, own, prev.at[mid], ahead)

        @pl.when(c == 0)
        def _():
            put(count + n, own, prev.at[end], partner)

        @pl.when(c == 1)
        def _():
            put(3 * count + n, own.at[tail], relay_ref.at[n], down)

        yield

    for n, (own, prev) in enumerate(pairs):

        @pl.when(c == 1)
        def _():
            sends.copy(3 * count + n, relay_ref.at[n], relay_ref.at[n], up).wait_recv()
            put(2 * count + n, relay_ref.at[n], prev.at[head], relay_to)

        yield
    for group in (range(count // 2), range(count // 2, count)):
        for n in group:
            own, prev = pairs[n]
            sends.arrived(n, prev.at[mid], behind)

            @pl.when(c == 0)
            def _():
                put(2 * count + n, prev.at[pl.ds(rows, short)], prev.at[head], partner)

            @pl.when(c == 1)
            def _():
                put(count + n, prev.at[mid], prev.at[end], partner)

            yield
        for n in group:
            own, prev = pairs[n]
            sends.arrived(count + n, prev.at[end], partner)
            sends.arrived(2 * count + n, prev.at[head], partner)
            sends.copy(n, own, prev.at[mid], ahead).wait_send()
            sends.copy(count + n, own, prev.at[end], partner).wait_send()
            sends.copy(2 * count + n, own.at[tail], prev.at[head], partner).wait_send()

            @pl.when(c == 1)
            def _():
                sends.copy(3 * count + n, own.at[tail], relay_ref.at[n], down).wait_send()

            yield


def relay_target():
    x, y, z, c = place()
    pos = lax.axis_index("outer") * 16 + lax.axis_index("inner")
    above_o, above_i = device_at(x, (y + 1) % NY, z, 1)
    to_o, to_i = device_of(above_o * 16 + above_i + 3)
    from_o, from_i = device_of(pos - 3)
    fx, fy, fz = (from_o % 2) * 2 + from_i // 8, (from_i // 2) % NY, from_o // 2
    by_o, by_i = device_at(fx, (fy + 3) % NY, fz, 1)
    return jnp.where(c == 1, to_o, by_o), jnp.where(c == 1, to_i, by_i)


def fine_part(
    sends, background,
    gain_ref, x_src, q_src, k_src, v_src, w_src,
    state_ref, pooled_ref, normed_ref,
    x_ref, q_ref, k_ref, v_ref, mix_ref, edge_out, edge_in, kp_ref, vp_ref, relay_ref, w_ref,
    load_sem, local_sem, send_sem, recv_sem,
):
    pieces, head, out = background
    rows = q_ref.shape[0]
    heads = q_ref.shape[1] // HE
    position = lax.axis_index("outer") * 16 + lax.axis_index("inner")
    weights = plane_gather(sends, half_rows(w_src), w_ref, local_sem, W_FIRSTS)
    before_rows = halo_copies(sends, k_src, v_src, kp_ref, vp_ref, relay_ref)
    loads = [
        pltpu.make_async_copy(src, dst, load_sem.at[n])
        for n, (src, dst) in enumerate(
            ((q_src, q_ref), (k_src, k_ref), (v_src, v_ref), (x_src, x_ref))
        )
    ]
    next(weights)
    next(before_rows)
    next(before_rows)
    for load in loads:
        load.start()
    for steps in (weights, before_rows, before_rows, pieces, weights, before_rows, before_rows, weights):
        next(steps)
    for steps in (before_rows,) * 4 + (weights,) + (before_rows,) * 2:
        next(steps)
    for load in loads:
        load.wait()
    between = {
        0: (weights,),
        1: (before_rows,),
        2: (before_rows,),
        3: (before_rows, before_rows, pieces, head),
        4: (out,),
        5: (weights,),
        7: (out,),
    }
    t_prev = lax.broadcasted_iota(jnp.int32, (rows, WIN), 0)
    u_prev = lax.broadcasted_iota(jnp.int32, (rows, WIN), 1)
    ok_prev = (u_prev > t_prev) & (position * rows - WIN + u_prev >= 0)
    t_own = lax.broadcasted_iota(jnp.int32, (rows, rows), 0)
    u_own = lax.broadcasted_iota(jnp.int32, (rows, rows), 1)
    ok_own = u_own <= t_own
    for h in range(heads):
        cols = slice(h * HE, (h + 1) * HE)
        q = q_ref[:, cols]
        s_prev = lax.dot_general(q, kp_ref[:, cols], TRANS, preferred_element_type=F32) * SCALE
        s_own = lax.dot_general(q, k_ref[:, cols], TRANS, preferred_element_type=F32) * SCALE
        s_prev = jnp.where(ok_prev, s_prev, NEG)
        s_own = jnp.where(ok_own, s_own, NEG)
        top = jnp.maximum(
            jnp.max(s_prev, axis=-1, keepdims=True), jnp.max(s_own, axis=-1, keepdims=True)
        )
        p_prev = jnp.exp(s_prev - top)
        p_own = jnp.exp(s_own - top)
        total = jnp.sum(p_prev, axis=-1, keepdims=True) + jnp.sum(p_own, axis=-1, keepdims=True)
        mixed = jnp.dot(p_prev.astype(BF), vp_ref[:, cols], preferred_element_type=F32)
        mixed += jnp.dot(p_own.astype(BF), v_ref[:, cols], preferred_element_type=F32)
        mix_ref[:, cols] = (mixed / total).astype(BF)
        for steps in between.get(h, ()):
            next(steps)
    width = x_ref.shape[1]
    half = w_ref.shape[1]
    per = w_ref.shape[2]

    @pl.loop(0, NP // 4)
    def _(m):
        n = 2 * m
        at = pl.ds(pl.multiple_of(n * per, 2 * per), 2 * per)
        upper = jnp.concatenate([w_ref[n], w_ref[n + 1]], axis=1)
        lower = jnp.concatenate([w_ref[n + NP // 2], w_ref[n + 1 + NP // 2]], axis=1)
        prod = jnp.dot(mix_ref[:, :half], upper, preferred_element_type=F32)
        prod += jnp.dot(mix_ref[:, half:], lower, preferred_element_type=F32)
        state_ref[:, at] = (x_ref[:, at].astype(F32) + prod).astype(BF)

    edge_out[...] = state_ref[rows - POOL :, :]
    send = pltpu.make_async_remote_copy(
        src_ref=edge_out,
        dst_ref=edge_in,
        send_sem=send_sem.at[EDGE_COPY],
        recv_sem=recv_sem.at[EDGE_COPY],
        device_id=device_of(position + 1),
        device_id_type=MESH,
    )
    send.start()
    next(head)
    next(out)
    groups = state_ref[...].astype(F32).reshape(rows // POOL, POOL, width)
    first = groups[:, 0, :]
    rest = jnp.sum(groups[:, 1:, :], axis=1)
    next(head)
    send.wait()
    edge = jnp.sum(edge_in[...].astype(F32)[1:, :], axis=0, keepdims=True)
    edge = jnp.where(position == 0, 0.0, edge)
    before = jnp.concatenate([edge, rest[: rows // POOL - 1, :]], axis=0)
    pooled = ((before + first) / POOL).astype(BF)
    pooled_ref[...] = pooled
    wide = pooled.astype(F32)
    moment = jnp.mean(wide * wide, axis=-1, keepdims=True)
    normed_ref[...] = (wide * lax.rsqrt(moment + 1e-06) * gain_ref[...]).astype(BF)


EDGE_COPY = HALO_COPIES
EXCHANGE_COPY = EDGE_COPY + 1
FIXED_COPIES = EXCHANGE_COPY + 32


ZCHUNK = 8


def z_copies(rows):
    return (NZ - 1) * (rows // ZCHUNK)


def z_gather(sends, src_ref, dst_ref, local_sem):
    x, y, z, c = place()
    up, down = device_at(x, y, (z + 1) % NZ, c), device_at(x, y, (z + NZ - 1) % NZ, c)
    chunks = src_ref.shape[0] // ZCHUNK
    first = sends.next
    sends.next += z_copies(src_ref.shape[0])
    count_up, count_down = NZ // 2, NZ // 2 - 1
    local = pltpu.make_async_copy(src_ref, dst_ref.at[z], local_sem)
    for s in range(count_up + 1):
        for part in range(chunks):
            at = pl.ds(part * ZCHUNK, ZCHUNK)
            for sign, count, base, to, origin in (
                (-1, count_up, first, up, down),
                (1, count_down, first + count_up * chunks, down, up),
            ):
                if s > count:
                    continue
                held = (z + sign * s + NZ) % NZ
                if s > 0:
                    sends.arrived(base + (s - 1) * chunks + part, dst_ref.at[held, at], origin)
                if s < count:
                    src = src_ref.at[at] if s == 0 else dst_ref.at[held, at]
                    sends.start(base + s * chunks + part, src, dst_ref.at[held, at], to)
        if s == 0:
            local.start()
        if s == count_up:
            local.wait()
        yield


def scatter(weights, dst_ref, local_sem, send_sem, recv_sem):
    outer = lax.axis_index("outer")
    inner = lax.axis_index("inner")
    head = outer // 2
    rows = dst_ref.shape[0]
    base = (outer % 2) * (16 * rows)
    columns = [pl.ds(n * HE, HE) for n in range(len(weights))]

    def rows_of(w, to):
        return w.at[pl.ds(pl.multiple_of(base + to * rows, rows), rows)]

    def to_self(n, w):
        return pltpu.make_async_copy(rows_of(w, inner), dst_ref.at[:, columns[n]], local_sem.at[n])

    @pl.when(inner == head)
    def _():
        for n, w in enumerate(weights):
            to_self(n, w).start()
        for d in range(1, 16):
            to = (inner + d) % 16
            for n, w in enumerate(weights):
                pltpu.make_async_remote_copy(
                    src_ref=rows_of(w, to),
                    dst_ref=dst_ref.at[:, columns[n]],
                    send_sem=send_sem.at[n, d - 1],
                    recv_sem=recv_sem.at[n],
                    device_id=(outer, to),
                    device_id_type=MESH,
                ).start()

    yield

    @pl.when(inner == head)
    def _():
        for n, w in enumerate(weights):
            to_self(n, w).wait()
            for d in range(1, 16):
                piece = rows_of(w, 0)
                pltpu.make_async_copy(piece, piece, send_sem.at[n, d - 1]).wait()

    @pl.when(inner != head)
    def _():
        for n in range(len(weights)):
            piece = dst_ref.at[:, columns[n]]
            pltpu.make_async_copy(piece, piece, recv_sem.at[n]).wait()

    yield


def half_rows(w_ref):
    size = w_ref.shape[0] // 2
    copy = lax.axis_index("outer") % 2
    return w_ref.at[pl.ds(pl.multiple_of(copy * size, size), size)]


PIECE_COPIES = 32


def to_all_of_plane(sends, src, dst, local_sem):
    x, y, z, c = place()
    partner = device_at(x, y, z, 1 - c)
    mine = slot_of(x, y, c)
    first = sends.next
    sends.next += PIECE_COPIES
    offsets = [(a, b) for a in range(NX) for b in range(NY)]
    local = pltpu.make_async_copy(src, dst.at[mine], local_sem)
    local.start()
    for n, (a, b) in enumerate(offsets):
        to = device_at((x + a) % NX, (y + b) % NY, z, c) if n else partner
        sends.start(first + n, src, dst.at[mine], to)
    yield
    for n, (a, b) in enumerate(offsets):
        if n:
            px, py = (x + NX - a) % NX, (y + NY - b) % NY
            s = slot_of(px, py, c)
            sends.arrived(first + n, dst.at[s], device_at(px, py, z, c))
            sends.start(first + len(offsets) + n, dst.at[s], dst.at[s], partner)
    yield
    local.wait()
    sends.arrived(first, dst.at[slot_of(x, y, 1 - c)], partner)
    for n, (a, b) in enumerate(offsets):
        if n:
            s = slot_of((x + NX - a) % NX, (y + NY - b) % NY, 1 - c)
            sends.arrived(first + len(offsets) + n, dst.at[s], partner)
    yield


PLANE_GROUP = 4
STATS = 3


def coarse_part(
    sends, out,
    normed_ref, pooled_ref, out_ref,
    tokens_ref, w_ref, head_ref, proj_ref,
    kv_ref, q_ref, top_ref, acc_ref, part_out, part_in, mix_ref, heads_ref, local_sem,
):
    x, y, z, c = place()
    others = [device_at(x, y, (z + d) % NZ, c) for d in range(1, NZ)]
    along_x = [device_at((x + d) % NX, y, z, c) for d in range(NX)]
    along_y = [device_at(x, (y + d) % NY, z, c) for d in range(NY)]
    partner = device_at(x, y, z, 1 - c)
    base_k, base_p, base_q, base_o, base_z = (EXCHANGE_COPY + n for n in (0, 4, 8, 12, 16))
    along = z_gather(sends, normed_ref, tokens_ref, local_sem)
    for steps in (along,) * 3 + (out, along, along, out, along, along, along, along):
        next(steps)
    count = proj_ref.shape[0]
    deep = tokens_ref.shape[2]
    proj_ref[...] = jnp.dot(
        tokens_ref[...].reshape(count, deep),
        head_ref[...].reshape(deep, proj_ref.shape[1]),
        preferred_element_type=F32,
    ).astype(BF)
    own_kv = proj_ref.at[:, HE:]
    own_q = proj_ref.at[:, :HE]
    mine = y * NC + c
    for d in (2, 1, 3):
        sends.start(base_k + d, own_kv, kv_ref.at[mine], along_y[d])
        sends.start(base_q + d, own_q, q_ref.at[d], along_x[d])
    sends.start(base_p, own_kv, kv_ref.at[mine], partner)
    kv_ref[mine] = proj_ref[:, HE:]
    q_ref[0] = proj_ref[:, :HE]
    next(out)
    for d in (1, 3, 2):
        s = (y + NY - d) % NY * NC + c
        sends.arrived(base_k + d, kv_ref.at[s], along_y[NY - d])
        sends.start(base_p + d, kv_ref.at[s], kv_ref.at[s], partner)
    sends.arrived(base_p, kv_ref.at[y * NC + 1 - c], partner)
    for d in (1, 3, 2):
        sends.arrived(base_p + d, kv_ref.at[(y + NY - d) % NY * NC + 1 - c], partner)
    per = count // NZ
    step = PLANE_GROUP * per
    factor = SCALE * LOG2E
    side = NY * NC
    width = side * step
    ones = jnp.ones((width, HE), BF)
    t = lax.broadcasted_iota(jnp.int32, (step, 1), 0)
    u = lax.broadcasted_iota(jnp.int32, (1, width), 1)
    t_order = t // per * (NP * 32) + t % per
    u_order = (u % step // per * NP + u // step) * 32 + u % per
    lane = lax.broadcasted_iota(jnp.int32, (count, HE), 1)

    def attend(d):
        owner = slot_of((x + NX - d) % NX, y, c)
        allowed = u_order <= t_order + (owner - side * x) * 32
        for n in range(NZ // PLANE_GROUP):
            lo = n * step
            keys = kv_ref[:, lo : lo + step, :HE].reshape(width, HE)
            values = kv_ref[:, lo : lo + step, HE:].reshape(width, HE)
            s = lax.dot_general(
                q_ref[d, lo:, :], keys, TRANS, preferred_element_type=F32
            ) * factor
            edge = jnp.where(allowed, s[:step], NEG)
            s = jnp.concatenate([edge, s[step:]], axis=0) if lo + step < count else edge
            best = jnp.max(s, axis=-1, keepdims=True)
            wide = jnp.concatenate([values, ones], axis=1)
            if n == 0:
                top_ref[...] = best
                acc_ref[...] = jnp.dot(
                    jnp.exp2(s - best).astype(BF), wide, preferred_element_type=F32
                )
            else:
                old = top_ref[lo:, :]
                new = jnp.maximum(old, best)
                acc_ref[lo:, :] = acc_ref[lo:, :] * jnp.exp2(old - new) + jnp.dot(
                    jnp.exp2(s - new).astype(BF), wide, preferred_element_type=F32
                )
                top_ref[lo:, :] = new
        weight = top_ref[...] + jnp.log2(acc_ref[:, HE:])
        return acc_ref[:, :HE] / acc_ref[:, HE:], weight

    for d in (2, 1, 3):
        sends.arrived(base_q + d, q_ref.at[d], along_x[NX - d])
        mixed, weight = attend(d)
        high = weight.astype(BF).astype(F32)
        middle = (weight - high).astype(BF).astype(F32)
        low = weight - high - middle
        pieces = jnp.where(lane < 32, high, jnp.where(lane < 64, middle, low))
        part_out[d, :, :HE] = mixed.astype(BF)
        part_out[d, :, HE:] = pieces.astype(BF)
        sends.start(base_o + d, part_out.at[d], part_in.at[d], along_x[NX - d])
    mixed, weight = attend(0)
    parts = [(mixed, weight)]
    for d in (2, 1, 3):
        sends.arrived(base_o + d, part_in.at[d], along_x[d])
        got = part_in[d, :, HE:].astype(F32)
        weight = sum(got[:, 32 * n : 32 * n + 1] for n in range(STATS))
        parts.append((part_in[d, :, :HE].astype(F32), weight + jnp.zeros((count, HE), F32)))
    best = functools.reduce(jnp.maximum, [w for _, w in parts])
    total, mixed = 0.0, 0.0
    for m, w in parts:
        share = jnp.exp2(w - best)
        total += share
        mixed += share * m
    mix_ref[...] = (mixed / total).astype(BF).reshape(mix_ref.shape)
    for d in (8, 7, 9, 6, 10, 5, 11, 4, 12, 3, 13, 2, 14, 1, 15):
        sends.start(base_z + d, mix_ref.at[(z + d) % NZ], heads_ref.at[z], others[d - 1])
    heads_ref[z] = mix_ref[z]
    next(out)
    for d in range(1, NZ):
        origin = (z + NZ - d) % NZ
        sends.arrived(base_z + d, heads_ref.at[origin], others[NZ - d - 1])
    sends.drain()
    total = pooled_ref[...].astype(F32)
    for n in range(NZ // 2):
        two = jnp.concatenate([heads_ref[2 * n], heads_ref[2 * n + 1]], axis=1)
        rows = [w_ref[h + half] for h in (2 * n, 2 * n + 1) for half in (0, NP // 2)]
        w = jnp.concatenate(rows, axis=0)
        total += jnp.dot(two, w, preferred_element_type=F32)
    out_ref[...] = total.astype(BF)


def layer_kernel(
    gain_ref, x_src, q_src, k_src, v_src, w_fine, w_out, wq_ref, wk_ref, wv_ref,
    state_ref, out_ref,
    x_ref, q_ref, k_ref, v_ref, fine_mix, edge_out, edge_in, kp_ref, vp_ref, relay_ref, w_fine_all,
    pooled_ref, normed_ref, tokens_ref, w_out_all, head_ref, piece_ref, proj_ref,
    kv_ref, cq_ref, top_ref, acc_ref, part_out, part_in, mix_ref, heads_ref,
    load_sem, local_sem, scatter_send, scatter_recv, send_sem, recv_sem,
):
    x, y, z, c = place()
    outer = lax.axis_index("outer")
    inner = lax.axis_index("inner")
    position = outer * 16 + inner
    plane = [(a, b) for a in range(NX) for b in range(NY)][1:]
    greet(
        [device_at((x + a) % NX, (y + b) % NY, z, c) for a, b in plane]
        + [device_at(x, y, z, 1 - c)]
        + [device_at(x, y, (z + d) % NZ, c) for d in range(1, NZ)]
        + [(outer, (inner + d) % 16) for d in range(1, 16)]
        + [device_of(position + d) for d in (2, -2, 1, -1)]
        + [relay_target()]
    )
    sends = Sends(send_sem, recv_sem, FIXED_COPIES)
    pieces = scatter((wq_ref, wk_ref, wv_ref), piece_ref, local_sem.at[pl.ds(2, 3)], scatter_send, scatter_recv)
    head = to_all_of_plane(sends, piece_ref, head_ref, local_sem.at[5])
    out = plane_gather(sends, half_rows(w_out), w_out_all, local_sem.at[1])
    fine_part(
        sends, (pieces, head, out),
        gain_ref, x_src, q_src, k_src, v_src, w_fine,
        state_ref, pooled_ref, normed_ref,
        x_ref, q_ref, k_ref, v_ref, fine_mix, edge_out, edge_in, kp_ref, vp_ref, relay_ref, w_fine_all,
        load_sem, local_sem.at[6], send_sem, recv_sem,
    )
    coarse_part(
        sends, out,
        normed_ref, pooled_ref, out_ref,
        tokens_ref, w_out_all, head_ref, proj_ref,
        kv_ref, cq_ref, top_ref, acc_ref, part_out, part_in, mix_ref, heads_ref, local_sem.at[0],
    )


def layer_stage(x, q, k, v, gain, w_fine, w_out, *head_weights):
    rows, width = x.shape
    per = rows // POOL
    tokens = NZ * per
    block = (per, width)
    piece = (width // NP, len(head_weights) * HE)
    heads = pltpu.VMEM((NZ, per, HE), BF)
    parts = pltpu.VMEM((NX, tokens, 2 * HE), BF)
    edge = pltpu.VMEM((POOL, width), BF)
    before = pltpu.VMEM((WIN, k.shape[1]), BF)
    count = FIXED_COPIES + plane_copies(W_FIRSTS) + plane_copies((0, 1)) + PIECE_COPIES + z_copies(per)
    return pl.pallas_call(
        layer_kernel,
        out_shape=[jax.ShapeDtypeStruct((rows, width), BF), jax.ShapeDtypeStruct(block, BF)],
        in_specs=[vmem_spec()] + [hbm_spec()] * 9,
        out_specs=[vmem_spec()] * 2,
        scratch_shapes=[
            *[pltpu.VMEM(a.shape, BF) for a in (x, q, k, v)],
            pltpu.VMEM(q.shape, BF),
            edge,
            edge,
            before,
            before,
            pltpu.VMEM((HALO_PARTS, WIN - 2 * rows, k.shape[1] // 2), BF),
            pltpu.VMEM((NP, w_fine.shape[0] // 2, w_fine.shape[1]), BF),
            pltpu.VMEM(block, BF),
            pltpu.VMEM(block, BF),
            pltpu.VMEM((NZ, *block), BF),
            pltpu.VMEM((NP, w_out.shape[0] // 2, width), BF),
            pltpu.VMEM((NP, *piece), BF),
            pltpu.VMEM(piece, BF),
            pltpu.VMEM((tokens, piece[1]), BF),
            pltpu.VMEM((NY * NC, tokens, 2 * HE), BF),
            pltpu.VMEM((NX, tokens, HE), BF),
            pltpu.VMEM((tokens, 1), F32),
            pltpu.VMEM((tokens, 2 * HE), F32),
            parts,
            parts,
            heads,
            heads,
            pltpu.SemaphoreType.DMA((4,)),
            pltpu.SemaphoreType.DMA((7,)),
            pltpu.SemaphoreType.DMA((3, 15)),
            pltpu.SemaphoreType.DMA((3,)),
            pltpu.SemaphoreType.DMA((count,)),
            pltpu.SemaphoreType.DMA((count,)),
        ],
        compiler_params=pltpu.CompilerParams(
            collective_id=4, has_side_effects=True, vmem_limit_bytes=52 << 20
        ),
        name="layer",
    )(gain.reshape(1, width), *[in_hbm(a) for a in (x, q, k, v, w_fine, w_out, *head_weights)])


def on_device(
    fine_input,
    fine_query,
    fine_key,
    fine_value,
    w_fine_out,
    norm_gain,
    w_query,
    w_key,
    w_value,
    w_coarse_out,
):
    rows, width = fine_input.shape
    state, coarse_out = layer_stage(
        fine_input, fine_query, fine_key, fine_value, norm_gain,
        w_fine_out, w_coarse_out, w_query, w_key, w_value,
    )
    groups = state.reshape(rows // POOL, POOL, width).astype(F32)
    lifted = groups + coarse_out.astype(F32)[:, None, :]
    return lifted.reshape(rows, width).astype(BF)


def solution(mesh):
    placed = (
        P(("outer", "inner"), None),
        P(("outer", "inner"), None),
        P(("outer", "inner"), None),
        P(("outer", "inner"), None),
        P(None, "inner"),
        P(),
        P(None, "inner"),
        P(None, "inner"),
        P(None, "inner"),
        P("inner", None),
    )
    return jax.shard_map(
        on_device,
        mesh=mesh,
        in_specs=placed,
        out_specs=P(("outer", "inner"), None),
        check_vma=False,
    )
```

```python
import functools
import math

import jax
import jax.numpy as jnp
from jax import lax
from jax.experimental import pallas as pl
from jax.experimental.pallas import tpu as pltpu
from jax.sharding import PartitionSpec as P

HE = 128
WIN = 512
POOL = 8
NEG = -1e30
LOG2E = math.log2(math.e)
SCALE = 1.0 / math.sqrt(HE)
BF = jnp.bfloat16
F32 = jnp.float32
TRANS = (((1,), (1,)), ((), ()))
MESH = pl.DeviceIdType.MESH
NX, NY, NZ, NC = 4, 4, 16, 2
NP = NX * NY * NC


def vmem_spec():
    return pl.BlockSpec(memory_space=pltpu.VMEM)


def any_spec():
    return pl.BlockSpec(memory_space=pl.ANY)


def hbm_spec():
    return pl.BlockSpec(memory_space=pltpu.HBM)


def in_hbm(a):
    return pltpu.with_memory_space_constraint(a, pltpu.HBM)


def place():
    outer = lax.axis_index("outer")
    inner = lax.axis_index("inner")
    x = (outer % 2) * 2 + inner // 8
    return x, (inner // 2) % NY, outer // 2, inner % NC


def device_at(x, y, z, c):
    return (z * 2 + x // 2, (x % 2) * 8 + y * 2 + c)


def device_of(pos):
    pos = (pos + 512) % 512
    return (pos // 16, pos % 16)


def slot_of(x, y, c):
    return x * 8 + y * 2 + c


def greet(devices):
    barrier = pltpu.get_barrier_semaphore()
    for d in devices:
        pl.semaphore_signal(barrier, inc=1, device_id=d, device_id_type=MESH)
    pl.semaphore_wait(barrier, len(devices))


def plane_neighbours():
    x, y, z, c = place()
    return [
        device_at((x + 1) % NX, y, z, c),
        device_at((x + 3) % NX, y, z, c),
        device_at(x, (y + 1) % NY, z, c),
        device_at(x, (y + 3) % NY, z, c),
        device_at(x, y, z, 1 - c),
    ]


class Sends:
    def __init__(self, send_sem, recv_sem, base=0):
        self.send_sem, self.recv_sem, self.next = send_sem, recv_sem, base
        self.started = []

    def new(self):
        self.next += 1
        return self.next - 1

    def copy(self, k, src, dst, to):
        return pltpu.make_async_remote_copy(
            src_ref=src,
            dst_ref=dst,
            send_sem=self.send_sem.at[k],
            recv_sem=self.recv_sem.at[k],
            device_id=to,
            device_id_type=MESH,
        )

    def start(self, k, src, dst, to):
        c = self.copy(k, src, dst, to)
        c.start()
        self.started.append(c)

    def arrived(self, k, dst, to):
        self.copy(k, dst, dst, to).wait_recv()

    def drain(self):
        for c in self.started:
            c.wait_send()
        self.started = []


def plane_copies(firsts):
    return 35 * len(firsts) + 1


def plane_gather(sends, src, dst, local_sem, firsts=(0, 1)):
    x, y, z, c = place()
    part = src.shape[0] // len(firsts)

    def near(axis, off):
        if axis == 0:
            return device_at((x + off) % NX, y, z, c)
        return device_at(x, (y + off) % NY, z, c)

    def at(axis, a, b):
        if axis == 0:
            return slot_of((x + a) % NX, (y + b) % NY, c)
        return slot_of((x + b) % NX, (y + a) % NY, c)

    partner = device_at(x, y, z, 1 - c)
    halves = []
    for n, first in enumerate(firsts):
        lo = n * part
        h = dict(first=first, whole=pl.ds(lo, part), k={})
        h["q0"] = pl.ds(lo, part // 2)
        h["q1"] = pl.ds(lo + part // 2, part // 2)
        for name in ("r1", "l1", "r2", "l2"):
            h["k"][name] = sends.new()
        for j in (0, -1, 1, 2):
            for name in ("r1", "l1", "r2", "l2"):
                h["k"][name, j] = sends.new()
        for j in (0, -1, 1, 2):
            for i in (0, -1, 1, 2):
                if (i, j) != (0, 0):
                    h["k"]["p", j, i] = sends.new()
        halves.append(h)
    own_pair = sends.new()
    mine = slot_of(x, y, c)
    theirs = slot_of(x, y, 1 - c)
    local = pltpu.make_async_copy(src, dst.at[mine], local_sem)

    def to_partner(h, j, i):
        s = at(h["first"], j, i)
        sends.start(h["k"]["p", j, i], dst.at[s, h["whole"]], dst.at[s, h["whole"]], partner)

    for second_axis in (False, True):
        for h in halves:
            a = 1 - h["first"] if second_axis else h["first"]
            for name, off in (("r1", 1), ("l1", -1)):
                k = h["k"][(name, 0) if second_axis else name]
                sends.start(k, src.at[h["whole"]], dst.at[mine, h["whole"]], near(a, off % 4))
    sends.start(own_pair, src, dst.at[mine], partner)
    local.start()
    yield

    def second(h, j):
        s = at(h["first"], j, 0)
        for name, off in (("r1", 1), ("l1", -1)):
            sends.start(
                h["k"][name, j],
                dst.at[s, h["whole"]],
                dst.at[s, h["whole"]],
                near(1 - h["first"], off % 4),
            )
        to_partner(h, j, 0)

    directions = (("r1", "r2", -1, "q0"), ("l1", "l2", 1, "q1"))
    for h in halves:
        a = h["first"]
        for name, fwd, off, q in directions:
            s = at(a, off, 0)
            sends.arrived(h["k"][name], dst.at[s, h["whole"]], near(a, off % 4))
            sends.start(h["k"][fwd], dst.at[s, h[q]], dst.at[s, h[q]], near(a, (-off) % 4))
    for h in halves:
        for off in (-1, 1):
            second(h, off)
    yield

    def relay(h, j):
        b = 1 - h["first"]
        for name, fwd, off, q in directions:
            s = at(h["first"], j, off)
            sends.arrived(h["k"][name, j], dst.at[s, h["whole"]], near(b, off % 4))
            sends.start(h["k"][fwd, j], dst.at[s, h[q]], dst.at[s, h[q]], near(b, (-off) % 4))
            to_partner(h, j, off)

    for h in halves:
        relay(h, 0)
    yield
    for h in halves:
        a = h["first"]
        s = at(a, 2, 0)
        sends.arrived(h["k"]["r2"], dst.at[s, h["q0"]], near(a, 3))
        sends.arrived(h["k"]["l2"], dst.at[s, h["q1"]], near(a, 1))
        second(h, 2)
    yield

    def last(h, j):
        b = 1 - h["first"]
        s = at(h["first"], j, 2)
        sends.arrived(h["k"]["r2", j], dst.at[s, h["q0"]], near(b, 3))
        sends.arrived(h["k"]["l2", j], dst.at[s, h["q1"]], near(b, 1))
        to_partner(h, j, 2)

    for j in (-1, 1):
        for h in halves:
            relay(h, j)
    for h in halves:
        last(h, 0)
    yield
    for h in halves:
        relay(h, 2)
    for j in (-1, 1):
        for h in halves:
            last(h, j)
    yield
    for h in halves:
        last(h, 2)
    local.wait()
    sends.arrived(own_pair, dst.at[theirs], partner)
    for h in halves:
        for j in (0, -1, 1, 2):
            for i in (0, -1, 1, 2):
                if (i, j) != (0, 0):
                    s = at(h["first"], j, i) + 1 - 2 * c
                    sends.arrived(h["k"]["p", j, i], dst.at[s, h["whole"]], partner)
    yield


def run_all(steps):
    for _ in steps:
        pass


HALO_PARTS = 4
HALO_COPIES = 4 * HALO_PARTS
W_FIRSTS = (1,)


def halo_copies(sends, k_ref, v_ref, kp_ref, vp_ref, relay_ref):
    x, y, z, c = place()
    pos = lax.axis_index("outer") * 16 + lax.axis_index("inner")
    rows = k_ref.shape[0]
    short = WIN - 2 * rows
    ahead, behind = device_of(pos + 2), device_of(pos - 2)
    partner = device_at(x, y, z, 1 - c)
    down, up = device_at(x, (y + 3) % NY, z, c), device_at(x, (y + 1) % NY, z, c)
    relay_to = relay_target()
    half = k_ref.shape[1] // 2
    pairs = [
        (own.at[:, pl.ds(lo, half)], prev.at[:, pl.ds(lo, half)])
        for lo in (0, half)
        for own, prev in ((k_ref, kp_ref), (v_ref, vp_ref))
    ]
    count = len(pairs)
    mid, end = pl.ds(short, rows), pl.ds(short + rows, rows)
    head, tail = pl.ds(0, short), pl.ds(rows - short, short)

    def put(n, src, dst, to):
        sends.copy(n, src, dst, to).start()

    for n, (own, prev) in enumerate(pairs):
        put(n, own, prev.at[mid], ahead)

        @pl.when(c == 0)
        def _():
            put(count + n, own, prev.at[end], partner)

        @pl.when(c == 1)
        def _():
            put(3 * count + n, own.at[tail], relay_ref.at[n], down)

        yield

    for n, (own, prev) in enumerate(pairs):

        @pl.when(c == 1)
        def _():
            sends.copy(3 * count + n, relay_ref.at[n], relay_ref.at[n], up).wait_recv()
            put(2 * count + n, relay_ref.at[n], prev.at[head], relay_to)

        yield
    for group in (range(count // 2), range(count // 2, count)):
        for n in group:
            own, prev = pairs[n]
            sends.arrived(n, prev.at[mid], behind)

            @pl.when(c == 0)
            def _():
                put(2 * count + n, prev.at[pl.ds(rows, short)], prev.at[head], partner)

            @pl.when(c == 1)
            def _():
                put(count + n, prev.at[mid], prev.at[end], partner)

            yield
        for n in group:
            own, prev = pairs[n]
            sends.arrived(count + n, prev.at[end], partner)
            sends.arrived(2 * count + n, prev.at[head], partner)
            sends.copy(n, own, prev.at[mid], ahead).wait_send()
            sends.copy(count + n, own, prev.at[end], partner).wait_send()
            sends.copy(2 * count + n, own.at[tail], prev.at[head], partner).wait_send()

            @pl.when(c == 1)
            def _():
                sends.copy(3 * count + n, own.at[tail], relay_ref.at[n], down).wait_send()

            yield


def relay_target():
    x, y, z, c = place()
    pos = lax.axis_index("outer") * 16 + lax.axis_index("inner")
    above_o, above_i = device_at(x, (y + 1) % NY, z, 1)
    to_o, to_i = device_of(above_o * 16 + above_i + 3)
    from_o, from_i = device_of(pos - 3)
    fx, fy, fz = (from_o % 2) * 2 + from_i // 8, (from_i // 2) % NY, from_o // 2
    by_o, by_i = device_at(fx, (fy + 3) % NY, fz, 1)
    return jnp.where(c == 1, to_o, by_o), jnp.where(c == 1, to_i, by_i)


def fine_kernel(
    gain_ref, x_src, q_src, k_src, v_src, w_src,
    state_ref, pooled_ref, normed_ref,
    x_ref, q_ref, k_ref, v_ref, mix_ref, edge_out, edge_in, kp_ref, vp_ref, relay_ref, w_ref,
    load_sem, local_sem, send_sem, recv_sem,
):
    rows = q_ref.shape[0]
    heads = q_ref.shape[1] // HE
    position = lax.axis_index("outer") * 16 + lax.axis_index("inner")
    greet(
        plane_neighbours()
        + [device_of(position + d) for d in (2, -2, 1, -1)]
        + [relay_target()]
    )
    sends = Sends(send_sem, recv_sem, HALO_COPIES)
    weights = plane_gather(sends, half_rows(w_src), w_ref, local_sem, W_FIRSTS)
    before_rows = halo_copies(sends, k_src, v_src, kp_ref, vp_ref, relay_ref)
    loads = [
        pltpu.make_async_copy(src, dst, load_sem.at[n])
        for n, (src, dst) in enumerate(
            ((q_src, q_ref), (k_src, k_ref), (v_src, v_ref), (x_src, x_ref))
        )
    ]
    next(weights)
    next(before_rows)
    next(before_rows)
    for load in loads:
        load.start()
    for steps in (weights, before_rows, before_rows, weights, before_rows, before_rows, weights):
        next(steps)
    for steps in (before_rows,) * 4 + (weights,) + (before_rows,) * 2:
        next(steps)
    for load in loads:
        load.wait()
    between = {0: (weights,), 1: (before_rows,), 2: (before_rows,), 3: (before_rows,) * 2, 5: (weights,)}
    near = WIN // 2
    t_far = lax.broadcasted_iota(jnp.int32, (rows, near), 0)
    u_far = lax.broadcasted_iota(jnp.int32, (rows, near), 1)
    first_row = WIN - position * rows
    ok_far = (u_far > t_far) & (u_far >= first_row)
    ok_near = lax.broadcasted_iota(jnp.int32, (1, near), 1) + near >= first_row
    t_own = lax.broadcasted_iota(jnp.int32, (rows, rows), 0)
    u_own = lax.broadcasted_iota(jnp.int32, (rows, rows), 1)
    ok_own = u_own <= t_own
    factor = SCALE * LOG2E
    for h in range(heads):
        cols = slice(h * HE, (h + 1) * HE)
        q = q_ref[:, cols]
        blocks = (
            (kp_ref[:near, cols], vp_ref[:near, cols], ok_far),
            (kp_ref[near:, cols], vp_ref[near:, cols], ok_near),
            (k_ref[:, cols], v_ref[:, cols], ok_own),
        )
        scores = [
            jnp.where(
                ok, lax.dot_general(q, keys, TRANS, preferred_element_type=F32) * factor, NEG
            )
            for keys, _, ok in blocks
        ]
        top = functools.reduce(
            jnp.maximum, [jnp.max(s, axis=-1, keepdims=True) for s in scores]
        )
        mixed = 0.0
        for s, (_, values, _) in zip(scores, blocks):
            wide = jnp.concatenate([values, jnp.ones((values.shape[0], HE), BF)], axis=1)
            mixed += jnp.dot(jnp.exp2(s - top).astype(BF), wide, preferred_element_type=F32)
        mix_ref[:, cols] = (mixed[:, :HE] / mixed[:, HE:]).astype(BF)
        for steps in between.get(h, ()):
            next(steps)
    width = x_ref.shape[1]
    half = w_ref.shape[1]
    per = w_ref.shape[2]

    @pl.loop(0, NP // 4)
    def _(m):
        n = 2 * m
        at = pl.ds(pl.multiple_of(n * per, 2 * per), 2 * per)
        upper = jnp.concatenate([w_ref[n], w_ref[n + 1]], axis=1)
        lower = jnp.concatenate([w_ref[n + NP // 2], w_ref[n + 1 + NP // 2]], axis=1)
        prod = jnp.dot(mix_ref[:, :half], upper, preferred_element_type=F32)
        prod += jnp.dot(mix_ref[:, half:], lower, preferred_element_type=F32)
        state_ref[:, at] = (x_ref[:, at].astype(F32) + prod).astype(BF)

    edge_out[...] = state_ref[rows - POOL :, :]
    send = pltpu.make_async_remote_copy(
        src_ref=edge_out,
        dst_ref=edge_in,
        send_sem=send_sem.at[EDGE_COPY],
        recv_sem=recv_sem.at[EDGE_COPY],
        device_id=device_of(position + 1),
        device_id_type=MESH,
    )
    send.start()
    groups = state_ref[...].astype(F32).reshape(rows // POOL, POOL, width)
    first = groups[:, 0, :]
    rest = jnp.sum(groups[:, 1:, :], axis=1)
    send.wait()
    edge = jnp.sum(edge_in[...].astype(F32)[1:, :], axis=0, keepdims=True)
    edge = jnp.where(position == 0, 0.0, edge)
    before = jnp.concatenate([edge, rest[: rows // POOL - 1, :]], axis=0)
    pooled = ((before + first) / POOL).astype(BF)
    pooled_ref[...] = pooled
    wide = pooled.astype(F32)
    moment = jnp.mean(wide * wide, axis=-1, keepdims=True)
    normed_ref[...] = (wide * lax.rsqrt(moment + 1e-06) * gain_ref[...]).astype(BF)
    sends.drain()


EDGE_COPY = HALO_COPIES + plane_copies(W_FIRSTS)


def fine_stage(x, q, k, v, gain, w):
    rows, width = x.shape
    coarse = jax.ShapeDtypeStruct((rows // POOL, width), BF)
    return pl.pallas_call(
        fine_kernel,
        out_shape=[jax.ShapeDtypeStruct((rows, width), BF), coarse, coarse],
        in_specs=[vmem_spec()] + [hbm_spec()] * 5,
        out_specs=[vmem_spec()] * 3,
        scratch_shapes=[
            *[pltpu.VMEM(a.shape, BF) for a in (x, q, k, v)],
            pltpu.VMEM(q.shape, BF),
            pltpu.VMEM((POOL, width), BF),
            pltpu.VMEM((POOL, width), BF),
            pltpu.VMEM((WIN, k.shape[1]), BF),
            pltpu.VMEM((WIN, k.shape[1]), BF),
            pltpu.VMEM((HALO_PARTS, WIN - 2 * rows, k.shape[1] // 2), BF),
            pltpu.VMEM((NP, w.shape[0] // 2, w.shape[1]), BF),
            pltpu.SemaphoreType.DMA((4,)),
            pltpu.SemaphoreType.DMA,
            pltpu.SemaphoreType.DMA((EDGE_COPY + 1,)),
            pltpu.SemaphoreType.DMA((EDGE_COPY + 1,)),
        ],
        compiler_params=pltpu.CompilerParams(
            collective_id=2, has_side_effects=True, vmem_limit_bytes=32 << 20
        ),
        name="fine",
    )(gain.reshape(1, width), *[in_hbm(a) for a in (x, q, k, v, w)])


ZCHUNK = 8


def z_copies(rows):
    return (NZ - 1) * (rows // ZCHUNK)


def z_gather(sends, src_ref, dst_ref, local_sem):
    x, y, z, c = place()
    up, down = device_at(x, y, (z + 1) % NZ, c), device_at(x, y, (z + NZ - 1) % NZ, c)
    chunks = src_ref.shape[0] // ZCHUNK
    first = sends.next
    sends.next += z_copies(src_ref.shape[0])
    count_up, count_down = NZ // 2, NZ // 2 - 1
    local = pltpu.make_async_copy(src_ref, dst_ref.at[z], local_sem)
    for s in range(count_up + 1):
        for part in range(chunks):
            at = pl.ds(part * ZCHUNK, ZCHUNK)
            for sign, count, base, to, origin in (
                (-1, count_up, first, up, down),
                (1, count_down, first + count_up * chunks, down, up),
            ):
                if s > count:
                    continue
                held = (z + sign * s + NZ) % NZ
                if s > 0:
                    sends.arrived(base + (s - 1) * chunks + part, dst_ref.at[held, at], origin)
                if s < count:
                    src = src_ref.at[at] if s == 0 else dst_ref.at[held, at]
                    sends.start(base + s * chunks + part, src, dst_ref.at[held, at], to)
        if s == 0:
            local.start()
        if s == count_up:
            local.wait()
        yield


def scatter(weights, dst_ref, local_sem, send_sem, recv_sem):
    outer = lax.axis_index("outer")
    inner = lax.axis_index("inner")
    head = outer // 2
    rows = dst_ref.shape[0]
    base = (outer % 2) * (16 * rows)
    columns = [pl.ds(n * HE, HE) for n in range(len(weights))]

    def rows_of(w, to):
        return w.at[pl.ds(pl.multiple_of(base + to * rows, rows), rows)]

    def to_self(n, w):
        return pltpu.make_async_copy(rows_of(w, inner), dst_ref.at[:, columns[n]], local_sem.at[n])

    @pl.when(inner == head)
    def _():
        for n, w in enumerate(weights):
            to_self(n, w).start()
        for d in range(1, 16):
            to = (inner + d) % 16
            for n, w in enumerate(weights):
                pltpu.make_async_remote_copy(
                    src_ref=rows_of(w, to),
                    dst_ref=dst_ref.at[:, columns[n]],
                    send_sem=send_sem.at[n, d - 1],
                    recv_sem=recv_sem.at[n],
                    device_id=(outer, to),
                    device_id_type=MESH,
                ).start()

    yield

    @pl.when(inner == head)
    def _():
        for n, w in enumerate(weights):
            to_self(n, w).wait()
            for d in range(1, 16):
                piece = rows_of(w, 0)
                pltpu.make_async_copy(piece, piece, send_sem.at[n, d - 1]).wait()

    @pl.when(inner != head)
    def _():
        for n in range(len(weights)):
            piece = dst_ref.at[:, columns[n]]
            pltpu.make_async_copy(piece, piece, recv_sem.at[n]).wait()

    yield


def half_rows(w_ref):
    size = w_ref.shape[0] // 2
    copy = lax.axis_index("outer") % 2
    return w_ref.at[pl.ds(pl.multiple_of(copy * size, size), size)]


PIECE_COPIES = 32


def to_all_of_plane(sends, src, dst, local_sem):
    x, y, z, c = place()
    partner = device_at(x, y, z, 1 - c)
    mine = slot_of(x, y, c)
    first = sends.next
    sends.next += PIECE_COPIES
    offsets = [(a, b) for a in range(NX) for b in range(NY)]
    local = pltpu.make_async_copy(src, dst.at[mine], local_sem)
    local.start()
    for n, (a, b) in enumerate(offsets):
        to = device_at((x + a) % NX, (y + b) % NY, z, c) if n else partner
        sends.start(first + n, src, dst.at[mine], to)
    yield
    for n, (a, b) in enumerate(offsets):
        if n:
            px, py = (x + NX - a) % NX, (y + NY - b) % NY
            s = slot_of(px, py, c)
            sends.arrived(first + n, dst.at[s], device_at(px, py, z, c))
            sends.start(first + len(offsets) + n, dst.at[s], dst.at[s], partner)
    yield
    local.wait()
    sends.arrived(first, dst.at[slot_of(x, y, 1 - c)], partner)
    for n, (a, b) in enumerate(offsets):
        if n:
            s = slot_of((x + NX - a) % NX, (y + NY - b) % NY, 1 - c)
            sends.arrived(first + len(offsets) + n, dst.at[s], partner)
    yield


PLANE_GROUP = 4
STATS = 3


def coarse_kernel(
    normed_ref, pooled_ref, w_src, wq_ref, wk_ref, wv_ref, out_ref,
    tokens_ref, w_ref, head_ref, piece_ref, proj_ref,
    kv_ref, q_ref, top_ref, acc_ref, part_out, part_in, mix_ref, heads_ref,
    local_sem, scatter_send, scatter_recv, send_sem, recv_sem,
):
    x, y, z, c = place()
    outer = lax.axis_index("outer")
    inner = lax.axis_index("inner")
    plane = [(a, b) for a in range(NX) for b in range(NY)][1:]
    others = [device_at(x, y, (z + d) % NZ, c) for d in range(1, NZ)]
    along_x = [device_at((x + d) % NX, y, z, c) for d in range(NX)]
    along_y = [device_at(x, (y + d) % NY, z, c) for d in range(NY)]
    partner = device_at(x, y, z, 1 - c)
    greet(
        [device_at((x + a) % NX, (y + b) % NY, z, c) for a, b in plane]
        + [partner]
        + others
        + [(outer, (inner + d) % 16) for d in range(1, 16)]
    )
    base_k, base_p, base_q, base_o, base_z = 0, 4, 8, 12, 16
    sends = Sends(send_sem, recv_sem, base_z + NZ)
    along = z_gather(sends, normed_ref, tokens_ref, local_sem.at[0])
    out = plane_gather(sends, half_rows(w_src), w_ref, local_sem.at[1])
    pieces = scatter((wq_ref, wk_ref, wv_ref), piece_ref, local_sem.at[pl.ds(2, 3)], scatter_send, scatter_recv)
    head = to_all_of_plane(sends, piece_ref, head_ref, local_sem.at[5])
    order = (along, pieces, out, along, along, pieces, head, out, along, out, along, out, along, out)
    for steps in order + (along, head, along, along, head):
        next(steps)
    count = proj_ref.shape[0]
    deep = tokens_ref.shape[2]
    proj_ref[...] = jnp.dot(
        tokens_ref[...].reshape(count, deep),
        head_ref[...].reshape(deep, proj_ref.shape[1]),
        preferred_element_type=F32,
    ).astype(BF)
    own_kv = proj_ref.at[:, HE:]
    own_q = proj_ref.at[:, :HE]
    mine = y * NC + c
    for d in (2, 1, 3):
        sends.start(base_k + d, own_kv, kv_ref.at[mine], along_y[d])
        sends.start(base_q + d, own_q, q_ref.at[d], along_x[d])
    sends.start(base_p, own_kv, kv_ref.at[mine], partner)
    kv_ref[mine] = proj_ref[:, HE:]
    q_ref[0] = proj_ref[:, :HE]
    next(out)
    for d in (1, 3, 2):
        s = (y + NY - d) % NY * NC + c
        sends.arrived(base_k + d, kv_ref.at[s], along_y[NY - d])
        sends.start(base_p + d, kv_ref.at[s], kv_ref.at[s], partner)
    sends.arrived(base_p, kv_ref.at[y * NC + 1 - c], partner)
    for d in (1, 3, 2):
        sends.arrived(base_p + d, kv_ref.at[(y + NY - d) % NY * NC + 1 - c], partner)
    per = count // NZ
    step = PLANE_GROUP * per
    factor = SCALE * LOG2E
    side = NY * NC
    width = side * step
    ones = jnp.ones((width, HE), BF)
    t = lax.broadcasted_iota(jnp.int32, (step, 1), 0)
    u = lax.broadcasted_iota(jnp.int32, (1, width), 1)
    t_order = t // per * (NP * 32) + t % per
    u_order = (u % step // per * NP + u // step) * 32 + u % per
    lane = lax.broadcasted_iota(jnp.int32, (count, HE), 1)

    def attend(d):
        owner = slot_of((x + NX - d) % NX, y, c)
        allowed = u_order <= t_order + (owner - side * x) * 32
        for n in range(NZ // PLANE_GROUP):
            lo = n * step
            keys = kv_ref[:, lo : lo + step, :HE].reshape(width, HE)
            values = kv_ref[:, lo : lo + step, HE:].reshape(width, HE)
            s = lax.dot_general(
                q_ref[d, lo:, :], keys, TRANS, preferred_element_type=F32
            ) * factor
            edge = jnp.where(allowed, s[:step], NEG)
            s = jnp.concatenate([edge, s[step:]], axis=0) if lo + step < count else edge
            best = jnp.max(s, axis=-1, keepdims=True)
            wide = jnp.concatenate([values, ones], axis=1)
            if n == 0:
                top_ref[...] = best
                acc_ref[...] = jnp.dot(
                    jnp.exp2(s - best).astype(BF), wide, preferred_element_type=F32
                )
            else:
                old = top_ref[lo:, :]
                new = jnp.maximum(old, best)
                acc_ref[lo:, :] = acc_ref[lo:, :] * jnp.exp2(old - new) + jnp.dot(
                    jnp.exp2(s - new).astype(BF), wide, preferred_element_type=F32
                )
                top_ref[lo:, :] = new
        weight = top_ref[...] + jnp.log2(acc_ref[:, HE:])
        return acc_ref[:, :HE] / acc_ref[:, HE:], weight

    for d in (2, 1, 3):
        sends.arrived(base_q + d, q_ref.at[d], along_x[NX - d])
        mixed, weight = attend(d)
        high = weight.astype(BF).astype(F32)
        middle = (weight - high).astype(BF).astype(F32)
        low = weight - high - middle
        pieces = jnp.where(lane < 32, high, jnp.where(lane < 64, middle, low))
        part_out[d, :, :HE] = mixed.astype(BF)
        part_out[d, :, HE:] = pieces.astype(BF)
        sends.start(base_o + d, part_out.at[d], part_in.at[d], along_x[NX - d])
    mixed, weight = attend(0)
    parts = [(mixed, weight)]
    for d in (2, 1, 3):
        sends.arrived(base_o + d, part_in.at[d], along_x[d])
        got = part_in[d, :, HE:].astype(F32)
        weight = sum(got[:, 32 * n : 32 * n + 1] for n in range(STATS))
        parts.append((part_in[d, :, :HE].astype(F32), weight + jnp.zeros((count, HE), F32)))
    best = functools.reduce(jnp.maximum, [w for _, w in parts])
    total, mixed = 0.0, 0.0
    for m, w in parts:
        share = jnp.exp2(w - best)
        total += share
        mixed += share * m
    mix_ref[...] = (mixed / total).astype(BF).reshape(mix_ref.shape)
    for d in (8, 7, 9, 6, 10, 5, 11, 4, 12, 3, 13, 2, 14, 1, 15):
        sends.start(base_z + d, mix_ref.at[(z + d) % NZ], heads_ref.at[z], others[d - 1])
    heads_ref[z] = mix_ref[z]
    next(out)
    for d in range(1, NZ):
        origin = (z + NZ - d) % NZ
        sends.arrived(base_z + d, heads_ref.at[origin], others[NZ - d - 1])
    sends.drain()
    total = pooled_ref[...].astype(F32)
    for n in range(NZ // 2):
        two = jnp.concatenate([heads_ref[2 * n], heads_ref[2 * n + 1]], axis=1)
        rows = [w_ref[h + half] for h in (2 * n, 2 * n + 1) for half in (0, NP // 2)]
        w = jnp.concatenate(rows, axis=0)
        total += jnp.dot(two, w, preferred_element_type=F32)
    out_ref[...] = total.astype(BF)


def coarse_stage(normed, pooled, w, *head_weights):
    width = normed.shape[1]
    rows = NZ * normed.shape[0]
    count = 16 + NZ + z_copies(normed.shape[0]) + plane_copies((0, 1)) + PIECE_COPIES
    piece = (width // NP, len(head_weights) * HE)
    heads = pltpu.VMEM((NZ, rows // NZ, HE), BF)
    parts = pltpu.VMEM((NX, rows, 2 * HE), BF)
    return pl.pallas_call(
        coarse_kernel,
        out_shape=jax.ShapeDtypeStruct(pooled.shape, BF),
        in_specs=[vmem_spec(), vmem_spec()] + [hbm_spec()] * 4,
        out_specs=vmem_spec(),
        scratch_shapes=[
            pltpu.VMEM((NZ, *normed.shape), BF),
            pltpu.VMEM((NP, w.shape[0] // 2, width), BF),
            pltpu.VMEM((NP, *piece), BF),
            pltpu.VMEM(piece, BF),
            pltpu.VMEM((rows, piece[1]), BF),
            pltpu.VMEM((NY * NC, rows, 2 * HE), BF),
            pltpu.VMEM((NX, rows, HE), BF),
            pltpu.VMEM((rows, 1), F32),
            pltpu.VMEM((rows, 2 * HE), F32),
            parts,
            parts,
            heads,
            heads,
            pltpu.SemaphoreType.DMA((6,)),
            pltpu.SemaphoreType.DMA((3, 15)),
            pltpu.SemaphoreType.DMA((3,)),
            pltpu.SemaphoreType.DMA((count,)),
            pltpu.SemaphoreType.DMA((count,)),
        ],
        compiler_params=pltpu.CompilerParams(
            collective_id=4, has_side_effects=True, vmem_limit_bytes=40 << 20
        ),
        name="coarse",
    )(normed, pooled, *[in_hbm(a) for a in (w, *head_weights)])


def on_device(
    fine_input,
    fine_query,
    fine_key,
    fine_value,
    w_fine_out,
    norm_gain,
    w_query,
    w_key,
    w_value,
    w_coarse_out,
):
    rows, width = fine_input.shape
    state, pooled, normed = fine_stage(
        fine_input, fine_query, fine_key, fine_value, norm_gain, w_fine_out
    )
    coarse_out = coarse_stage(normed, pooled, w_coarse_out, w_query, w_key, w_value)
    groups = state.reshape(rows // POOL, POOL, width).astype(F32)
    lifted = groups + coarse_out.astype(F32)[:, None, :]
    return lifted.reshape(rows, width).astype(BF)


def solution(mesh):
    placed = (
        P(("outer", "inner"), None),
        P(("outer", "inner"), None),
        P(("outer", "inner"), None),
        P(("outer", "inner"), None),
        P(None, "inner"),
        P(),
        P(None, "inner"),
        P(None, "inner"),
        P(None, "inner"),
        P("inner", None),
    )
    return jax.shard_map(
        on_device,
        mesh=mesh,
        in_specs=placed,
        out_specs=P(("outer", "inner"), None),
        check_vma=False,
    )
```
